128 devices in a mesh: ctx: 16 (over x, y_lo, core), head: 8 (over z, y_hi).
Axes of the slice: x: 4, y: 4 (y_hi: 2, y_lo: 2; y = y_hi * 2 + y_lo), z: 4, core: 2. Of those that a mesh axis runs over, the one named last changes fastest.
Arguments:
- queries: bfloat16 [4096, 8192], P(('ctx', 'head')), may hold values from -6 to 6
- key_rows: bfloat16 [4096, 1024], P(('ctx', 'head')), may hold values from -6 to 6
- value_rows: bfloat16 [4096, 1024], P(('ctx', 'head')), may hold values from -6 to 6
- cotangent: bfloat16 [4096, 8192], P(('ctx', 'head')), may hold values from -6 to 6
- doc_lengths: int32 [8], replicated, may hold values from 1 to 2048, 4096 in all
- block_route: int32 [16, 16], replicated, may hold values from 0 to 15, each once within a row
Outputs:
- attended: bfloat16 [4096, 8192], P('ctx', 'head')
- grad_query: float32 [4096, 8192], P('ctx', 'head')
- grad_key: float32 [4096, 1024], P('ctx', 'head')
- grad_value: float32 [4096, 1024], P('ctx', 'head')
The draws below stay inside these ranges and needn't reach their ends.
Inputs may be any that keep to these rules, and one draw needn't show every extreme that they name: `doc_lengths`: the lengths split the 4096 positions into consecutive documents; the longest is exactly 2048. Each row is a permutation: block b (16 positions) of loader shard s goes to context shard block_route[s, b].
All inputs are finite; a program needn't handle non-finite values.
Results may differ from the reference program's by a relative error of at most 0.028.
Values may be sent and summed in bfloat16 or wider, within the bound.
A program may use at most 64 MiB of HBM per device.

```python
import math
import jax
import jax.numpy as jnp
import numpy as np
from jax import lax

HD = 128
GROUP = 8
TOK_DEV = 256
DOCS = 8
KVH = 8
QH = 64
SEQ = 4096
SHARDS = 16


def draw_queries(key, part):
    result = jax.random.truncated_normal(jax.random.fold_in(key, 21), -6.0, 6.0, (SEQ, QH * HD), jnp.float32)
    return result.astype(jnp.bfloat16)


def draw_key_rows(key, part):
    result = jax.random.truncated_normal(jax.random.fold_in(key, 22), -6.0, 6.0, (SEQ, KVH * HD), jnp.float32)
    return result.astype(jnp.bfloat16)


def shard_levels(stream_key, shape, cuts, low, largest):
    def one(axis_at, blocks):
        steps = jax.random.uniform(jax.random.fold_in(jax.random.fold_in(stream_key, 6), axis_at), (blocks,), jnp.float32, low / len(cuts), largest / len(cuts))
        return jnp.repeat(jnp.exp(steps), shape[axis_at] // blocks).reshape((-1,) + (1,) * (len(shape) - axis_at - 1))

    level = one(*cuts[0])
    for cut in cuts[1:]:
        level = level * one(*cut)
    return level


def profile(number_of, total, reach, slope):
    weights = [(1 << 20) // math.isqrt(rank ** slope) + 1 for rank in range(2, number_of + 1)]
    rest, holding = total - reach - (number_of - 1), [1] * (number_of - 1)
    while rest > 0:
        free = [i for i in range(number_of - 1) if holding[i] < reach]
        pool, budget = sum([weights[i] for i in free]), rest
        for i in free:
            more = min(reach - holding[i], max(1, budget * weights[i] // pool), rest)
            holding[i] = holding[i] + more
            rest = rest - more
    return np.array([reach] + holding)


def ragged(own_key, number_of, total, reach, slope):
    if number_of == 2:
        one = jax.random.randint(own_key, (), max(1, total - reach), min(reach, total - 1) + 1)
        return jnp.stack([one, total - one])
    sizes = jnp.asarray(profile(number_of, total, reach, slope), jnp.int32)
    pairs = (number_of - 1) // 2
    donor, receiver = sizes[1:1 + 2 * pairs:2], sizes[2:2 + 2 * pairs:2]
    slack = jnp.minimum(donor - 1, reach - receiver)
    moved = jax.random.randint(jax.random.fold_in(own_key, 1), (pairs,), 0, 1 << 20) % (slack + 1)
    sizes = sizes.at[1:1 + 2 * pairs:2].set(donor - moved).at[2:2 + 2 * pairs:2].set(receiver + moved)
    return sizes[jax.random.permutation(jax.random.fold_in(own_key, 2), number_of)]


def gaussian(own_key, extent, scale, most, pieces=(), kind=jnp.bfloat16):
    loudness = shard_levels(own_key, extent, pieces, -0.22, 0.18) if pieces else 1.0
    drawn = jax.random.normal(own_key, extent, jnp.float32) * scale * loudness
    return jnp.minimum(jnp.maximum(drawn, -most), most).astype(kind)


def setup_inputs(seed: int = 0) -> dict:
    arg_keys = jax.random.split(jax.random.key(seed), 7)
    queries = draw_queries(jax.random.fold_in(arg_keys[6], 71), 0)
    key_rows = draw_key_rows(jax.random.fold_in(arg_keys[6], 71), 0)
    value_rows = gaussian(arg_keys[2], (SEQ, KVH * HD), 1.0, 6.0, ((0, 128),))
    cotangent = gaussian(arg_keys[3], (SEQ, QH * HD), 1.0, 6.0, ((0, 128),))
    doc_lengths = ragged(arg_keys[4], DOCS, SEQ, SEQ // 2, 2).astype(jnp.int32)
    block_route = jax.vmap(lambda own: jax.random.permutation(own, SHARDS))(jax.random.split(arg_keys[5], SHARDS)).reshape((SHARDS, SHARDS)).astype(jnp.int32)
    return {"queries": queries, "key_rows": key_rows, "value_rows": value_rows, "cotangent": cotangent, "doc_lengths": doc_lengths, "block_route": block_route}


def slot_positions(block_route, shard_count, shard_rows):
    block_rows = shard_rows // shard_count
    slots = jnp.arange(shard_count * shard_rows, dtype=jnp.int32)
    target = slots // shard_rows
    source = slots % shard_rows // block_rows
    within = slots % block_rows
    blocks = jnp.arange(shard_count, dtype=jnp.int32)
    block_of = lax.optimization_barrier(jnp.sum(jnp.where(block_route[:, :, None] == blocks[None, None, :], blocks[None, :, None], 0), axis=1)).astype(jnp.int32)
    chosen = jnp.take(block_of.reshape(-1), (source * shard_count + target).astype(jnp.int32)).astype(jnp.int32)
    return (source * shard_rows + chosen * block_rows + within).astype(jnp.int32)

def reference(queries, key_rows, value_rows, cotangent, doc_lengths, block_route):
    positions = slot_positions(block_route, SHARDS, TOK_DEV)
    ends = jnp.cumsum(doc_lengths).astype(jnp.int32)
    documents = lax.optimization_barrier(jnp.sum((positions[:, None] >= ends[None, :]).astype(jnp.int32), axis=1)).astype(jnp.int32)
    visible = (documents[:, None] == documents[None, :]) & (positions[None, :] <= positions[:, None])
    q_all = jnp.take(queries, positions, axis=0)
    k_all = jnp.take(key_rows, positions, axis=0)
    v_all = jnp.take(value_rows, positions, axis=0)
    g_all = jnp.take(cotangent, positions, axis=0)
    scale = 1.0 / math.sqrt(HD)

    def one_head(head):
        group_start = (head // GROUP * HD).astype(jnp.int32)
        q_head = lax.dynamic_slice_in_dim(q_all, (head * HD).astype(jnp.int32), HD, 1)
        g_head = lax.dynamic_slice_in_dim(g_all, (head * HD).astype(jnp.int32), HD, 1)
        k_head = lax.dynamic_slice_in_dim(k_all, group_start, HD, 1)
        v_head = lax.dynamic_slice_in_dim(v_all, group_start, HD, 1)
        scores = jnp.dot(q_head, k_head.T, preferred_element_type=jnp.float32) * scale
        masked = jnp.where(visible, scores, -jnp.inf)
        peak = lax.optimization_barrier(jnp.max(masked, axis=1, keepdims=True))
        total = lax.optimization_barrier(jnp.sum(jnp.exp(masked - peak), axis=1, keepdims=True))
        log_total = peak + jnp.log(total)
        weights = jnp.where(visible, jnp.exp(masked - log_total), jnp.float32(0.0))
        weights_low = weights.astype(jnp.bfloat16)
        attended = jnp.dot(weights_low, v_head, preferred_element_type=jnp.float32).astype(jnp.bfloat16)
        delta = lax.optimization_barrier(jnp.sum(g_head.astype(jnp.float32) * attended.astype(jnp.float32), axis=1, keepdims=True))
        dprob = jnp.dot(g_head, v_head.T, preferred_element_type=jnp.float32)
        dscore = (weights * (dprob - delta)).astype(jnp.bfloat16)
        grad_q = jnp.dot(dscore, k_head, preferred_element_type=jnp.float32) * scale
        grad_k = jnp.dot(dscore.T, q_head, preferred_element_type=jnp.float32) * scale
        grad_v = jnp.dot(weights_low.T, g_head, preferred_element_type=jnp.float32)
        return (attended, grad_q, grad_k, grad_v)
    heads = jnp.arange(QH, dtype=jnp.int32)
    att, grad_q, grad_k, grad_v = lax.map(one_head, heads)
    attended = jnp.transpose(att, (1, 0, 2)).reshape(SEQ, QH * HD)
    grad_query = jnp.transpose(grad_q, (1, 0, 2)).reshape(SEQ, QH * HD)
    grad_key = jnp.transpose(lax.optimization_barrier(jnp.sum(grad_k.reshape(KVH, GROUP, SEQ, HD), axis=1)), (1, 0, 2)).reshape(SEQ, KVH * HD)
    grad_value = jnp.transpose(lax.optimization_barrier(jnp.sum(grad_v.reshape(KVH, GROUP, SEQ, HD), axis=1)), (1, 0, 2)).reshape(SEQ, KVH * HD)
    return (attended, grad_query, grad_key, grad_value)
```

```python
import math

import jax
import jax.numpy as jnp
from jax import lax
from jax.experimental import pallas as pl
from jax.experimental.pallas import tpu as pltpu
from jax.sharding import PartitionSpec as P

HD = 128
GROUP = 8
SHARDS = 16
BLOCK = 16
ROWS = SHARDS * BLOCK
SEQ = SHARDS * ROWS
DOCS = 8
HEADS = 8
COLS = GROUP * HD

SPAN = 4
LANES = SPAN * GROUP * BLOCK
NEGATIVE = -1e30
FLOOR = -0.5e30
SCALE = 1.0 / math.sqrt(HD)
LOG2E = 1.4426950408889634

BF = jnp.bfloat16
F32 = jnp.float32
MESH = pl.DeviceIdType.MESH
ANY = pl.BlockSpec(memory_space=pl.ANY)
VMEM = pl.BlockSpec(memory_space=pltpu.VMEM)
SMEM = pl.BlockSpec(memory_space=pltpu.SMEM)


def ctx_of(x, y, core):
    return (lax.rem(x, 4) * 2 + lax.rem(y, 2)) * 2 + lax.rem(core, 2)


def head_of(z, y):
    return lax.rem(z, 4) * 2 + lax.rem(y, 2)


def remote(src, dst, send, recv, ctx, head):
    return pltpu.make_async_remote_copy(
        src_ref=src,
        dst_ref=dst,
        send_sem=send,
        recv_sem=recv,
        device_id=(ctx, head),
        device_id_type=MESH,
    )


def exchange_kernel(
    route, q, k, v, g, qo, go, ko, vo, xq, xg, sq, sg,
    p1s, p1r, p2s, p2r, rs, rr, cs, cr, local,
):
    c = lax.axis_index("ctx")
    h = lax.axis_index("head")
    z, yh = h // 2, lax.rem(h, 2)
    x, yl, core = c // 4, lax.rem(c // 2, 2), lax.rem(c, 2)
    head_peers = [(jz, jy) for jz in range(4) for jy in range(2) if (jz, jy) != (0, 0)]
    ctx_peers = [
        (jx, jy, jc) for jx in range(4) for jy in range(2) for jc in range(2)
        if (jx, jy, jc) != (0, 0, 0)
    ]

    barrier = pltpu.get_barrier_semaphore()
    for jz, jy in head_peers:
        pl.semaphore_signal(
            barrier, inc=1, device_id=(c, head_of(z + jz, yh + jy)), device_id_type=MESH
        )
    for jx, jy, jc in ctx_peers:
        pl.semaphore_signal(
            barrier, inc=1, device_id=(ctx_of(x + jx, yl + jy, core + jc), h), device_id_type=MESH
        )
    pl.semaphore_wait(barrier, len(head_peers) + len(ctx_peers))

    sent = []

    def go_remote(copy):
        copy.start()
        sent.append(copy)
        return copy

    kv_rows = pl.ds(c * ROWS + h * 32, 32)
    p1 = [[], [], [], []]
    for jz, jy in head_peers:
        j = jz * 2 + jy
        peer = head_of(z + jz, yh + jy)
        cols = pl.ds(pl.multiple_of(peer * HD, HD), HD)
        for a, (src, dst) in enumerate(((k, ko), (v, vo))):
            p1[a].append(go_remote(remote(
                src.at[:, cols], dst.at[kv_rows], p1s.at[a, j], p1r.at[a, j], c, peer)))
    own_cols = pl.ds(pl.multiple_of(h * HD, HD), HD)
    own = [
        pltpu.make_async_copy(k.at[:, own_cols], ko.at[kv_rows], local.at[0]),
        pltpu.make_async_copy(v.at[:, own_cols], vo.at[kv_rows], local.at[1]),
    ]
    for a, (src, dst) in enumerate(((q, xq), (g, xg))):
        for jz, jy in head_peers:
            j = jz * 2 + jy
            peer = head_of(z + jz, yh + jy)
            cols = pl.ds(pl.multiple_of(peer * COLS, COLS), COLS)
            p1[2 + a].append(go_remote(remote(
                src.at[:, :, cols], dst.at[pl.ds(h * 2, 2)],
                p1s.at[2 + a, j], p1r.at[2 + a, j], c, peer)))
        cols = pl.ds(pl.multiple_of(h * COLS, COLS), COLS)
        own.append(pltpu.make_async_copy(
            src.at[:, :, cols], dst.at[pl.ds(h * 2, 2)], local.at[2 + a]))
    for copy in own:
        copy.start()

    kv = (ko, vo)

    def shard(a, dx, dy):
        return kv[a].at[pl.ds(ctx_of(x + dx, yl + dy, core) * ROWS, ROWS)]

    def ring(a, dx, dy, tx, ty):
        slot = ((dx - tx) % 4) * 2 + (dy - ty) % 2
        part = shard(a, dx, dy)
        return remote(part, part, rs.at[a, slot], rr.at[a, slot],
                      ctx_of(x + tx + 4, yl + ty + 2, core), h)

    def partner(a, dx, dy):
        slot = dx * 2 + dy
        part = shard(a, dx, dy)
        return remote(part, part, cs.at[a, slot], cr.at[a, slot], ctx_of(x, yl, core + 1), h)

    def arrived(a, dx, dy):
        slot = dx * 2 + dy
        part = shard(a, dx, dy)
        remote(part, part, rs.at[a, slot], rr.at[a, slot], c, h).wait_recv()

    for a in range(2):
        own[a].wait()
        for copy in p1[a]:
            copy.wait_recv()
    for a in range(2):
        go_remote(ring(a, 0, 0, 0, 1))
        go_remote(ring(a, 0, 0, 1, 0))
        go_remote(ring(a, 0, 0, -1, 0))
        go_remote(partner(a, 0, 0))

    def second(a, stage, send, out):
        own[2 + a].wait()
        for copy in p1[2 + a]:
            copy.wait_recv()

        def pick(d, carry):
            block = jnp.int32(0)
            for b in range(SHARDS):
                block = jnp.where(route[c, b] == d, b, block)
            send[d] = stage[block]
            return carry

        lax.fori_loop(0, SHARDS, pick, 0)
        mine = pltpu.make_async_copy(send.at[c], out.at[c], local.at[4 + a])
        mine.start()
        copies = []
        for jx, jy, jc in ctx_peers:
            j = (jx * 2 + jy) * 2 + jc
            d = ctx_of(x + jx, yl + jy, core + jc)
            copies.append(go_remote(remote(
                send.at[d], out.at[c], p2s.at[a, j], p2r.at[a, j], d, h)))
        return mine, copies

    for a in range(2):
        arrived(a, 0, 1)
        go_remote(ring(a, 0, 1, 1, 0))
        go_remote(ring(a, 0, 1, -1, 0))
        go_remote(partner(a, 0, 1))
    mine_q, p2q = second(0, xq, sq, qo)
    for dy in range(2):
        for a in range(2):
            arrived(a, 3, dy)
            if a == 0:
                go_remote(ring(a, 3, dy, 1, 0))
            go_remote(partner(a, 3, dy))
            arrived(a, 1, dy)
            if a == 1:
                go_remote(ring(a, 1, dy, -1, 0))
            go_remote(partner(a, 1, dy))
    mine_g, p2g = second(1, xg, sg, go)
    for dy in range(2):
        for a in range(2):
            arrived(a, 2, dy)
            go_remote(partner(a, 2, dy))
    mine_q.wait()
    mine_g.wait()

    def received(a, out):
        for jx, jy, jc in ctx_peers:
            j = (jx * 2 + jy) * 2 + jc
            src = ctx_of(x - jx + 4, yl - jy + 2, core - jc + 2)
            remote(out.at[src], out.at[src], p2s.at[a, j], p2r.at[a, j], c, h).wait_recv()

    received(0, qo)
    received(1, go)
    for a in range(2):
        for dx in range(4):
            for dy in range(2):
                slot = dx * 2 + dy
                part = kv[a].at[pl.ds(ctx_of(x + dx, yl + dy, core + 1) * ROWS, ROWS)]
                remote(part, part, cs.at[a, slot], cr.at[a, slot], c, h).wait_recv()
    for copy in sent:
        copy.wait_send()


def exchange(route, q, k, v, g):
    return pl.pallas_call(
        exchange_kernel,
        name="exchange",
        out_shape=(
            jax.ShapeDtypeStruct((SHARDS, BLOCK, COLS), BF),
            jax.ShapeDtypeStruct((SHARDS, BLOCK, COLS), BF),
            jax.ShapeDtypeStruct((SEQ, HD), BF),
            jax.ShapeDtypeStruct((SEQ, HD), BF),
        ),
        in_specs=[SMEM, ANY, VMEM, VMEM, ANY],
        out_specs=(ANY, ANY, ANY, ANY),
        scratch_shapes=[
            pltpu.VMEM((SHARDS, BLOCK, COLS), BF),
            pltpu.VMEM((SHARDS, BLOCK, COLS), BF),
            pltpu.VMEM((SHARDS, BLOCK, COLS), BF),
            pltpu.VMEM((SHARDS, BLOCK, COLS), BF),
            pltpu.SemaphoreType.DMA((4, 8)),
            pltpu.SemaphoreType.DMA((4, 8)),
            pltpu.SemaphoreType.DMA((2, 16)),
            pltpu.SemaphoreType.DMA((2, 16)),
            pltpu.SemaphoreType.DMA((2, 24)),
            pltpu.SemaphoreType.DMA((2, 8)),
            pltpu.SemaphoreType.DMA((2, 8)),
            pltpu.SemaphoreType.DMA((2, 8)),
            pltpu.SemaphoreType.DMA((6,)),
        ],
        compiler_params=pltpu.CompilerParams(collective_id=0, has_side_effects=True),
    )(route, q, k, v, g)


def attention_kernel(
    route, docs, q, g, k, v, att, dq, dkv,
    s_buf, kt, vt, dk_acc, dv_acc, ot_acc, dqt_acc, starts,
):
    c = lax.axis_index("ctx")
    ends = []
    total = jnp.int32(0)
    for j in range(DOCS):
        total = total + docs[j]
        ends.append(total)

    def find(s, carry):
        block = jnp.int32(0)
        for b in range(SHARDS):
            block = jnp.where(route[s, b] == c, b, block)
        starts[s] = s * ROWS + block * BLOCK
        return carry

    lax.fori_loop(0, SHARDS, find, 0)

    def prepare(t, carry):
        kt[t] = k[pl.ds(t * ROWS, ROWS), :].T
        vt[t] = v[pl.ds(t * ROWS, ROWS), :].T
        zero = jnp.zeros((ROWS, HD), F32)
        dk_acc[pl.ds(t * ROWS, ROWS), :] = zero
        dv_acc[pl.ds(t * ROWS, ROWS), :] = zero
        return carry

    lax.fori_loop(0, SHARDS, prepare, 0)

    def stack(ref, first):
        parts = []
        for i in range(SPAN):
            rows = ref[first + i]
            parts += [rows[:, n * HD:(n + 1) * HD] for n in range(GROUP)]
        return jnp.concatenate(parts, axis=0)

    lane = lax.broadcasted_iota(jnp.int32, (1, GROUP * BLOCK), 1)
    within = lax.rem(lane, BLOCK)

    def group(n, carry):
        first = n * SPAN
        qg = stack(q, first)
        gg = stack(g, first)
        qt = qg.T
        gt = gg.T
        q_pos = jnp.concatenate([within + starts[first + i] for i in range(SPAN)], axis=1)
        q_doc = jnp.zeros_like(q_pos)
        low = jnp.int32(0)
        p_first = starts[first]
        for end in ends:
            q_doc = jnp.where(q_pos >= end, end, q_doc)
            low = jnp.where(p_first >= end, end, low)
        t_low = low // ROWS
        t_high = first + SPAN
        key = lax.broadcasted_iota(jnp.int32, (ROWS, LANES), 0)
        ot_acc[...] = jnp.zeros_like(ot_acc)
        dqt_acc[...] = jnp.zeros_like(dqt_acc)

        def forward(t, carried):
            peak, mass = carried
            s = jnp.dot(k[pl.ds(t * ROWS, ROWS), :], qt, preferred_element_type=F32)
            base = t * ROWS
            seen = (key >= q_doc - base) & (key <= q_pos - base)
            s = jnp.where(seen, s * (SCALE * LOG2E), NEGATIVE)
            s_buf[t] = s
            new_peak = jnp.maximum(peak, jnp.max(s, axis=0, keepdims=True))
            p = jnp.exp2(s - new_peak)
            fade = jnp.exp2(peak - new_peak)
            mass = mass * fade + jnp.sum(p, axis=0, keepdims=True)
            ot_acc[...] = ot_acc[...] * fade + jnp.dot(
                vt[t], p.astype(BF), preferred_element_type=F32)
            return new_peak, mass

        peak, mass = lax.fori_loop(
            t_low, t_high, forward,
            (jnp.full((1, LANES), FLOOR, F32), jnp.zeros((1, LANES), F32)))
        lse = peak + jnp.log2(mass)
        ot = (ot_acc[...] * (1.0 / mass)).astype(BF)
        delta = jnp.sum(gt.astype(F32) * ot.astype(F32), axis=0, keepdims=True)
        o = ot.T
        for i in range(SPAN):
            for m in range(GROUP):
                r = (i * GROUP + m) * BLOCK
                att[first + i, :, m * HD:(m + 1) * HD] = o[r:r + BLOCK]

        def backward(t, carried):
            rows = pl.ds(t * ROWS, ROWS)
            p = jnp.exp2(s_buf[t] - lse)
            dp = jnp.dot(v[rows, :], gt, preferred_element_type=F32)
            ds = (p * (dp - delta)).astype(BF)
            dv_acc[rows, :] += jnp.dot(p.astype(BF), gg, preferred_element_type=F32)
            dk_acc[rows, :] += jnp.dot(ds, qg, preferred_element_type=F32)
            dqt_acc[...] += jnp.dot(kt[t], ds, preferred_element_type=F32)
            return carried

        lax.fori_loop(t_low, t_high, backward, 0)
        grad = dqt_acc[...].T * SCALE
        for i in range(SPAN):
            for m in range(GROUP):
                r = (i * GROUP + m) * BLOCK
                dq[first + i, :, m * HD:(m + 1) * HD] = grad[r:r + BLOCK]
        return carry

    lax.fori_loop(0, SHARDS // SPAN, group, 0)

    def regroup(s, carry):
        for b in range(SHARDS):
            d = route[s, b]
            to = lax.rem(d, 2) * 8 + d // 2
            rows = pl.ds(s * ROWS + b * BLOCK, BLOCK)
            dkv[to, 0, s] = (dk_acc[rows, :] * SCALE).astype(BF)
            dkv[to, 1, s] = dv_acc[rows, :].astype(BF)
        return carry

    lax.fori_loop(0, SHARDS, regroup, 0)


def attention(route, docs, q, g, k, v):
    return pl.pallas_call(
        attention_kernel,
        name="attention",
        out_shape=(
            jax.ShapeDtypeStruct((SHARDS, BLOCK, COLS), BF),
            jax.ShapeDtypeStruct((SHARDS, BLOCK, COLS), F32),
            jax.ShapeDtypeStruct((SHARDS, 2, SHARDS, BLOCK, HD), BF),
        ),
        in_specs=[SMEM, SMEM, VMEM, VMEM, VMEM, VMEM],
        out_specs=(VMEM, VMEM, VMEM),
        scratch_shapes=[
            pltpu.VMEM((SHARDS, ROWS, LANES), F32),
            pltpu.VMEM((SHARDS, HD, ROWS), BF),
            pltpu.VMEM((SHARDS, HD, ROWS), BF),
            pltpu.VMEM((SEQ, HD), F32),
            pltpu.VMEM((SEQ, HD), F32),
            pltpu.VMEM((HD, LANES), F32),
            pltpu.VMEM((HD, LANES), F32),
            pltpu.SMEM((SHARDS,), jnp.int32),
        ],
        compiler_params=pltpu.CompilerParams(vmem_limit_bytes=48 << 20),
    )(route, docs, q, g, k, v)


def reduce_kernel(part, dk, dv, mate, chip, total, s1, r1, s2, r2):
    c = lax.axis_index("ctx")
    h = lax.axis_index("head")
    x, yl, core = c // 4, lax.rem(c // 2, 2), lax.rem(c, 2)
    peers = [(jx, jy) for jx in range(4) for jy in range(2) if (jx, jy) != (0, 0)]
    order = peers + [(0, 0)]
    other = ctx_of(x, yl, core + 1)

    barrier = pltpu.get_barrier_semaphore()
    pl.semaphore_signal(barrier, inc=1, device_id=(other, h), device_id_type=MESH)
    for jx, jy in peers:
        pl.semaphore_signal(
            barrier, inc=1, device_id=(ctx_of(x + jx, yl + jy, core), h), device_id_type=MESH)
    pl.semaphore_wait(barrier, len(peers) + 1)

    def place(jx, jy):
        return lax.rem(x + jx, 4) * 2 + lax.rem(yl + jy, 2)

    first = []
    for jx, jy in order:
        j = jx * 2 + jy
        t = place(jx, jy)
        copy = remote(part.at[(1 - core) * 8 + t], mate.at[t], s1.at[j], r1.at[j], other, h)
        copy.start()
        first.append(copy)
    second = []
    for (jx, jy), copy in zip(order, first):
        j = jx * 2 + jy
        t = place(jx, jy)
        copy.wait_recv()
        pair = part[core * 8 + t].astype(F32) + mate[t].astype(F32)
        if (jx, jy) == (0, 0):
            total[...] = pair
        else:
            mate[t] = pair.astype(BF)
            copy = remote(mate.at[t], chip.at[j], s2.at[j], r2.at[j],
                          ctx_of(x + jx, yl + jy, core), h)
            copy.start()
            second.append(copy)
    for copy, (jx, jy) in zip(second, peers):
        copy.wait_recv()
        total[...] += chip[jx * 2 + jy].astype(F32)
    dk[...] = total[0]
    dv[...] = total[1]
    for copy in first + second:
        copy.wait_send()


def reduce(part):
    shape = (2, SHARDS, BLOCK, HD)
    return pl.pallas_call(
        reduce_kernel,
        name="reduce",
        out_shape=(
            jax.ShapeDtypeStruct((SHARDS, BLOCK, HD), F32),
            jax.ShapeDtypeStruct((SHARDS, BLOCK, HD), F32),
        ),
        in_specs=[VMEM],
        out_specs=(VMEM, VMEM),
        scratch_shapes=[
            pltpu.VMEM((8,) + shape, BF),
            pltpu.VMEM((8,) + shape, BF),
            pltpu.VMEM(shape, F32),
            pltpu.SemaphoreType.DMA((8,)),
            pltpu.SemaphoreType.DMA((8,)),
            pltpu.SemaphoreType.DMA((8,)),
            pltpu.SemaphoreType.DMA((8,)),
        ],
        compiler_params=pltpu.CompilerParams(collective_id=1, has_side_effects=True),
    )(part)


def on_device(queries, key_rows, value_rows, cotangent, doc_lengths, block_route):
    q, g, k, v = exchange(
        block_route,
        queries.reshape(2, BLOCK, HEADS * COLS),
        key_rows,
        value_rows,
        cotangent.reshape(2, BLOCK, HEADS * COLS),
    )
    att, dq, part = attention(block_route, doc_lengths, q, g, k, v)
    dk, dv = reduce(part)
    return (
        att.reshape(ROWS, COLS),
        dq.reshape(ROWS, COLS),
        dk.reshape(ROWS, HD),
        dv.reshape(ROWS, HD),
    )


def solution(mesh):
    placed = P(("ctx", "head"), None)
    return jax.shard_map(
        on_device,
        mesh=mesh,
        in_specs=(placed, placed, placed, placed, P(), P()),
        out_specs=(P("ctx", "head"),) * 4,
        check_vma=False,
    )
```

```python
import functools
import math

import jax
import jax.numpy as jnp
from jax import lax
from jax.experimental import pallas as pl
from jax.experimental.pallas import tpu as pltpu
from jax.sharding import PartitionSpec as P

HD = 128
GROUP = 8
SHARDS = 16
BLOCK = 16
ROWS = SHARDS * BLOCK
SEQ = SHARDS * ROWS
DOCS = 8
HEADS = 8
COLS = GROUP * HD

SPAN = 4
WIDTH = GROUP * BLOCK
LANES = SPAN * WIDTH
NEGATIVE = -1e30
FLOOR = -0.5e30
SCALE = 1.0 / math.sqrt(HD)
LOG2E = 1.4426950408889634

BF = jnp.bfloat16
F32 = jnp.float32
MESH = pl.DeviceIdType.MESH
ANY = pl.BlockSpec(memory_space=pl.ANY)
VMEM = pl.BlockSpec(memory_space=pltpu.VMEM)
SMEM = pl.BlockSpec(memory_space=pltpu.SMEM)


def ctx_of(x, y, core):
    return (lax.rem(x, 4) * 2 + lax.rem(y, 2)) * 2 + lax.rem(core, 2)


def head_of(z, y):
    return lax.rem(z, 4) * 2 + lax.rem(y, 2)


def remote(src, dst, send, recv, ctx, head):
    return pltpu.make_async_remote_copy(
        src_ref=src,
        dst_ref=dst,
        send_sem=send,
        recv_sem=recv,
        device_id=(ctx, head),
        device_id_type=MESH,
    )


def exchange_kernel(
    route, q, k, v, g, qo, go, ko, vo, xq, xg, sq, sg,
    p1s, p1r, p2s, p2r, rs, rr, cs, cr, local,
):
    c = lax.axis_index("ctx")
    h = lax.axis_index("head")
    z, yh = h // 2, lax.rem(h, 2)
    x, yl, core = c // 4, lax.rem(c // 2, 2), lax.rem(c, 2)
    head_peers = [(jz, jy) for jz in range(4) for jy in range(2) if (jz, jy) != (0, 0)]
    ctx_peers = [
        (jx, jy, jc) for jx in range(4) for jy in range(2) for jc in range(2)
        if (jx, jy, jc) != (0, 0, 0)
    ]

    barrier = pltpu.get_barrier_semaphore()
    for jz, jy in head_peers:
        pl.semaphore_signal(
            barrier, inc=1, device_id=(c, head_of(z + jz, yh + jy)), device_id_type=MESH
        )
    for jx, jy, jc in ctx_peers:
        pl.semaphore_signal(
            barrier, inc=1, device_id=(ctx_of(x + jx, yl + jy, core + jc), h), device_id_type=MESH
        )
    pl.semaphore_wait(barrier, len(head_peers) + len(ctx_peers))

    sent = []

    def go_remote(copy):
        copy.start()
        sent.append(copy)
        return copy

    kv_rows = pl.ds(c * ROWS + h * 32, 32)
    p1 = [[], [], [], []]
    for jz, jy in head_peers:
        j = jz * 2 + jy
        peer = head_of(z + jz, yh + jy)
        cols = pl.ds(pl.multiple_of(peer * HD, HD), HD)
        for a, (src, dst) in enumerate(((k, ko), (v, vo))):
            p1[a].append(go_remote(remote(
                src.at[:, cols], dst.at[kv_rows], p1s.at[a, j], p1r.at[a, j], c, peer)))
    own_cols = pl.ds(pl.multiple_of(h * HD, HD), HD)
    own = [
        pltpu.make_async_copy(k.at[:, own_cols], ko.at[kv_rows], local.at[0]),
        pltpu.make_async_copy(v.at[:, own_cols], vo.at[kv_rows], local.at[1]),
    ]

    def first(a, src, dst):
        for jz, jy in head_peers:
            j = jz * 2 + jy
            peer = head_of(z + jz, yh + jy)
            cols = pl.ds(pl.multiple_of(peer * COLS, COLS), COLS)
            p1[2 + a].append(go_remote(remote(
                src.at[:, :, cols], dst.at[pl.ds(h * 2, 2)],
                p1s.at[2 + a, j], p1r.at[2 + a, j], c, peer)))
        cols = pl.ds(pl.multiple_of(h * COLS, COLS), COLS)
        own.append(pltpu.make_async_copy(
            src.at[:, :, cols], dst.at[pl.ds(h * 2, 2)], local.at[2 + a]))
        own[-1].start()

    for copy in own:
        copy.start()
    first(0, q, xq)

    kv = (ko, vo)

    def shard(a, dx, dy):
        return kv[a].at[pl.ds(ctx_of(x + dx, yl + dy, core) * ROWS, ROWS)]

    def ring(a, dx, dy, tx, ty):
        slot = ((dx - tx) % 4) * 2 + (dy - ty) % 2
        part = shard(a, dx, dy)
        return remote(part, part, rs.at[a, slot], rr.at[a, slot],
                      ctx_of(x + tx + 4, yl + ty + 2, core), h)

    def partner(a, dx, dy):
        slot = dx * 2 + dy
        part = shard(a, dx, dy)
        return remote(part, part, cs.at[a, slot], cr.at[a, slot], ctx_of(x, yl, core + 1), h)

    def arrived(a, dx, dy):
        slot = dx * 2 + dy
        part = shard(a, dx, dy)
        remote(part, part, rs.at[a, slot], rr.at[a, slot], c, h).wait_recv()

    for a in range(2):
        own[a].wait()
        for copy in p1[a]:
            copy.wait_recv()
    for a in range(2):
        go_remote(ring(a, 0, 0, 0, 1))
        go_remote(ring(a, 0, 0, 1, 0))
        go_remote(ring(a, 0, 0, -1, 0))
    first(1, g, xg)
    for a in range(2):
        go_remote(partner(a, 0, 0))

    def second(a, stage, send, out):
        own[2 + a].wait()
        for copy in p1[2 + a]:
            copy.wait_recv()

        def pick(d, carry):
            block = jnp.int32(0)
            for b in range(SHARDS):
                block = jnp.where(route[c, b] == d, b, block)
            send[d] = stage[block]
            return carry

        lax.fori_loop(0, SHARDS, pick, 0)
        mine = pltpu.make_async_copy(send.at[c], out.at[c], local.at[4 + a])
        mine.start()
        copies = []
        for jx, jy, jc in ctx_peers:
            j = (jx * 2 + jy) * 2 + jc
            d = ctx_of(x + jx, yl + jy, core + jc)
            copies.append(go_remote(remote(
                send.at[d], out.at[c], p2s.at[a, j], p2r.at[a, j], d, h)))
        return mine, copies

    def sides(dy):
        arrived(0, 3, dy)
        go_remote(ring(0, 3, dy, 1, 0))
        arrived(1, 1, dy)
        go_remote(ring(1, 1, dy, -1, 0))
        arrived(0, 1, dy)
        arrived(1, 3, dy)
        for a in range(2):
            go_remote(partner(a, 3, dy))
            go_remote(partner(a, 1, dy))

    sides(0)
    for a in range(2):
        arrived(a, 0, 1)
        go_remote(ring(a, 0, 1, 1, 0))
        go_remote(ring(a, 0, 1, -1, 0))
        go_remote(partner(a, 0, 1))
    mine_q, p2q = second(0, xq, sq, qo)
    sides(1)
    for a in range(2):
        arrived(a, 2, 0)
        go_remote(partner(a, 2, 0))
    mine_g, p2g = second(1, xg, sg, go)
    for a in range(2):
        arrived(a, 2, 1)
        go_remote(partner(a, 2, 1))
    mine_q.wait()
    mine_g.wait()

    def received(a, out):
        for jx, jy, jc in ctx_peers:
            j = (jx * 2 + jy) * 2 + jc
            src = ctx_of(x - jx + 4, yl - jy + 2, core - jc + 2)
            remote(out.at[src], out.at[src], p2s.at[a, j], p2r.at[a, j], c, h).wait_recv()

    received(0, qo)
    received(1, go)
    for a in range(2):
        for dx in range(4):
            for dy in range(2):
                slot = dx * 2 + dy
                part = kv[a].at[pl.ds(ctx_of(x + dx, yl + dy, core + 1) * ROWS, ROWS)]
                remote(part, part, cs.at[a, slot], cr.at[a, slot], c, h).wait_recv()
    for copy in sent:
        copy.wait_send()


def exchange(route, q, k, v, g):
    return pl.pallas_call(
        exchange_kernel,
        name="exchange",
        out_shape=(
            jax.ShapeDtypeStruct((SHARDS, BLOCK, COLS), BF),
            jax.ShapeDtypeStruct((SHARDS, BLOCK, COLS), BF),
            jax.ShapeDtypeStruct((SEQ, HD), BF),
            jax.ShapeDtypeStruct((SEQ, HD), BF),
        ),
        in_specs=[SMEM, ANY, VMEM, VMEM, ANY],
        out_specs=(ANY, ANY, ANY, ANY),
        scratch_shapes=[
            pltpu.VMEM((SHARDS, BLOCK, COLS), BF),
            pltpu.VMEM((SHARDS, BLOCK, COLS), BF),
            pltpu.VMEM((SHARDS, BLOCK, COLS), BF),
            pltpu.VMEM((SHARDS, BLOCK, COLS), BF),
            pltpu.SemaphoreType.DMA((4, 8)),
            pltpu.SemaphoreType.DMA((4, 8)),
            pltpu.SemaphoreType.DMA((2, 16)),
            pltpu.SemaphoreType.DMA((2, 16)),
            pltpu.SemaphoreType.DMA((2, 24)),
            pltpu.SemaphoreType.DMA((2, 8)),
            pltpu.SemaphoreType.DMA((2, 8)),
            pltpu.SemaphoreType.DMA((2, 8)),
            pltpu.SemaphoreType.DMA((6,)),
        ],
        compiler_params=pltpu.CompilerParams(collective_id=0, has_side_effects=True),
    )(route, q, k, v, g)


def attention_kernel(
    route, docs, q_hbm, g_hbm, k_hbm, v_hbm, att_hbm, dq_hbm, dkv_hbm,
    q, g, k, v, att, dq, dkv,
    s_buf, kt, vt, dk_acc, dv_acc, ot_acc, dqt_acc, starts, load, store,
):
    loads = [
        pltpu.make_async_copy(k_hbm, k, load.at[0]),
        pltpu.make_async_copy(v_hbm, v, load.at[1]),
        pltpu.make_async_copy(q_hbm, q, load.at[2]),
        pltpu.make_async_copy(g_hbm, g, load.at[3]),
    ]
    for copy in loads:
        copy.start()
    c = lax.axis_index("ctx")
    ends = []
    total = jnp.int32(0)
    for j in range(DOCS):
        total = total + docs[j]
        ends.append(total)

    def find(s, carry):
        block = jnp.int32(0)
        for b in range(SHARDS):
            block = jnp.where(route[s, b] == c, b, block)
        starts[s] = s * ROWS + block * BLOCK
        return carry

    lax.fori_loop(0, SHARDS, find, 0)
    loads[0].wait()
    loads[1].wait()

    def prepare(t, carry):
        kt[t] = k[t].T
        vt[t] = v[t].T
        return carry

    lax.fori_loop(0, SHARDS, prepare, 0)
    loads[2].wait()
    loads[3].wait()

    def stack(ref, first):
        parts = []
        for i in range(SPAN):
            rows = ref[first + i]
            parts += [rows[:, n * HD:(n + 1) * HD] for n in range(GROUP)]
        return jnp.concatenate(parts, axis=0)

    def outgoing(n):
        rows = pl.ds(n * SPAN, SPAN)
        return (
            pltpu.make_async_copy(att.at[rows], att_hbm.at[rows], store.at[0]),
            pltpu.make_async_copy(dq.at[rows], dq_hbm.at[rows], store.at[1]),
        )

    within = lax.rem(lax.broadcasted_iota(jnp.int32, (1, WIDTH), 1), BLOCK)
    key = lax.broadcasted_iota(jnp.int32, (ROWS, WIDTH), 0)

    def group(n, carry):
        first = n * SPAN
        qg = stack(q, first)
        gg = stack(g, first)
        qt = qg.T
        gt = gg.T
        q_pos = jnp.concatenate([within + starts[first + i] for i in range(SPAN)], axis=1)
        q_doc = jnp.zeros_like(q_pos)
        low = jnp.int32(0)
        high = jnp.int32(0)
        p_first = starts[first]
        p_last = starts[first + SPAN - 1] + BLOCK - 1
        for end in ends:
            q_doc = jnp.where(q_pos >= end, end, q_doc)
            low = jnp.where(p_first >= end, end, low)
            high = jnp.where(p_last >= end, end, high)
        t_low = low // ROWS
        t_full = jnp.minimum((high + ROWS - 1) // ROWS, first)
        reach = (q_pos - q_doc).astype(jnp.uint32)

        def scores(t, lane):
            s = jnp.dot(k[t], qt[:, lane:], preferred_element_type=F32)
            return s * (SCALE * LOG2E)

        def masked(t, lane):
            s = scores(t, lane)
            offset = t * ROWS - q_doc[:, lane:]
            parts = []
            for i in range(0, LANES - lane, WIDTH):
                past = (key + offset[:, i:i + WIDTH]).astype(jnp.uint32)
                seen = past <= reach[:, lane + i:lane + i + WIDTH]
                parts.append(jnp.where(seen, s[:, i:i + WIDTH], NEGATIVE))
            return jnp.concatenate(parts, axis=1)

        ot_acc[...] = jnp.zeros_like(ot_acc)
        dqt_acc[...] = jnp.zeros_like(dqt_acc)

        def forward(produce):
            def step(t, carried):
                peak, mass = carried
                s = produce(t, 0)
                s_buf[t] = s
                new_peak = jnp.maximum(peak, jnp.max(s, axis=0, keepdims=True))
                p = jnp.exp2(s - new_peak)
                fade = jnp.exp2(peak - new_peak)
                mass = mass * fade + jnp.sum(p, axis=0, keepdims=True)
                ot_acc[...] = ot_acc[...] * fade + jnp.dot(
                    vt[t], p.astype(BF), preferred_element_type=F32)
                return new_peak, mass

            return step

        peak, mass = lax.fori_loop(
            t_low, t_full, forward(masked),
            (jnp.full((1, LANES), FLOOR, F32), jnp.zeros((1, LANES), F32)))
        peak, mass = lax.fori_loop(t_full, first, forward(scores), (peak, mass))

        tops = [[peak[:, i * WIDTH:(i + 1) * WIDTH]] for i in range(SPAN)]
        for e in range(SPAN):
            s = masked(first + e, e * WIDTH)
            s_buf[first + e, :, e * WIDTH:] = s
            top = jnp.max(s, axis=0, keepdims=True)
            for i in range(e, SPAN):
                tops[i].append(top[:, (i - e) * WIDTH:(i - e + 1) * WIDTH])
        new_peak = jnp.concatenate([functools.reduce(jnp.maximum, t) for t in tops], axis=1)
        fade = jnp.exp2(peak - new_peak)
        mass = mass * fade
        masses = [[mass[:, i * WIDTH:(i + 1) * WIDTH]] for i in range(SPAN)]
        ot_acc[...] = ot_acc[...] * fade
        for e in range(SPAN):
            p = jnp.exp2(s_buf[first + e, :, e * WIDTH:] - new_peak[:, e * WIDTH:])
            add = jnp.sum(p, axis=0, keepdims=True)
            for i in range(e, SPAN):
                masses[i].append(add[:, (i - e) * WIDTH:(i - e + 1) * WIDTH])
            ot_acc[:, e * WIDTH:] += jnp.dot(
                vt[first + e], p.astype(BF), preferred_element_type=F32)
        mass = jnp.concatenate([functools.reduce(jnp.add, t) for t in masses], axis=1)
        lse = new_peak + jnp.log2(mass)
        ot = (ot_acc[...] * (1.0 / mass)).astype(BF)
        delta = jnp.sum(gt.astype(F32) * ot.astype(F32), axis=0, keepdims=True)
        o = ot.T
        for i in range(SPAN):
            for m in range(GROUP):
                r = (i * GROUP + m) * BLOCK
                att[first + i, :, m * HD:(m + 1) * HD] = o[r:r + BLOCK]

        def pull(t, lane):
            p = jnp.exp2(s_buf[t, :, lane:] - lse[:, lane:])
            dp = jnp.dot(v[t], gt[:, lane:], preferred_element_type=F32)
            ds = (p * (dp - delta[:, lane:])).astype(BF)
            grad_v = jnp.dot(p.astype(BF), gg[lane:], preferred_element_type=F32)
            grad_k = jnp.dot(ds, qg[lane:], preferred_element_type=F32)
            dqt_acc[:, lane:] += jnp.dot(kt[t], ds, preferred_element_type=F32)
            return grad_v, grad_k

        for e in range(SPAN):
            grad_v, grad_k = pull(first + e, e * WIDTH)
            dv_acc[first + e] = grad_v
            dk_acc[first + e] = grad_k

        def backward(t, carried):
            grad_v, grad_k = pull(t, 0)
            dv_acc[t] += grad_v
            dk_acc[t] += grad_k
            return carried

        lax.fori_loop(t_low, first, backward, 0)
        grad = dqt_acc[...].T * SCALE
        for i in range(SPAN):
            for m in range(GROUP):
                r = (i * GROUP + m) * BLOCK
                dq[first + i, :, m * HD:(m + 1) * HD] = grad[r:r + BLOCK]
        for copy in outgoing(n):
            copy.start()
        return carry

    lax.fori_loop(0, SHARDS // SPAN, group, 0)

    def regroup(s, carry):
        for b in range(SHARDS):
            d = route[s, b]
            rows = slice(b * BLOCK, (b + 1) * BLOCK)
            dkv[d, 0, s] = (dk_acc[s, rows] * SCALE).astype(BF)
            dkv[d, 1, s] = dv_acc[s, rows].astype(BF)
        return carry

    lax.fori_loop(0, SHARDS, regroup, 0)
    last = pltpu.make_async_copy(dkv, dkv_hbm, load.at[0])
    last.start()
    pltpu.make_async_copy(att, att_hbm, store.at[0]).wait()
    pltpu.make_async_copy(dq, dq_hbm, store.at[1]).wait()
    last.wait()


def attention(route, docs, q, g, k, v):
    return pl.pallas_call(
        attention_kernel,
        name="attention",
        out_shape=(
            jax.ShapeDtypeStruct((SHARDS, BLOCK, COLS), BF),
            jax.ShapeDtypeStruct((SHARDS, BLOCK, COLS), F32),
            jax.ShapeDtypeStruct((SHARDS, 2, SHARDS, BLOCK, HD), BF),
        ),
        in_specs=[SMEM, SMEM, ANY, ANY, ANY, ANY],
        out_specs=(ANY, ANY, ANY),
        scratch_shapes=[
            pltpu.VMEM((SHARDS, BLOCK, COLS), BF),
            pltpu.VMEM((SHARDS, BLOCK, COLS), BF),
            pltpu.VMEM((SHARDS, ROWS, HD), BF),
            pltpu.VMEM((SHARDS, ROWS, HD), BF),
            pltpu.VMEM((SHARDS, BLOCK, COLS), BF),
            pltpu.VMEM((SHARDS, BLOCK, COLS), F32),
            pltpu.VMEM((SHARDS, 2, SHARDS, BLOCK, HD), BF),
            pltpu.VMEM((SHARDS, ROWS, LANES), F32),
            pltpu.VMEM((SHARDS, HD, ROWS), BF),
            pltpu.VMEM((SHARDS, HD, ROWS), BF),
            pltpu.VMEM((SHARDS, ROWS, HD), F32),
            pltpu.VMEM((SHARDS, ROWS, HD), F32),
            pltpu.VMEM((HD, LANES), F32),
            pltpu.VMEM((HD, LANES), F32),
            pltpu.SMEM((SHARDS,), jnp.int32),
            pltpu.SemaphoreType.DMA((4,)),
            pltpu.SemaphoreType.DMA((2,)),
        ],
    )(route, docs, q, g, k, v)


def reduce_kernel(part, chip, keep, mine, mate, kept, s1, r1, s2, r2, local):
    c = lax.axis_index("ctx")
    h = lax.axis_index("head")
    x, yl, core = c // 4, lax.rem(c // 2, 2), lax.rem(c, 2)
    peers = [(jx, jy) for jx in range(4) for jy in range(2) if (jx, jy) != (0, 0)]
    order = peers + [(0, 0)]
    other = ctx_of(x, yl, core + 1)

    def place(jx, jy):
        return lax.rem(x + jx, 4) * 2 + lax.rem(yl + jy, 2)

    loads = []
    for jx, jy in order:
        t = place(jx, jy)
        copy = pltpu.make_async_copy(part.at[t * 2 + core], mine.at[t], local.at[jx * 2 + jy])
        copy.start()
        loads.append(copy)

    barrier = pltpu.get_barrier_semaphore()
    pl.semaphore_signal(barrier, inc=1, device_id=(other, h), device_id_type=MESH)
    for jx, jy in peers:
        pl.semaphore_signal(
            barrier, inc=1, device_id=(ctx_of(x + jx, yl + jy, core), h), device_id_type=MESH)
    pl.semaphore_wait(barrier, len(peers) + 1)

    first = []
    for jx, jy in order:
        j = jx * 2 + jy
        t = place(jx, jy)
        copy = remote(part.at[t * 2 + 1 - core], mate.at[t], s1.at[j], r1.at[j], other, h)
        copy.start()
        first.append(copy)
    second = []
    for (jx, jy), copy, load in zip(order, first, loads):
        j = jx * 2 + jy
        t = place(jx, jy)
        load.wait()
        copy.wait_recv()
        pair = mine[t].astype(F32) + mate[t].astype(F32)
        if (jx, jy) == (0, 0):
            kept[...] = pair
        else:
            mate[t] = pair.astype(BF)
            copy = remote(mate.at[t], chip.at[j - 1], s2.at[j], r2.at[j],
                          ctx_of(x + jx, yl + jy, core), h)
            copy.start()
            second.append(copy)
    out = pltpu.make_async_copy(kept, keep, local.at[0])
    out.start()
    for copy in second:
        copy.wait_recv()
    for copy in first + second:
        copy.wait_send()
    out.wait()


def reduce(part):
    shape = (2, SHARDS, BLOCK, HD)
    return pl.pallas_call(
        reduce_kernel,
        name="reduce",
        out_shape=(
            jax.ShapeDtypeStruct((7,) + shape, BF),
            jax.ShapeDtypeStruct(shape, F32),
        ),
        in_specs=[ANY],
        out_specs=(ANY, ANY),
        scratch_shapes=[
            pltpu.VMEM((8,) + shape, BF),
            pltpu.VMEM((8,) + shape, BF),
            pltpu.VMEM(shape, F32),
            pltpu.SemaphoreType.DMA((8,)),
            pltpu.SemaphoreType.DMA((8,)),
            pltpu.SemaphoreType.DMA((8,)),
            pltpu.SemaphoreType.DMA((8,)),
            pltpu.SemaphoreType.DMA((8,)),
        ],
        compiler_params=pltpu.CompilerParams(collective_id=1, has_side_effects=True),
    )(part)


def finish_kernel(chip, keep, dk, dv):
    for a, out in enumerate((dk, dv)):
        def add(s, carry):
            total = keep[a, s]
            for j in range(7):
                total = total + chip[j, a, s].astype(F32)
            out[s] = total
            return carry

        lax.fori_loop(0, SHARDS, add, 0)


def finish(chip, keep):
    out = jax.ShapeDtypeStruct((SHARDS, BLOCK, HD), F32)
    return pl.pallas_call(
        finish_kernel,
        name="finish",
        out_shape=(out, out),
        in_specs=[VMEM, VMEM],
        out_specs=(VMEM, VMEM),
    )(chip, keep)


def on_device(queries, key_rows, value_rows, cotangent, doc_lengths, block_route):
    q, g, k, v = exchange(
        block_route,
        queries.reshape(2, BLOCK, HEADS * COLS),
        key_rows,
        value_rows,
        cotangent.reshape(2, BLOCK, HEADS * COLS),
    )
    att, dq, part = attention(
        block_route, doc_lengths, q, g, k.reshape(SHARDS, ROWS, HD), v.reshape(SHARDS, ROWS, HD))
    dk, dv = finish(*reduce(part))
    return (
        att.reshape(ROWS, COLS),
        dq.reshape(ROWS, COLS),
        dk.reshape(ROWS, HD),
        dv.reshape(ROWS, HD),
    )


def solution(mesh):
    placed = P(("ctx", "head"), None)
    return jax.shard_map(
        on_device,
        mesh=mesh,
        in_specs=(placed, placed, placed, placed, P(), P()),
        out_specs=(P("ctx", "head"),) * 4,
        check_vma=False,
    )
```

```python
import functools
import math

import jax
import jax.numpy as jnp
from jax import lax
from jax.experimental import pallas as pl
from jax.experimental.pallas import tpu as pltpu
from jax.sharding import PartitionSpec as P

HD = 128
GROUP = 8
SHARDS = 16
BLOCK = 16
ROWS = SHARDS * BLOCK
SEQ = SHARDS * ROWS
DOCS = 8
HEADS = 8
COLS = GROUP * HD

SPAN = 4
WIDTH = GROUP * BLOCK
LANES = SPAN * WIDTH
NEGATIVE = -1e30
FLOOR = -0.5e30
SCALE = 1.0 / math.sqrt(HD)
LOG2E = 1.4426950408889634

BF = jnp.bfloat16
F32 = jnp.float32
MESH = pl.DeviceIdType.MESH
ANY = pl.BlockSpec(memory_space=pl.ANY)
VMEM = pl.BlockSpec(memory_space=pltpu.VMEM)
SMEM = pl.BlockSpec(memory_space=pltpu.SMEM)


def ctx_of(x, y, core):
    return (lax.rem(x, 4) * 2 + lax.rem(y, 2)) * 2 + lax.rem(core, 2)


def head_of(z, y):
    return lax.rem(z, 4) * 2 + lax.rem(y, 2)


def remote(src, dst, send, recv, ctx, head):
    return pltpu.make_async_remote_copy(
        src_ref=src,
        dst_ref=dst,
        send_sem=send,
        recv_sem=recv,
        device_id=(ctx, head),
        device_id_type=MESH,
    )


def exchange_kernel(
    route, q, k, v, g, qo, go, ko, vo, xq, xg, sq, sg,
    p1s, p1r, p2s, p2r, rs, rr, cs, cr, local,
):
    c = lax.axis_index("ctx")
    h = lax.axis_index("head")
    z, yh = h // 2, lax.rem(h, 2)
    x, yl, core = c // 4, lax.rem(c // 2, 2), lax.rem(c, 2)
    head_peers = [(jz, jy) for jz in range(4) for jy in range(2) if (jz, jy) != (0, 0)]
    ctx_peers = [
        (jx, jy, jc) for jx in range(4) for jy in range(2) for jc in range(2)
        if (jx, jy, jc) != (0, 0, 0)
    ]

    barrier = pltpu.get_barrier_semaphore()
    for jz, jy in head_peers:
        pl.semaphore_signal(
            barrier, inc=1, device_id=(c, head_of(z + jz, yh + jy)), device_id_type=MESH
        )
    for jx, jy, jc in ctx_peers:
        pl.semaphore_signal(
            barrier, inc=1, device_id=(ctx_of(x + jx, yl + jy, core + jc), h), device_id_type=MESH
        )
    pl.semaphore_wait(barrier, len(head_peers) + len(ctx_peers))

    sent = []

    def go_remote(copy):
        copy.start()
        sent.append(copy)
        return copy

    kv_rows = pl.ds(c * ROWS + h * 32, 32)
    p1 = [[], [], [], []]
    for jz, jy in head_peers:
        j = jz * 2 + jy
        peer = head_of(z + jz, yh + jy)
        cols = pl.ds(pl.multiple_of(peer * HD, HD), HD)
        for a, (src, dst) in enumerate(((k, ko), (v, vo))):
            p1[a].append(go_remote(remote(
                src.at[:, cols], dst.at[kv_rows], p1s.at[a, j], p1r.at[a, j], c, peer)))
    own_cols = pl.ds(pl.multiple_of(h * HD, HD), HD)
    own = [
        pltpu.make_async_copy(k.at[:, own_cols], ko.at[kv_rows], local.at[0]),
        pltpu.make_async_copy(v.at[:, own_cols], vo.at[kv_rows], local.at[1]),
    ]

    def first(a, src, dst):
        for jz, jy in head_peers:
            j = jz * 2 + jy
            peer = head_of(z + jz, yh + jy)
            cols = pl.ds(pl.multiple_of(peer * COLS, COLS), COLS)
            p1[2 + a].append(go_remote(remote(
                src.at[:, :, cols], dst.at[pl.ds(h * 2, 2)],
                p1s.at[2 + a, j], p1r.at[2 + a, j], c, peer)))
        cols = pl.ds(pl.multiple_of(h * COLS, COLS), COLS)
        own.append(pltpu.make_async_copy(
            src.at[:, :, cols], dst.at[pl.ds(h * 2, 2)], local.at[2 + a]))
        own[-1].start()

    for copy in own:
        copy.start()
    first(0, q, xq)

    kv = (ko, vo)

    def shard(a, dx, dy):
        return kv[a].at[pl.ds(ctx_of(x + dx, yl + dy, core) * ROWS, ROWS)]

    def ring(a, dx, dy, tx, ty):
        slot = ((dx - tx) % 4) * 2 + (dy - ty) % 2
        part = shard(a, dx, dy)
        return remote(part, part, rs.at[a, slot], rr.at[a, slot],
                      ctx_of(x + tx + 4, yl + ty + 2, core), h)

    def partner(a, dx, dy):
        slot = dx * 2 + dy
        part = shard(a, dx, dy)
        return remote(part, part, cs.at[a, slot], cr.at[a, slot], ctx_of(x, yl, core + 1), h)

    def arrived(a, dx, dy):
        slot = dx * 2 + dy
        part = shard(a, dx, dy)
        remote(part, part, rs.at[a, slot], rr.at[a, slot], c, h).wait_recv()

    for a in range(2):
        own[a].wait()
        for copy in p1[a]:
            copy.wait_recv()
    for a in range(2):
        go_remote(ring(a, 0, 0, 0, 1))
        go_remote(ring(a, 0, 0, 1, 0))
        go_remote(ring(a, 0, 0, -1, 0))
    first(1, g, xg)
    for a in range(2):
        go_remote(partner(a, 0, 0))

    def second(a, stage, send, out):
        own[2 + a].wait()
        for copy in p1[2 + a]:
            copy.wait_recv()

        def pick(d, carry):
            block = jnp.int32(0)
            for b in range(SHARDS):
                block = jnp.where(route[c, b] == d, b, block)
            send[d] = stage[block]
            return carry

        lax.fori_loop(0, SHARDS, pick, 0)
        mine = pltpu.make_async_copy(send.at[c], out.at[c], local.at[4 + a])
        mine.start()
        copies = []
        for jx, jy, jc in ctx_peers:
            j = (jx * 2 + jy) * 2 + jc
            d = ctx_of(x + jx, yl + jy, core + jc)
            copies.append(go_remote(remote(
                send.at[d], out.at[c], p2s.at[a, j], p2r.at[a, j], d, h)))
        return mine, copies

    def sides(dy):
        arrived(0, 3, dy)
        go_remote(ring(0, 3, dy, 1, 0))
        arrived(1, 1, dy)
        go_remote(ring(1, 1, dy, -1, 0))
        arrived(0, 1, dy)
        arrived(1, 3, dy)
        for a in range(2):
            go_remote(partner(a, 3, dy))
            go_remote(partner(a, 1, dy))

    sides(0)
    for a in range(2):
        arrived(a, 0, 1)
        go_remote(ring(a, 0, 1, 1, 0))
        go_remote(ring(a, 0, 1, -1, 0))
        go_remote(partner(a, 0, 1))
    mine_q, p2q = second(0, xq, sq, qo)
    sides(1)
    for a in range(2):
        arrived(a, 2, 0)
        go_remote(partner(a, 2, 0))
    mine_g, p2g = second(1, xg, sg, go)
    for a in range(2):
        arrived(a, 2, 1)
        go_remote(partner(a, 2, 1))
    mine_q.wait()
    mine_g.wait()

    def received(a, out):
        for jx, jy, jc in ctx_peers:
            j = (jx * 2 + jy) * 2 + jc
            src = ctx_of(x - jx + 4, yl - jy + 2, core - jc + 2)
            remote(out.at[src], out.at[src], p2s.at[a, j], p2r.at[a, j], c, h).wait_recv()

    received(0, qo)
    received(1, go)
    for a in range(2):
        for dx in range(4):
            for dy in range(2):
                slot = dx * 2 + dy
                part = kv[a].at[pl.ds(ctx_of(x + dx, yl + dy, core + 1) * ROWS, ROWS)]
                remote(part, part, cs.at[a, slot], cr.at[a, slot], c, h).wait_recv()
    for copy in sent:
        copy.wait_send()


def exchange(route, q, k, v, g):
    return pl.pallas_call(
        exchange_kernel,
        name="exchange",
        out_shape=(
            jax.ShapeDtypeStruct((SHARDS, BLOCK, COLS), BF),
            jax.ShapeDtypeStruct((SHARDS, BLOCK, COLS), BF),
            jax.ShapeDtypeStruct((SEQ, HD), BF),
            jax.ShapeDtypeStruct((SEQ, HD), BF),
        ),
        in_specs=[SMEM, ANY, VMEM, VMEM, ANY],
        out_specs=(ANY, ANY, ANY, ANY),
        scratch_shapes=[
            pltpu.VMEM((SHARDS, BLOCK, COLS), BF),
            pltpu.VMEM((SHARDS, BLOCK, COLS), BF),
            pltpu.VMEM((SHARDS, BLOCK, COLS), BF),
            pltpu.VMEM((SHARDS, BLOCK, COLS), BF),
            pltpu.SemaphoreType.DMA((4, 8)),
            pltpu.SemaphoreType.DMA((4, 8)),
            pltpu.SemaphoreType.DMA((2, 16)),
            pltpu.SemaphoreType.DMA((2, 16)),
            pltpu.SemaphoreType.DMA((2, 24)),
            pltpu.SemaphoreType.DMA((2, 8)),
            pltpu.SemaphoreType.DMA((2, 8)),
            pltpu.SemaphoreType.DMA((2, 8)),
            pltpu.SemaphoreType.DMA((6,)),
        ],
        compiler_params=pltpu.CompilerParams(collective_id=0, has_side_effects=True),
    )(route, q, k, v, g)


def attention_kernel(
    route, docs, q_hbm, g_hbm, k_hbm, v_hbm, att_hbm, dq_hbm, dkv_hbm,
    q, g, k, v, att, dq, dkv,
    s_buf, kt, vt, dk_acc, dv_acc, ot_acc, dqt_acc, starts, load, store,
):
    loads = [
        pltpu.make_async_copy(k_hbm, k, load.at[0]),
        pltpu.make_async_copy(v_hbm, v, load.at[1]),
        pltpu.make_async_copy(q_hbm, q, load.at[2]),
        pltpu.make_async_copy(g_hbm, g, load.at[3]),
    ]
    for copy in loads:
        copy.start()
    c = lax.axis_index("ctx")
    ends = []
    total = jnp.int32(0)
    for j in range(DOCS):
        total = total + docs[j]
        ends.append(total)

    def find(s, carry):
        block = jnp.int32(0)
        for b in range(SHARDS):
            block = jnp.where(route[s, b] == c, b, block)
        starts[s] = s * ROWS + block * BLOCK
        return carry

    lax.fori_loop(0, SHARDS, find, 0)
    loads[0].wait()
    loads[1].wait()

    def prepare(t, carry):
        kt[t] = k[t].T
        vt[t] = v[t].T
        return carry

    lax.fori_loop(0, SHARDS, prepare, 0)
    loads[2].wait()
    loads[3].wait()

    def stack(ref, first):
        parts = []
        for i in range(SPAN):
            rows = ref[first + i]
            parts += [rows[:, n * HD:(n + 1) * HD] for n in range(GROUP)]
        return jnp.concatenate(parts, axis=0)

    def outgoing(n):
        rows = pl.ds(n * SPAN, SPAN)
        return (
            pltpu.make_async_copy(att.at[rows], att_hbm.at[rows], store.at[0]),
            pltpu.make_async_copy(dq.at[rows], dq_hbm.at[rows], store.at[1]),
        )

    within = lax.rem(lax.broadcasted_iota(jnp.int32, (1, WIDTH), 1), BLOCK)
    key = lax.broadcasted_iota(jnp.int32, (ROWS, WIDTH), 0)

    def group(n, carry):
        first = n * SPAN
        qg = stack(q, first)
        gg = stack(g, first)
        qt = qg.T
        gt = gg.T
        q_pos = jnp.concatenate([within + starts[first + i] for i in range(SPAN)], axis=1)
        q_doc = jnp.zeros_like(q_pos)
        marks = [starts[first], starts[first + 1], starts[first + 2],
                 starts[first + SPAN - 1] + BLOCK - 1]
        lows = [jnp.int32(0)] * 4
        for end in ends:
            q_doc = jnp.where(q_pos >= end, end, q_doc)
            lows = [jnp.where(mark >= end, end, low) for mark, low in zip(marks, lows)]
        t_one, t_two, t_low = [jnp.minimum(low // ROWS, first) for low in lows[:3]]
        t_full = jnp.minimum((lows[3] + ROWS - 1) // ROWS, first)
        reach = (q_pos - q_doc).astype(jnp.uint32)

        def scores(t, lane, stop=LANES):
            s = jnp.dot(k[t], qt[:, lane:stop], preferred_element_type=F32)
            return s * (SCALE * LOG2E)

        def masked(t, lane, stop=LANES):
            s = scores(t, lane, stop)
            offset = t * ROWS - q_doc[:, lane:stop]
            parts = []
            for i in range(0, stop - lane, WIDTH):
                past = (key + offset[:, i:i + WIDTH]).astype(jnp.uint32)
                seen = past <= reach[:, lane + i:lane + i + WIDTH]
                parts.append(jnp.where(seen, s[:, i:i + WIDTH], NEGATIVE))
            return jnp.concatenate(parts, axis=1)

        ot_acc[...] = jnp.zeros_like(ot_acc)
        dqt_acc[...] = jnp.zeros_like(dqt_acc)

        def forward(produce, stop=LANES):
            def step(t, carried):
                peak, mass = carried
                s = produce(t, 0, stop)
                s_buf[t, :, :stop] = s
                new_peak = jnp.maximum(peak[:, :stop], jnp.max(s, axis=0, keepdims=True))
                p = jnp.exp2(s - new_peak)
                fade = jnp.exp2(peak[:, :stop] - new_peak)
                new_mass = mass[:, :stop] * fade + jnp.sum(p, axis=0, keepdims=True)
                ot_acc[:, :stop] = ot_acc[:, :stop] * fade + jnp.dot(
                    vt[t], p.astype(BF), preferred_element_type=F32)
                if stop < LANES:
                    new_peak = jnp.concatenate([new_peak, peak[:, stop:]], axis=1)
                    new_mass = jnp.concatenate([new_mass, mass[:, stop:]], axis=1)
                return new_peak, new_mass

            return step

        state = (jnp.full((1, LANES), FLOOR, F32), jnp.zeros((1, LANES), F32))
        state = lax.fori_loop(t_one, t_two, forward(masked, WIDTH), state)
        state = lax.fori_loop(t_two, t_low, forward(masked, 2 * WIDTH), state)
        state = lax.fori_loop(t_low, t_full, forward(masked), state)
        peak, mass = lax.fori_loop(t_full, first, forward(scores), state)

        tops = [[peak[:, i * WIDTH:(i + 1) * WIDTH]] for i in range(SPAN)]
        for e in range(SPAN):
            s = masked(first + e, e * WIDTH)
            s_buf[first + e, :, e * WIDTH:] = s
            top = jnp.max(s, axis=0, keepdims=True)
            for i in range(e, SPAN):
                tops[i].append(top[:, (i - e) * WIDTH:(i - e + 1) * WIDTH])
        new_peak = jnp.concatenate([functools.reduce(jnp.maximum, t) for t in tops], axis=1)
        fade = jnp.exp2(peak - new_peak)
        mass = mass * fade
        masses = [[mass[:, i * WIDTH:(i + 1) * WIDTH]] for i in range(SPAN)]
        ot_acc[...] = ot_acc[...] * fade
        for e in range(SPAN):
            p = jnp.exp2(s_buf[first + e, :, e * WIDTH:] - new_peak[:, e * WIDTH:])
            add = jnp.sum(p, axis=0, keepdims=True)
            for i in range(e, SPAN):
                masses[i].append(add[:, (i - e) * WIDTH:(i - e + 1) * WIDTH])
            ot_acc[:, e * WIDTH:] += jnp.dot(
                vt[first + e], p.astype(BF), preferred_element_type=F32)
        mass = jnp.concatenate([functools.reduce(jnp.add, t) for t in masses], axis=1)
        lse = new_peak + jnp.log2(mass)
        ot = (ot_acc[...] * (1.0 / mass)).astype(BF)
        delta = jnp.sum(gt.astype(F32) * ot.astype(F32), axis=0, keepdims=True)
        o = ot.T
        for i in range(SPAN):
            for m in range(GROUP):
                r = (i * GROUP + m) * BLOCK
                att[first + i, :, m * HD:(m + 1) * HD] = o[r:r + BLOCK]

        def pull(t, lane, stop=LANES):
            p = jnp.exp2(s_buf[t, :, lane:stop] - lse[:, lane:stop])
            dp = jnp.dot(v[t], gt[:, lane:stop], preferred_element_type=F32)
            ds = (p * (dp - delta[:, lane:stop])).astype(BF)
            grad_v = jnp.dot(p.astype(BF), gg[lane:stop], preferred_element_type=F32)
            grad_k = jnp.dot(ds, qg[lane:stop], preferred_element_type=F32)
            dqt_acc[:, lane:stop] += jnp.dot(kt[t], ds, preferred_element_type=F32)
            return grad_v, grad_k

        for e in range(SPAN):
            grad_v, grad_k = pull(first + e, e * WIDTH)
            dv_acc[first + e] = grad_v
            dk_acc[first + e] = grad_k

        def backward(stop):
            def step(t, carried):
                grad_v, grad_k = pull(t, 0, stop)
                dv_acc[t] += grad_v
                dk_acc[t] += grad_k
                return carried

            return step

        lax.fori_loop(t_one, t_two, backward(WIDTH), 0)
        lax.fori_loop(t_two, t_low, backward(2 * WIDTH), 0)
        lax.fori_loop(t_low, first, backward(LANES), 0)
        grad = dqt_acc[...].T * SCALE
        for i in range(SPAN):
            for m in range(GROUP):
                r = (i * GROUP + m) * BLOCK
                dq[first + i, :, m * HD:(m + 1) * HD] = grad[r:r + BLOCK]
        for copy in outgoing(n):
            copy.start()
        return carry

    lax.fori_loop(0, SHARDS // SPAN, group, 0)

    def regroup(s, carry):
        for b in range(SHARDS):
            d = route[s, b]
            rows = slice(b * BLOCK, (b + 1) * BLOCK)
            dkv[d, 0, s] = (dk_acc[s, rows] * SCALE).astype(BF)
            dkv[d, 1, s] = dv_acc[s, rows].astype(BF)
        return carry

    lax.fori_loop(0, SHARDS, regroup, 0)
    last = pltpu.make_async_copy(dkv, dkv_hbm, load.at[0])
    last.start()
    pltpu.make_async_copy(att, att_hbm, store.at[0]).wait()
    pltpu.make_async_copy(dq, dq_hbm, store.at[1]).wait()
    last.wait()


def attention(route, docs, q, g, k, v):
    return pl.pallas_call(
        attention_kernel,
        name="attention",
        out_shape=(
            jax.ShapeDtypeStruct((SHARDS, BLOCK, COLS), BF),
            jax.ShapeDtypeStruct((SHARDS, BLOCK, COLS), F32),
            jax.ShapeDtypeStruct((SHARDS, 2, SHARDS, BLOCK, HD), BF),
        ),
        in_specs=[SMEM, SMEM, ANY, ANY, ANY, ANY],
        out_specs=(ANY, ANY, ANY),
        scratch_shapes=[
            pltpu.VMEM((SHARDS, BLOCK, COLS), BF),
            pltpu.VMEM((SHARDS, BLOCK, COLS), BF),
            pltpu.VMEM((SHARDS, ROWS, HD), BF),
            pltpu.VMEM((SHARDS, ROWS, HD), BF),
            pltpu.VMEM((SHARDS, BLOCK, COLS), BF),
            pltpu.VMEM((SHARDS, BLOCK, COLS), F32),
            pltpu.VMEM((SHARDS, 2, SHARDS, BLOCK, HD), BF),
            pltpu.VMEM((SHARDS, ROWS, LANES), F32),
            pltpu.VMEM((SHARDS, HD, ROWS), BF),
            pltpu.VMEM((SHARDS, HD, ROWS), BF),
            pltpu.VMEM((SHARDS, ROWS, HD), F32),
            pltpu.VMEM((SHARDS, ROWS, HD), F32),
            pltpu.VMEM((HD, LANES), F32),
            pltpu.VMEM((HD, LANES), F32),
            pltpu.SMEM((SHARDS,), jnp.int32),
            pltpu.SemaphoreType.DMA((4,)),
            pltpu.SemaphoreType.DMA((2,)),
        ],
    )(route, docs, q, g, k, v)


def reduce_kernel(
    part, chip, keep, mine, mate, hold, kept, from_y, from_x,
    s1, r1, sy, ry, sx, rx, s2, r2, local,
):
    c = lax.axis_index("ctx")
    h = lax.axis_index("head")
    x, yl, core = c // 4, lax.rem(c // 2, 2), lax.rem(c, 2)
    other = ctx_of(x, yl, core + 1)
    across = ctx_of(x, yl + 1, core)
    far = (2, 1, 3, 0)
    order = [(dx, dy) for dx in far for dy in (1, 0)]

    def along(dx):
        return ctx_of(x + dx, yl, core)

    def place(dx, dy):
        return lax.rem(x + dx, 4) * 2 + lax.rem(yl + dy, 2)

    loads = []
    for i, (dx, dy) in enumerate(order):
        t = place(dx, dy)
        copy = pltpu.make_async_copy(part.at[t * 2 + core], mine.at[t], local.at[i])
        copy.start()
        loads.append(copy)

    barrier = pltpu.get_barrier_semaphore()
    for peer in (other, across, along(1), along(2), along(3)):
        pl.semaphore_signal(barrier, inc=1, device_id=(peer, h), device_id_type=MESH)
    pl.semaphore_wait(barrier, 5)

    sent = []

    def start(*args):
        copy = remote(*args, h)
        copy.start()
        sent.append(copy)
        return copy

    pairs = []
    for i, (dx, dy) in enumerate(order):
        t = place(dx, dy)
        pairs.append(start(part.at[t * 2 + 1 - core], mate.at[t], s1.at[i], r1.at[i], other))

    for (dx, dy), pair, load in zip(order, pairs, loads):
        t = place(dx, dy)
        load.wait()
        pair.wait_recv()
        if dy == 1:
            mate[t, 0] = (mine[t, 0].astype(F32) + mate[t, 0].astype(F32)).astype(BF)
            start(mate.at[t, 0], from_y.at[dx], sy.at[dx], ry.at[dx], across)
        else:
            hold[dx] = mine[t, 0].astype(F32) + mate[t, 0].astype(F32)
        if dx == 0:
            kept[1 - dy] = mine[t, 1].astype(F32) + mate[t, 1].astype(F32)
        else:
            mate[t, 1] = (mine[t, 1].astype(F32) + mate[t, 1].astype(F32)).astype(BF)
            start(mate.at[t, 1], from_x.at[dx - 1, dy], sx.at[dx - 1, dy], rx.at[dx - 1, dy],
                  along(dx))

    for dx in far:
        remote(from_y.at[dx], from_y.at[dx], sy.at[dx], ry.at[dx], across, h).wait_recv()
        hold[dx] += from_y[dx].astype(F32)
        if dx:
            t = place(dx, 0)
            mate[t, 0] = hold[dx].astype(BF)
            start(mate.at[t, 0], chip.at[dx - 1], s2.at[dx], r2.at[dx], along(dx))
    for dy in (1, 0):
        for dx in (1, 3, 2):
            part_in = from_x.at[dx - 1, dy]
            remote(part_in, part_in, sx.at[dx - 1, dy], rx.at[dx - 1, dy], across, h).wait_recv()
            kept[1 - dy] += from_x[dx - 1, dy].astype(F32)
        if dy:
            t = place(0, 1)
            mate[t, 1] = kept[0].astype(BF)
            start(mate.at[t, 1], chip.at[3], s2.at[0], r2.at[0], across)
    outs = [
        pltpu.make_async_copy(hold.at[0], keep.at[0], local.at[0]),
        pltpu.make_async_copy(kept.at[1], keep.at[1], local.at[1]),
    ]
    for out in outs:
        out.start()
    for j in range(4):
        slot = chip.at[(j + 3) % 4]
        remote(slot, slot, s2.at[j], r2.at[j], across, h).wait_recv()
    for copy in sent:
        copy.wait_send()
    for out in outs:
        out.wait()


def reduce(part):
    shape = (SHARDS, BLOCK, HD)
    return pl.pallas_call(
        reduce_kernel,
        name="reduce",
        out_shape=(
            jax.ShapeDtypeStruct((4,) + shape, BF),
            jax.ShapeDtypeStruct((2,) + shape, F32),
        ),
        in_specs=[ANY],
        out_specs=(ANY, ANY),
        scratch_shapes=[
            pltpu.VMEM((8, 2) + shape, BF),
            pltpu.VMEM((8, 2) + shape, BF),
            pltpu.VMEM((4,) + shape, F32),
            pltpu.VMEM((2,) + shape, F32),
            pltpu.VMEM((4,) + shape, BF),
            pltpu.VMEM((3, 2) + shape, BF),
            pltpu.SemaphoreType.DMA((8,)),
            pltpu.SemaphoreType.DMA((8,)),
            pltpu.SemaphoreType.DMA((4,)),
            pltpu.SemaphoreType.DMA((4,)),
            pltpu.SemaphoreType.DMA((3, 2)),
            pltpu.SemaphoreType.DMA((3, 2)),
            pltpu.SemaphoreType.DMA((4,)),
            pltpu.SemaphoreType.DMA((4,)),
            pltpu.SemaphoreType.DMA((8,)),
        ],
        compiler_params=pltpu.CompilerParams(collective_id=1, has_side_effects=True),
    )(part)


def finish_kernel(chip, keep, dk, dv):
    def add(s, carry):
        dk[s] = keep[0, s] + chip[0, s].astype(F32) + chip[1, s].astype(F32) + chip[2, s].astype(F32)
        dv[s] = keep[1, s] + chip[3, s].astype(F32)
        return carry

    lax.fori_loop(0, SHARDS, add, 0)


def finish(chip, keep):
    out = jax.ShapeDtypeStruct((SHARDS, BLOCK, HD), F32)
    return pl.pallas_call(
        finish_kernel,
        name="finish",
        out_shape=(out, out),
        in_specs=[VMEM, VMEM],
        out_specs=(VMEM, VMEM),
    )(chip, keep)


def on_device(queries, key_rows, value_rows, cotangent, doc_lengths, block_route):
    q, g, k, v = exchange(
        block_route,
        queries.reshape(2, BLOCK, HEADS * COLS),
        key_rows,
        value_rows,
        cotangent.reshape(2, BLOCK, HEADS * COLS),
    )
    att, dq, part = attention(
        block_route, doc_lengths, q, g, k.reshape(SHARDS, ROWS, HD), v.reshape(SHARDS, ROWS, HD))
    dk, dv = finish(*reduce(part))
    return (
        att.reshape(ROWS, COLS),
        dq.reshape(ROWS, COLS),
        dk.reshape(ROWS, HD),
        dv.reshape(ROWS, HD),
    )


def solution(mesh):
    placed = P(("ctx", "head"), None)
    return jax.shard_map(
        on_device,
        mesh=mesh,
        in_specs=(placed, placed, placed, placed, P(), P()),
        out_specs=(P("ctx", "head"),) * 4,
        check_vma=False,
    )
```

```python
import functools
import math

import jax
import jax.numpy as jnp
from jax import lax
from jax.experimental import pallas as pl
from jax.experimental.pallas import tpu as pltpu
from jax.sharding import PartitionSpec as P

HD = 128
GROUP = 8
SHARDS = 16
BLOCK = 16
ROWS = SHARDS * BLOCK
SEQ = SHARDS * ROWS
DOCS = 8
HEADS = 8
COLS = GROUP * HD

SPAN = 4
WIDTH = GROUP * BLOCK
LANES = SPAN * WIDTH
NEGATIVE = -1e30
FLOOR = -0.5e30
SCALE = 1.0 / math.sqrt(HD)
LOG2E = 1.4426950408889634

BF = jnp.bfloat16
F32 = jnp.float32
MESH = pl.DeviceIdType.MESH
ANY = pl.BlockSpec(memory_space=pl.ANY)
VMEM = pl.BlockSpec(memory_space=pltpu.VMEM)
SMEM = pl.BlockSpec(memory_space=pltpu.SMEM)


def ctx_of(x, y, core):
    return (lax.rem(x, 4) * 2 + lax.rem(y, 2)) * 2 + lax.rem(core, 2)


def head_of(z, y):
    return lax.rem(z, 4) * 2 + lax.rem(y, 2)


def remote(src, dst, send, recv, ctx, head):
    return pltpu.make_async_remote_copy(
        src_ref=src,
        dst_ref=dst,
        send_sem=send,
        recv_sem=recv,
        device_id=(ctx, head),
        device_id_type=MESH,
    )


def exchange_kernel(
    route, q, k, v, g, qo, go, ko, vo, xq, xg, sq, sg,
    p1s, p1r, p2s, p2r, rs, rr, cs, cr, local,
):
    c = lax.axis_index("ctx")
    h = lax.axis_index("head")
    z, yh = h // 2, lax.rem(h, 2)
    x, yl, core = c // 4, lax.rem(c // 2, 2), lax.rem(c, 2)
    head_peers = [(jz, jy) for jz in range(4) for jy in range(2) if (jz, jy) != (0, 0)]
    ctx_peers = [
        (jx, jy, jc) for jx in range(4) for jy in range(2) for jc in range(2)
        if (jx, jy, jc) != (0, 0, 0)
    ]

    barrier = pltpu.get_barrier_semaphore()
    for jz, jy in head_peers:
        pl.semaphore_signal(
            barrier, inc=1, device_id=(c, head_of(z + jz, yh + jy)), device_id_type=MESH
        )
    for jx, jy, jc in ctx_peers:
        pl.semaphore_signal(
            barrier, inc=1, device_id=(ctx_of(x + jx, yl + jy, core + jc), h), device_id_type=MESH
        )
    pl.semaphore_wait(barrier, len(head_peers) + len(ctx_peers))

    sent = []

    def go_remote(copy):
        copy.start()
        sent.append(copy)
        return copy

    kv_rows = pl.ds(c * ROWS + h * 32, 32)
    p1 = [[], [], [], []]
    for jz, jy in head_peers:
        j = jz * 2 + jy
        peer = head_of(z + jz, yh + jy)
        cols = pl.ds(pl.multiple_of(peer * HD, HD), HD)
        for a, (src, dst) in enumerate(((k, ko), (v, vo))):
            p1[a].append(go_remote(remote(
                src.at[:, cols], dst.at[kv_rows], p1s.at[a, j], p1r.at[a, j], c, peer)))
    own_cols = pl.ds(pl.multiple_of(h * HD, HD), HD)
    own = [
        pltpu.make_async_copy(k.at[:, own_cols], ko.at[kv_rows], local.at[0]),
        pltpu.make_async_copy(v.at[:, own_cols], vo.at[kv_rows], local.at[1]),
    ]

    def first(a, src, dst):
        for jz, jy in head_peers:
            j = jz * 2 + jy
            peer = head_of(z + jz, yh + jy)
            cols = pl.ds(pl.multiple_of(peer * COLS, COLS), COLS)
            p1[2 + a].append(go_remote(remote(
                src.at[:, :, cols], dst.at[pl.ds(h * 2, 2)],
                p1s.at[2 + a, j], p1r.at[2 + a, j], c, peer)))
        cols = pl.ds(pl.multiple_of(h * COLS, COLS), COLS)
        own.append(pltpu.make_async_copy(
            src.at[:, :, cols], dst.at[pl.ds(h * 2, 2)], local.at[2 + a]))
        own[-1].start()

    for copy in own:
        copy.start()
    first(0, q, xq)

    kv = (ko, vo)

    def shard(a, dx, dy):
        return kv[a].at[pl.ds(ctx_of(x + dx, yl + dy, core) * ROWS, ROWS)]

    def ring(a, dx, dy, tx, ty):
        slot = ((dx - tx) % 4) * 2 + (dy - ty) % 2
        part = shard(a, dx, dy)
        return remote(part, part, rs.at[a, slot], rr.at[a, slot],
                      ctx_of(x + tx + 4, yl + ty + 2, core), h)

    def partner(a, dx, dy):
        slot = dx * 2 + dy
        part = shard(a, dx, dy)
        return remote(part, part, cs.at[a, slot], cr.at[a, slot], ctx_of(x, yl, core + 1), h)

    def arrived(a, dx, dy):
        slot = dx * 2 + dy
        part = shard(a, dx, dy)
        remote(part, part, rs.at[a, slot], rr.at[a, slot], c, h).wait_recv()

    for a in range(2):
        own[a].wait()
        for copy in p1[a]:
            copy.wait_recv()
    for a in range(2):
        go_remote(ring(a, 0, 0, 0, 1))
        go_remote(ring(a, 0, 0, 1, 0))
        go_remote(ring(a, 0, 0, -1, 0))
    first(1, g, xg)
    for a in range(2):
        go_remote(partner(a, 0, 0))

    def second(a, stage, send, out):
        own[2 + a].wait()
        for copy in p1[2 + a]:
            copy.wait_recv()

        def pick(d, carry):
            block = jnp.int32(0)
            for b in range(SHARDS):
                block = jnp.where(route[c, b] == d, b, block)
            send[d] = stage[block]
            return carry

        lax.fori_loop(0, SHARDS, pick, 0)
        mine = pltpu.make_async_copy(send.at[c], out.at[c], local.at[4 + a])
        mine.start()
        copies = []
        for jx, jy, jc in ctx_peers:
            j = (jx * 2 + jy) * 2 + jc
            d = ctx_of(x + jx, yl + jy, core + jc)
            copies.append(go_remote(remote(
                send.at[d], out.at[c], p2s.at[a, j], p2r.at[a, j], d, h)))
        return mine, copies

    def sides(dy):
        arrived(0, 3, dy)
        go_remote(ring(0, 3, dy, 1, 0))
        arrived(1, 1, dy)
        go_remote(ring(1, 1, dy, -1, 0))
        arrived(0, 1, dy)
        arrived(1, 3, dy)
        for a in range(2):
            go_remote(partner(a, 3, dy))
            go_remote(partner(a, 1, dy))

    sides(0)
    for a in range(2):
        arrived(a, 0, 1)
        go_remote(ring(a, 0, 1, 1, 0))
        go_remote(ring(a, 0, 1, -1, 0))
        go_remote(partner(a, 0, 1))
    mine_q, p2q = second(0, xq, sq, qo)
    sides(1)
    for a in range(2):
        arrived(a, 2, 0)
        go_remote(partner(a, 2, 0))
    mine_g, p2g = second(1, xg, sg, go)
    for a in range(2):
        arrived(a, 2, 1)
        go_remote(partner(a, 2, 1))
    mine_q.wait()
    mine_g.wait()

    def received(a, out):
        for jx, jy, jc in ctx_peers:
            j = (jx * 2 + jy) * 2 + jc
            src = ctx_of(x - jx + 4, yl - jy + 2, core - jc + 2)
            remote(out.at[src], out.at[src], p2s.at[a, j], p2r.at[a, j], c, h).wait_recv()

    received(0, qo)
    received(1, go)
    for a in range(2):
        for dx in range(4):
            for dy in range(2):
                slot = dx * 2 + dy
                part = kv[a].at[pl.ds(ctx_of(x + dx, yl + dy, core + 1) * ROWS, ROWS)]
                remote(part, part, cs.at[a, slot], cr.at[a, slot], c, h).wait_recv()
    for copy in sent:
        copy.wait_send()


def exchange(route, q, k, v, g):
    return pl.pallas_call(
        exchange_kernel,
        name="exchange",
        out_shape=(
            jax.ShapeDtypeStruct((SHARDS, BLOCK, COLS), BF),
            jax.ShapeDtypeStruct((SHARDS, BLOCK, COLS), BF),
            jax.ShapeDtypeStruct((SEQ, HD), BF),
            jax.ShapeDtypeStruct((SEQ, HD), BF),
        ),
        in_specs=[SMEM, ANY, VMEM, VMEM, ANY],
        out_specs=(ANY, ANY, ANY, ANY),
        scratch_shapes=[
            pltpu.VMEM((SHARDS, BLOCK, COLS), BF),
            pltpu.VMEM((SHARDS, BLOCK, COLS), BF),
            pltpu.VMEM((SHARDS, BLOCK, COLS), BF),
            pltpu.VMEM((SHARDS, BLOCK, COLS), BF),
            pltpu.SemaphoreType.DMA((4, 8)),
            pltpu.SemaphoreType.DMA((4, 8)),
            pltpu.SemaphoreType.DMA((2, 16)),
            pltpu.SemaphoreType.DMA((2, 16)),
            pltpu.SemaphoreType.DMA((2, 24)),
            pltpu.SemaphoreType.DMA((2, 8)),
            pltpu.SemaphoreType.DMA((2, 8)),
            pltpu.SemaphoreType.DMA((2, 8)),
            pltpu.SemaphoreType.DMA((6,)),
        ],
        compiler_params=pltpu.CompilerParams(collective_id=0, has_side_effects=True),
    )(route, q, k, v, g)


def attention_kernel(
    route, docs, q_hbm, g_hbm, k_hbm, v_hbm, att_hbm, dq_hbm, dkv_hbm,
    q, g, k, v, att, dq, dkv,
    s_buf, dp_buf, kt, vt, dk_acc, dv_acc, ot_acc, dqt_acc, starts, load, store,
):
    pairs = ((k_hbm, k), (q_hbm, q), (v_hbm, v), (g_hbm, g))

    def incoming(n):
        rows = pl.ds(n * SPAN, SPAN)
        return [
            pltpu.make_async_copy(src.at[rows], dst.at[rows], load.at[n, i])
            for i, (src, dst) in enumerate(pairs)
        ]

    for n in range(SHARDS // SPAN):
        for copy in incoming(n):
            copy.start()
    c = lax.axis_index("ctx")
    ends = []
    total = jnp.int32(0)
    for j in range(DOCS):
        total = total + docs[j]
        ends.append(total)

    def find(s, carry):
        block = jnp.int32(0)
        for b in range(SHARDS):
            block = jnp.where(route[s, b] == c, b, block)
        starts[s] = s * ROWS + block * BLOCK
        return carry

    lax.fori_loop(0, SHARDS, find, 0)
    def stack(ref, first):
        parts = []
        for i in range(SPAN):
            rows = ref[first + i]
            parts += [rows[:, n * HD:(n + 1) * HD] for n in range(GROUP)]
        return jnp.concatenate(parts, axis=0)

    def outgoing(n):
        rows = pl.ds(n * SPAN, SPAN)
        return (
            pltpu.make_async_copy(att.at[rows], att_hbm.at[rows], store.at[0]),
            pltpu.make_async_copy(dq.at[rows], dq_hbm.at[rows], store.at[1]),
        )

    within = lax.rem(lax.broadcasted_iota(jnp.int32, (1, WIDTH), 1), BLOCK)
    key = lax.broadcasted_iota(jnp.int32, (ROWS, WIDTH), 0)

    def group(n, carry):
        first = n * SPAN
        for copy in incoming(n):
            copy.wait()
        for e in range(SPAN):
            kt[first + e] = k[first + e].T
            vt[first + e] = v[first + e].T
        qg = stack(q, first)
        gg = stack(g, first)
        qt = qg.T
        gt = gg.T
        q_pos = jnp.concatenate([within + starts[first + i] for i in range(SPAN)], axis=1)
        q_doc = jnp.zeros_like(q_pos)
        marks = [starts[first], starts[first + 1], starts[first + 2],
                 starts[first + SPAN - 1] + BLOCK - 1]
        lows = [jnp.int32(0)] * 4
        for end in ends:
            q_doc = jnp.where(q_pos >= end, end, q_doc)
            lows = [jnp.where(mark >= end, end, low) for mark, low in zip(marks, lows)]
        t_one, t_two, t_low = [jnp.minimum(low // ROWS, first) for low in lows[:3]]
        t_full = jnp.minimum((lows[3] + ROWS - 1) // ROWS, first)
        reach = (q_pos - q_doc).astype(jnp.uint32)

        def scores(t, lane, stop=LANES):
            s = jnp.dot(k[t], qt[:, lane:stop], preferred_element_type=F32)
            return s * (SCALE * LOG2E)

        def slopes(t, lane, stop=LANES):
            return jnp.dot(v[t], gt[:, lane:stop], preferred_element_type=F32)

        def masked(t, lane, stop=LANES):
            s = scores(t, lane, stop)
            offset = t * ROWS - q_doc[:, lane:stop]
            parts = []
            for i in range(0, stop - lane, WIDTH):
                past = (key + offset[:, i:i + WIDTH]).astype(jnp.uint32)
                seen = past <= reach[:, lane + i:lane + i + WIDTH]
                parts.append(jnp.where(seen, s[:, i:i + WIDTH], NEGATIVE))
            return jnp.concatenate(parts, axis=1)

        ot_acc[...] = jnp.zeros_like(ot_acc)
        dqt_acc[...] = jnp.zeros_like(dqt_acc)

        def forward(produce, stop=LANES):
            def step(t, carried):
                peak, mass = carried
                s = produce(t, 0, stop)
                s_buf[t, :, :stop] = s
                if stop < LANES:
                    dp_buf[t, :, :stop] = slopes(t, 0, stop)
                new_peak = jnp.maximum(peak[:, :stop], jnp.max(s, axis=0, keepdims=True))
                p = jnp.exp2(s - new_peak)
                fade = jnp.exp2(peak[:, :stop] - new_peak)
                new_mass = mass[:, :stop] * fade + jnp.sum(p, axis=0, keepdims=True)
                ot_acc[:, :stop] = ot_acc[:, :stop] * fade + jnp.dot(
                    vt[t], p.astype(BF), preferred_element_type=F32)
                if stop < LANES:
                    new_peak = jnp.concatenate([new_peak, peak[:, stop:]], axis=1)
                    new_mass = jnp.concatenate([new_mass, mass[:, stop:]], axis=1)
                return new_peak, new_mass

            return step

        state = (jnp.full((1, LANES), FLOOR, F32), jnp.zeros((1, LANES), F32))
        state = lax.fori_loop(t_one, t_two, forward(masked, WIDTH), state)
        state = lax.fori_loop(t_two, t_low, forward(masked, 2 * WIDTH), state)
        state = lax.fori_loop(t_low, t_full, forward(masked), state)
        peak, mass = lax.fori_loop(t_full, first, forward(scores), state)

        tops = [[peak[:, i * WIDTH:(i + 1) * WIDTH]] for i in range(SPAN)]
        for e in range(SPAN):
            s = masked(first + e, e * WIDTH)
            s_buf[first + e, :, e * WIDTH:] = s
            dp_buf[first + e, :, e * WIDTH:] = slopes(first + e, e * WIDTH)
            top = jnp.max(s, axis=0, keepdims=True)
            for i in range(e, SPAN):
                tops[i].append(top[:, (i - e) * WIDTH:(i - e + 1) * WIDTH])
        new_peak = jnp.concatenate([functools.reduce(jnp.maximum, t) for t in tops], axis=1)
        fade = jnp.exp2(peak - new_peak)
        mass = mass * fade
        masses = [[mass[:, i * WIDTH:(i + 1) * WIDTH]] for i in range(SPAN)]
        ot_acc[...] = ot_acc[...] * fade
        for e in range(SPAN):
            p = jnp.exp2(s_buf[first + e, :, e * WIDTH:] - new_peak[:, e * WIDTH:])
            add = jnp.sum(p, axis=0, keepdims=True)
            for i in range(e, SPAN):
                masses[i].append(add[:, (i - e) * WIDTH:(i - e + 1) * WIDTH])
            ot_acc[:, e * WIDTH:] += jnp.dot(
                vt[first + e], p.astype(BF), preferred_element_type=F32)
        mass = jnp.concatenate([functools.reduce(jnp.add, t) for t in masses], axis=1)
        lse = new_peak + jnp.log2(mass)
        ot = (ot_acc[...] * (1.0 / mass)).astype(BF)
        delta = jnp.sum(gt.astype(F32) * ot.astype(F32), axis=0, keepdims=True)
        o = ot.T
        for i in range(SPAN):
            for m in range(GROUP):
                r = (i * GROUP + m) * BLOCK
                att[first + i, :, m * HD:(m + 1) * HD] = o[r:r + BLOCK]

        def pull(t, lane, stop=LANES, held=True):
            p = jnp.exp2(s_buf[t, :, lane:stop] - lse[:, lane:stop])
            dp = dp_buf[t, :, lane:stop] if held else slopes(t, lane, stop)
            ds = (p * (dp - delta[:, lane:stop])).astype(BF)
            grad_v = jnp.dot(p.astype(BF), gg[lane:stop], preferred_element_type=F32)
            grad_k = jnp.dot(ds, qg[lane:stop], preferred_element_type=F32)
            dqt_acc[:, lane:stop] += jnp.dot(kt[t], ds, preferred_element_type=F32)
            return grad_v, grad_k

        for e in range(SPAN):
            grad_v, grad_k = pull(first + e, e * WIDTH)
            dv_acc[first + e] = grad_v
            dk_acc[first + e] = grad_k

        def backward(stop):
            def step(t, carried):
                grad_v, grad_k = pull(t, 0, stop, stop < LANES)
                dv_acc[t] += grad_v
                dk_acc[t] += grad_k
                return carried

            return step

        lax.fori_loop(t_one, t_two, backward(WIDTH), 0)
        lax.fori_loop(t_two, t_low, backward(2 * WIDTH), 0)
        lax.fori_loop(t_low, first, backward(LANES), 0)
        grad = dqt_acc[...].T * SCALE
        for i in range(SPAN):
            for m in range(GROUP):
                r = (i * GROUP + m) * BLOCK
                dq[first + i, :, m * HD:(m + 1) * HD] = grad[r:r + BLOCK]
        for copy in outgoing(n):
            copy.start()
        return carry

    lax.fori_loop(0, SHARDS // SPAN, group, 0)

    def regroup(s, carry):
        for b in range(SHARDS):
            d = route[s, b]
            rows = slice(b * BLOCK, (b + 1) * BLOCK)
            dkv[d, 0, s] = (dk_acc[s, rows] * SCALE).astype(BF)
            dkv[d, 1, s] = dv_acc[s, rows].astype(BF)
        return carry

    lax.fori_loop(0, SHARDS, regroup, 0)
    last = pltpu.make_async_copy(dkv, dkv_hbm, load.at[0, 0])
    last.start()
    pltpu.make_async_copy(att, att_hbm, store.at[0]).wait()
    pltpu.make_async_copy(dq, dq_hbm, store.at[1]).wait()
    last.wait()


def attention(route, docs, q, g, k, v):
    return pl.pallas_call(
        attention_kernel,
        name="attention",
        out_shape=(
            jax.ShapeDtypeStruct((SHARDS, BLOCK, COLS), BF),
            jax.ShapeDtypeStruct((SHARDS, BLOCK, COLS), F32),
            jax.ShapeDtypeStruct((SHARDS, 2, SHARDS, BLOCK, HD), BF),
        ),
        in_specs=[SMEM, SMEM, ANY, ANY, ANY, ANY],
        out_specs=(ANY, ANY, ANY),
        scratch_shapes=[
            pltpu.VMEM((SHARDS, BLOCK, COLS), BF),
            pltpu.VMEM((SHARDS, BLOCK, COLS), BF),
            pltpu.VMEM((SHARDS, ROWS, HD), BF),
            pltpu.VMEM((SHARDS, ROWS, HD), BF),
            pltpu.VMEM((SHARDS, BLOCK, COLS), BF),
            pltpu.VMEM((SHARDS, BLOCK, COLS), F32),
            pltpu.VMEM((SHARDS, 2, SHARDS, BLOCK, HD), BF),
            pltpu.VMEM((SHARDS, ROWS, LANES), F32),
            pltpu.VMEM((SHARDS, ROWS, LANES), F32),
            pltpu.VMEM((SHARDS, HD, ROWS), BF),
            pltpu.VMEM((SHARDS, HD, ROWS), BF),
            pltpu.VMEM((SHARDS, ROWS, HD), F32),
            pltpu.VMEM((SHARDS, ROWS, HD), F32),
            pltpu.VMEM((HD, LANES), F32),
            pltpu.VMEM((HD, LANES), F32),
            pltpu.SMEM((SHARDS,), jnp.int32),
            pltpu.SemaphoreType.DMA((SHARDS // SPAN, 4)),
            pltpu.SemaphoreType.DMA((2,)),
        ],
    )(route, docs, q, g, k, v)


def reduce_kernel(
    part, chip, keep, mine, mate, hold, kept, from_y, from_x,
    s1, r1, sy, ry, sx, rx, s2, r2, local,
):
    c = lax.axis_index("ctx")
    h = lax.axis_index("head")
    x, yl, core = c // 4, lax.rem(c // 2, 2), lax.rem(c, 2)
    other = ctx_of(x, yl, core + 1)
    across = ctx_of(x, yl + 1, core)
    far = (2, 1, 3, 0)
    order = [(dx, dy) for dx in far for dy in (1, 0)]

    def along(dx):
        return ctx_of(x + dx, yl, core)

    def place(dx, dy):
        return lax.rem(x + dx, 4) * 2 + lax.rem(yl + dy, 2)

    loads = []
    for i, (dx, dy) in enumerate(order):
        t = place(dx, dy)
        copy = pltpu.make_async_copy(part.at[t * 2 + core], mine.at[t], local.at[i])
        copy.start()
        loads.append(copy)

    barrier = pltpu.get_barrier_semaphore()
    for peer in (other, across, along(1), along(2), along(3)):
        pl.semaphore_signal(barrier, inc=1, device_id=(peer, h), device_id_type=MESH)
    pl.semaphore_wait(barrier, 5)

    sent = []

    def start(*args):
        copy = remote(*args, h)
        copy.start()
        sent.append(copy)
        return copy

    pairs = []
    for i, (dx, dy) in enumerate(order):
        t = place(dx, dy)
        pairs.append(start(part.at[t * 2 + 1 - core], mate.at[t], s1.at[i], r1.at[i], other))

    for (dx, dy), pair, load in zip(order, pairs, loads):
        t = place(dx, dy)
        load.wait()
        pair.wait_recv()
        if dy == 1:
            mate[t, 0] = (mine[t, 0].astype(F32) + mate[t, 0].astype(F32)).astype(BF)
            start(mate.at[t, 0], from_y.at[dx], sy.at[dx], ry.at[dx], across)
        else:
            hold[dx] = mine[t, 0].astype(F32) + mate[t, 0].astype(F32)
        if dx == 0:
            kept[1 - dy] = mine[t, 1].astype(F32) + mate[t, 1].astype(F32)
        else:
            mate[t, 1] = (mine[t, 1].astype(F32) + mate[t, 1].astype(F32)).astype(BF)
            start(mate.at[t, 1], from_x.at[dx - 1, dy], sx.at[dx - 1, dy], rx.at[dx - 1, dy],
                  along(dx))

    for dx in far:
        remote(from_y.at[dx], from_y.at[dx], sy.at[dx], ry.at[dx], across, h).wait_recv()
        hold[dx] += from_y[dx].astype(F32)
        if dx:
            t = place(dx, 0)
            mate[t, 0] = hold[dx].astype(BF)
            start(mate.at[t, 0], chip.at[dx - 1], s2.at[dx], r2.at[dx], along(dx))
    for dy in (1, 0):
        for dx in (1, 3, 2):
            part_in = from_x.at[dx - 1, dy]
            remote(part_in, part_in, sx.at[dx - 1, dy], rx.at[dx - 1, dy], across, h).wait_recv()
            kept[1 - dy] += from_x[dx - 1, dy].astype(F32)
        if dy:
            t = place(0, 1)
            mate[t, 1] = kept[0].astype(BF)
            start(mate.at[t, 1], chip.at[3], s2.at[0], r2.at[0], across)
    outs = [
        pltpu.make_async_copy(hold.at[0], keep.at[0], local.at[0]),
        pltpu.make_async_copy(kept.at[1], keep.at[1], local.at[1]),
    ]
    for out in outs:
        out.start()
    for j in range(4):
        slot = chip.at[(j + 3) % 4]
        remote(slot, slot, s2.at[j], r2.at[j], across, h).wait_recv()
    for copy in sent:
        copy.wait_send()
    for out in outs:
        out.wait()


def reduce(part):
    shape = (SHARDS, BLOCK, HD)
    return pl.pallas_call(
        reduce_kernel,
        name="reduce",
        out_shape=(
            jax.ShapeDtypeStruct((4,) + shape, BF),
            jax.ShapeDtypeStruct((2,) + shape, F32),
        ),
        in_specs=[ANY],
        out_specs=(ANY, ANY),
        scratch_shapes=[
            pltpu.VMEM((8, 2) + shape, BF),
            pltpu.VMEM((8, 2) + shape, BF),
            pltpu.VMEM((4,) + shape, F32),
            pltpu.VMEM((2,) + shape, F32),
            pltpu.VMEM((4,) + shape, BF),
            pltpu.VMEM((3, 2) + shape, BF),
            pltpu.SemaphoreType.DMA((8,)),
            pltpu.SemaphoreType.DMA((8,)),
            pltpu.SemaphoreType.DMA((4,)),
            pltpu.SemaphoreType.DMA((4,)),
            pltpu.SemaphoreType.DMA((3, 2)),
            pltpu.SemaphoreType.DMA((3, 2)),
            pltpu.SemaphoreType.DMA((4,)),
            pltpu.SemaphoreType.DMA((4,)),
            pltpu.SemaphoreType.DMA((8,)),
        ],
        compiler_params=pltpu.CompilerParams(collective_id=1, has_side_effects=True),
    )(part)


def finish_kernel(chip, keep, dk, dv):
    def add(s, carry):
        dk[s] = keep[0, s] + chip[0, s].astype(F32) + chip[1, s].astype(F32) + chip[2, s].astype(F32)
        dv[s] = keep[1, s] + chip[3, s].astype(F32)
        return carry

    lax.fori_loop(0, SHARDS, add, 0)


def finish(chip, keep):
    out = jax.ShapeDtypeStruct((SHARDS, BLOCK, HD), F32)
    return pl.pallas_call(
        finish_kernel,
        name="finish",
        out_shape=(out, out),
        in_specs=[VMEM, VMEM],
        out_specs=(VMEM, VMEM),
    )(chip, keep)


def on_device(queries, key_rows, value_rows, cotangent, doc_lengths, block_route):
    q, g, k, v = exchange(
        block_route,
        queries.reshape(2, BLOCK, HEADS * COLS),
        key_rows,
        value_rows,
        cotangent.reshape(2, BLOCK, HEADS * COLS),
    )
    att, dq, part = attention(
        block_route, doc_lengths, q, g, k.reshape(SHARDS, ROWS, HD), v.reshape(SHARDS, ROWS, HD))
    dk, dv = finish(*reduce(part))
    return (
        att.reshape(ROWS, COLS),
        dq.reshape(ROWS, COLS),
        dk.reshape(ROWS, HD),
        dv.reshape(ROWS, HD),
    )


def solution(mesh):
    placed = P(("ctx", "head"), None)
    return jax.shard_map(
        on_device,
        mesh=mesh,
        in_specs=(placed, placed, placed, placed, P(), P()),
        out_specs=(P("ctx", "head"),) * 4,
        check_vma=False,
    )
```

```python
import functools
import math

import jax
import jax.numpy as jnp
from jax import lax
from jax.experimental import pallas as pl
from jax.experimental.pallas import tpu as pltpu
from jax.sharding import PartitionSpec as P

HD = 128
GROUP = 8
SHARDS = 16
BLOCK = 16
ROWS = SHARDS * BLOCK
SEQ = SHARDS * ROWS
DOCS = 8
HEADS = 8
COLS = GROUP * HD

SPAN = 4
WIDTH = GROUP * BLOCK
LANES = SPAN * WIDTH
NEGATIVE = -1e30
FLOOR = -0.5e30
SCALE = 1.0 / math.sqrt(HD)
LOG2E = 1.4426950408889634

BF = jnp.bfloat16
F32 = jnp.float32
MESH = pl.DeviceIdType.MESH
ANY = pl.BlockSpec(memory_space=pl.ANY)
VMEM = pl.BlockSpec(memory_space=pltpu.VMEM)
SMEM = pl.BlockSpec(memory_space=pltpu.SMEM)


def ctx_of(x, y, core):
    return (lax.rem(x, 4) * 2 + lax.rem(y, 2)) * 2 + lax.rem(core, 2)


def head_of(z, y):
    return lax.rem(z, 4) * 2 + lax.rem(y, 2)


def remote(src, dst, send, recv, ctx, head):
    return pltpu.make_async_remote_copy(
        src_ref=src,
        dst_ref=dst,
        send_sem=send,
        recv_sem=recv,
        device_id=(ctx, head),
        device_id_type=MESH,
    )


def exchange_kernel(
    route_hbm, q, k, v, g, qo, go, ko, vo, xq, xg, sq, sg, own_kv, route,
    p1s, p1r, p2s, p2r, rs, rr, cs, cr, local,
):
    c = lax.axis_index("ctx")
    h = lax.axis_index("head")
    z, yh = h // 2, lax.rem(h, 2)
    x, yl, core = c // 4, lax.rem(c // 2, 2), lax.rem(c, 2)
    head_peers = [(jz, jy) for jz in range(4) for jy in range(2) if (jz, jy) != (0, 0)]
    ctx_peers = [
        (jx, jy, jc) for jx in range(4) for jy in range(2) for jc in range(2)
        if (jx, jy, jc) != (0, 0, 0)
    ]

    table = pltpu.make_async_copy(route_hbm, route, local.at[6])
    table.start()
    own_cols = pl.ds(pl.multiple_of(h * HD, HD), HD)
    staged = [
        pltpu.make_async_copy(src.at[:, own_cols], own_kv.at[a], local.at[a])
        for a, src in enumerate((k, v))
    ]
    for copy in staged:
        copy.start()

    barrier = pltpu.get_barrier_semaphore()
    for jz, jy in head_peers:
        pl.semaphore_signal(
            barrier, inc=1, device_id=(c, head_of(z + jz, yh + jy)), device_id_type=MESH
        )
    for jx, jy, jc in ctx_peers:
        pl.semaphore_signal(
            barrier, inc=1, device_id=(ctx_of(x + jx, yl + jy, core + jc), h), device_id_type=MESH
        )
    pl.semaphore_wait(barrier, len(head_peers) + len(ctx_peers))

    sent = []

    def go_remote(copy):
        copy.start()
        sent.append(copy)
        return copy

    kv_rows = pl.ds(c * ROWS + h * 32, 32)
    p1 = [[], [], [], []]
    for jz, jy in head_peers:
        j = jz * 2 + jy
        peer = head_of(z + jz, yh + jy)
        cols = pl.ds(pl.multiple_of(peer * HD, HD), HD)
        for a, (src, dst) in enumerate(((k, ko), (v, vo))):
            p1[a].append(go_remote(remote(
                src.at[:, cols], dst.at[kv_rows], p1s.at[a, j], p1r.at[a, j], c, peer)))
    own = [
        pltpu.make_async_copy(own_kv.at[a], dst.at[kv_rows], local.at[a])
        for a, dst in enumerate((ko, vo))
    ]

    def first(a, src, dst):
        for jz, jy in head_peers:
            j = jz * 2 + jy
            peer = head_of(z + jz, yh + jy)
            cols = pl.ds(pl.multiple_of(peer * COLS, COLS), COLS)
            p1[2 + a].append(go_remote(remote(
                src.at[:, :, cols], dst.at[pl.ds(h * 2, 2)],
                p1s.at[2 + a, j], p1r.at[2 + a, j], c, peer)))
        cols = pl.ds(pl.multiple_of(h * COLS, COLS), COLS)
        own.append(pltpu.make_async_copy(
            src.at[:, :, cols], dst.at[pl.ds(h * 2, 2)], local.at[2 + a]))
        own[-1].start()

    first(0, q, xq)
    for a in range(2):
        staged[a].wait()
        own[a].start()

    kv = (ko, vo)

    def shard(a, dx, dy):
        return kv[a].at[pl.ds(ctx_of(x + dx, yl + dy, core) * ROWS, ROWS)]

    def ring(a, dx, dy, tx, ty):
        slot = ((dx - tx) % 4) * 2 + (dy - ty) % 2
        part = shard(a, dx, dy)
        return remote(part, part, rs.at[a, slot], rr.at[a, slot],
                      ctx_of(x + tx + 4, yl + ty + 2, core), h)

    def partner(a, dx, dy):
        slot = dx * 2 + dy
        part = shard(a, dx, dy)
        return remote(part, part, cs.at[a, slot], cr.at[a, slot], ctx_of(x, yl, core + 1), h)

    def arrived(a, dx, dy):
        slot = dx * 2 + dy
        part = shard(a, dx, dy)
        remote(part, part, rs.at[a, slot], rr.at[a, slot], c, h).wait_recv()

    for a in range(2):
        own[a].wait()
        for copy in p1[a]:
            copy.wait_recv()
    for a in range(2):
        go_remote(ring(a, 0, 0, 0, 1))
        go_remote(ring(a, 0, 0, 1, 0))
        go_remote(ring(a, 0, 0, -1, 0))
    first(1, g, xg)
    for a in range(2):
        go_remote(partner(a, 0, 0))

    table.wait()

    def second(a, stage, send, out):
        own[2 + a].wait()
        for copy in p1[2 + a]:
            copy.wait_recv()

        def pick(d, carry):
            block = jnp.int32(0)
            for b in range(SHARDS):
                block = jnp.where(route[c, b] == d, b, block)
            send[d] = stage[block]
            return carry

        lax.fori_loop(0, SHARDS, pick, 0)
        mine = pltpu.make_async_copy(send.at[c], out.at[c], local.at[4 + a])
        mine.start()
        copies = []
        for jx, jy, jc in ctx_peers:
            j = (jx * 2 + jy) * 2 + jc
            d = ctx_of(x + jx, yl + jy, core + jc)
            copies.append(go_remote(remote(
                send.at[d], out.at[c], p2s.at[a, j], p2r.at[a, j], d, h)))
        return mine, copies

    def sides(dy):
        arrived(0, 3, dy)
        go_remote(ring(0, 3, dy, 1, 0))
        arrived(1, 1, dy)
        go_remote(ring(1, 1, dy, -1, 0))
        arrived(0, 1, dy)
        arrived(1, 3, dy)
        for a in range(2):
            go_remote(partner(a, 3, dy))
            go_remote(partner(a, 1, dy))

    sides(0)
    for a in range(2):
        arrived(a, 0, 1)
        go_remote(ring(a, 0, 1, 1, 0))
        go_remote(ring(a, 0, 1, -1, 0))
        go_remote(partner(a, 0, 1))
    mine_q, p2q = second(0, xq, sq, qo)
    sides(1)
    for a in range(2):
        arrived(a, 2, 0)
        go_remote(partner(a, 2, 0))
    mine_g, p2g = second(1, xg, sg, go)
    for a in range(2):
        arrived(a, 2, 1)
        go_remote(partner(a, 2, 1))
    mine_q.wait()
    mine_g.wait()

    def received(a, out):
        for jx, jy, jc in ctx_peers:
            j = (jx * 2 + jy) * 2 + jc
            src = ctx_of(x - jx + 4, yl - jy + 2, core - jc + 2)
            remote(out.at[src], out.at[src], p2s.at[a, j], p2r.at[a, j], c, h).wait_recv()

    received(0, qo)
    received(1, go)
    for a in range(2):
        for dx in range(4):
            for dy in range(2):
                slot = dx * 2 + dy
                part = kv[a].at[pl.ds(ctx_of(x + dx, yl + dy, core + 1) * ROWS, ROWS)]
                remote(part, part, cs.at[a, slot], cr.at[a, slot], c, h).wait_recv()
    for copy in sent:
        copy.wait_send()


def exchange(route, q, k, v, g):
    return pl.pallas_call(
        exchange_kernel,
        name="exchange",
        out_shape=(
            jax.ShapeDtypeStruct((SHARDS, BLOCK, COLS), BF),
            jax.ShapeDtypeStruct((SHARDS, BLOCK, COLS), BF),
            jax.ShapeDtypeStruct((SEQ, HD), BF),
            jax.ShapeDtypeStruct((SEQ, HD), BF),
        ),
        in_specs=[ANY, ANY, ANY, ANY, ANY],
        out_specs=(ANY, ANY, ANY, ANY),
        scratch_shapes=[
            pltpu.VMEM((SHARDS, BLOCK, COLS), BF),
            pltpu.VMEM((SHARDS, BLOCK, COLS), BF),
            pltpu.VMEM((SHARDS, BLOCK, COLS), BF),
            pltpu.VMEM((SHARDS, BLOCK, COLS), BF),
            pltpu.VMEM((2, 32, HD), BF),
            pltpu.SMEM((SHARDS, SHARDS), jnp.int32),
            pltpu.SemaphoreType.DMA((4, 8)),
            pltpu.SemaphoreType.DMA((4, 8)),
            pltpu.SemaphoreType.DMA((2, 16)),
            pltpu.SemaphoreType.DMA((2, 16)),
            pltpu.SemaphoreType.DMA((2, 24)),
            pltpu.SemaphoreType.DMA((2, 8)),
            pltpu.SemaphoreType.DMA((2, 8)),
            pltpu.SemaphoreType.DMA((2, 8)),
            pltpu.SemaphoreType.DMA((7,)),
        ],
        compiler_params=pltpu.CompilerParams(collective_id=0, has_side_effects=True),
    )(route, q, k, v, g)


def attention_kernel(
    route_hbm, docs_hbm, q_hbm, g_hbm, k_hbm, v_hbm, att_hbm, dq_hbm, dkv_hbm,
    q, g, k, v, att, dq, dkv,
    s_buf, dp_buf, kt, vt, dk_acc, dv_acc, ot_acc, dqt_acc, route, docs, starts, load, store,
):
    tables = (
        pltpu.make_async_copy(route_hbm, route, store.at[0]),
        pltpu.make_async_copy(docs_hbm, docs, store.at[1]),
    )
    for copy in tables:
        copy.start()
    pairs = ((k_hbm, k), (q_hbm, q), (v_hbm, v), (g_hbm, g))

    def incoming(n):
        rows = pl.ds(n * SPAN, SPAN)
        return [
            pltpu.make_async_copy(src.at[rows], dst.at[rows], load.at[n, i])
            for i, (src, dst) in enumerate(pairs)
        ]

    for n in range(SHARDS // SPAN):
        for copy in incoming(n):
            copy.start()
    for copy in tables:
        copy.wait()
    c = lax.axis_index("ctx")
    ends = []
    total = jnp.int32(0)
    for j in range(DOCS):
        total = total + docs[j]
        ends.append(total)

    def find(s, carry):
        block = jnp.int32(0)
        for b in range(SHARDS):
            block = jnp.where(route[s, b] == c, b, block)
        starts[s] = s * ROWS + block * BLOCK
        return carry

    lax.fori_loop(0, SHARDS, find, 0)
    def stack(ref, first):
        parts = []
        for i in range(SPAN):
            rows = ref[first + i]
            parts += [rows[:, n * HD:(n + 1) * HD] for n in range(GROUP)]
        return jnp.concatenate(parts, axis=0)

    def outgoing(n):
        rows = pl.ds(n * SPAN, SPAN)
        return (
            pltpu.make_async_copy(att.at[rows], att_hbm.at[rows], store.at[0]),
            pltpu.make_async_copy(dq.at[rows], dq_hbm.at[rows], store.at[1]),
        )

    within = lax.rem(lax.broadcasted_iota(jnp.int32, (1, WIDTH), 1), BLOCK)
    key = lax.broadcasted_iota(jnp.int32, (ROWS, WIDTH), 0)

    def group(n, carry):
        first = n * SPAN
        for copy in incoming(n):
            copy.wait()
        for e in range(SPAN):
            kt[first + e] = k[first + e].T
            vt[first + e] = v[first + e].T
        qg = stack(q, first)
        gg = stack(g, first)
        qt = qg.T
        gt = gg.T
        q_pos = jnp.concatenate([within + starts[first + i] for i in range(SPAN)], axis=1)
        q_doc = jnp.zeros_like(q_pos)
        marks = [starts[first], starts[first + 1], starts[first + 2],
                 starts[first + SPAN - 1] + BLOCK - 1]
        lows = [jnp.int32(0)] * 4
        for end in ends:
            q_doc = jnp.where(q_pos >= end, end, q_doc)
            lows = [jnp.where(mark >= end, end, low) for mark, low in zip(marks, lows)]
        t_one, t_two, t_low = [jnp.minimum(low // ROWS, first) for low in lows[:3]]
        t_full = jnp.minimum((lows[3] + ROWS - 1) // ROWS, first)
        reach = (q_pos - q_doc).astype(jnp.uint32)

        def scores(t, lane, stop=LANES):
            s = jnp.dot(k[t], qt[:, lane:stop], preferred_element_type=F32)
            return s * (SCALE * LOG2E)

        def slopes(t, lane, stop=LANES):
            return jnp.dot(v[t], gt[:, lane:stop], preferred_element_type=F32)

        def masked(t, lane, stop=LANES):
            s = scores(t, lane, stop)
            offset = t * ROWS - q_doc[:, lane:stop]
            parts = []
            for i in range(0, stop - lane, WIDTH):
                past = (key + offset[:, i:i + WIDTH]).astype(jnp.uint32)
                seen = past <= reach[:, lane + i:lane + i + WIDTH]
                parts.append(jnp.where(seen, s[:, i:i + WIDTH], NEGATIVE))
            return jnp.concatenate(parts, axis=1)

        ot_acc[...] = jnp.zeros_like(ot_acc)
        dqt_acc[...] = jnp.zeros_like(dqt_acc)

        def forward(produce, stop=LANES):
            def step(t, carried):
                peak, mass = carried
                s = produce(t, 0, stop)
                s_buf[t, :, :stop] = s
                if stop < LANES:
                    dp_buf[t, :, :stop] = slopes(t, 0, stop)
                new_peak = jnp.maximum(peak[:, :stop], jnp.max(s, axis=0, keepdims=True))
                p = jnp.exp2(s - new_peak)
                fade = jnp.exp2(peak[:, :stop] - new_peak)
                new_mass = mass[:, :stop] * fade + jnp.sum(p, axis=0, keepdims=True)
                ot_acc[:, :stop] = ot_acc[:, :stop] * fade + jnp.dot(
                    vt[t], p.astype(BF), preferred_element_type=F32)
                if stop < LANES:
                    new_peak = jnp.concatenate([new_peak, peak[:, stop:]], axis=1)
                    new_mass = jnp.concatenate([new_mass, mass[:, stop:]], axis=1)
                return new_peak, new_mass

            return step

        state = (jnp.full((1, LANES), FLOOR, F32), jnp.zeros((1, LANES), F32))
        state = lax.fori_loop(t_one, t_two, forward(masked, WIDTH), state)
        state = lax.fori_loop(t_two, t_low, forward(masked, 2 * WIDTH), state)
        state = lax.fori_loop(t_low, t_full, forward(masked), state)
        peak, mass = lax.fori_loop(t_full, first, forward(scores), state)

        tops = [[peak[:, i * WIDTH:(i + 1) * WIDTH]] for i in range(SPAN)]
        for e in range(SPAN):
            s = masked(first + e, e * WIDTH)
            s_buf[first + e, :, e * WIDTH:] = s
            dp_buf[first + e, :, e * WIDTH:] = slopes(first + e, e * WIDTH)
            top = jnp.max(s, axis=0, keepdims=True)
            for i in range(e, SPAN):
                tops[i].append(top[:, (i - e) * WIDTH:(i - e + 1) * WIDTH])
        new_peak = jnp.concatenate([functools.reduce(jnp.maximum, t) for t in tops], axis=1)
        fade = jnp.exp2(peak - new_peak)
        mass = mass * fade
        masses = [[mass[:, i * WIDTH:(i + 1) * WIDTH]] for i in range(SPAN)]
        ot_acc[...] = ot_acc[...] * fade
        for e in range(SPAN):
            p = jnp.exp2(s_buf[first + e, :, e * WIDTH:] - new_peak[:, e * WIDTH:])
            add = jnp.sum(p, axis=0, keepdims=True)
            for i in range(e, SPAN):
                masses[i].append(add[:, (i - e) * WIDTH:(i - e + 1) * WIDTH])
            ot_acc[:, e * WIDTH:] += jnp.dot(
                vt[first + e], p.astype(BF), preferred_element_type=F32)
        mass = jnp.concatenate([functools.reduce(jnp.add, t) for t in masses], axis=1)
        lse = new_peak + jnp.log2(mass)
        ot = (ot_acc[...] * (1.0 / mass)).astype(BF)
        delta = jnp.sum(gt.astype(F32) * ot.astype(F32), axis=0, keepdims=True)
        o = ot.T
        for i in range(SPAN):
            for m in range(GROUP):
                r = (i * GROUP + m) * BLOCK
                att[first + i, :, m * HD:(m + 1) * HD] = o[r:r + BLOCK]

        def pull(t, lane, stop=LANES, held=True):
            p = jnp.exp2(s_buf[t, :, lane:stop] - lse[:, lane:stop])
            dp = dp_buf[t, :, lane:stop] if held else slopes(t, lane, stop)
            ds = (p * (dp - delta[:, lane:stop])).astype(BF)
            grad_v = jnp.dot(p.astype(BF), gg[lane:stop], preferred_element_type=F32)
            grad_k = jnp.dot(ds, qg[lane:stop], preferred_element_type=F32)
            dqt_acc[:, lane:stop] += jnp.dot(kt[t], ds, preferred_element_type=F32)
            return grad_v, grad_k

        for e in range(SPAN):
            grad_v, grad_k = pull(first + e, e * WIDTH)
            dv_acc[first + e] = grad_v
            dk_acc[first + e] = grad_k

        def backward(stop):
            def step(t, carried):
                grad_v, grad_k = pull(t, 0, stop, stop < LANES)
                dv_acc[t] += grad_v
                dk_acc[t] += grad_k
                return carried

            return step

        lax.fori_loop(t_one, t_two, backward(WIDTH), 0)
        lax.fori_loop(t_two, t_low, backward(2 * WIDTH), 0)
        lax.fori_loop(t_low, first, backward(LANES), 0)
        grad = dqt_acc[...].T * SCALE
        for i in range(SPAN):
            for m in range(GROUP):
                r = (i * GROUP + m) * BLOCK
                dq[first + i, :, m * HD:(m + 1) * HD] = grad[r:r + BLOCK]
        for copy in outgoing(n):
            copy.start()
        return carry

    lax.fori_loop(0, SHARDS // SPAN, group, 0)

    def outbound(n):
        cols = pl.ds(n * SPAN, SPAN)
        return pltpu.make_async_copy(dkv.at[:, cols], dkv_hbm.at[:, cols], load.at[n, 0])

    def regroup(s, carry):
        for b in range(SHARDS):
            rows = slice(b * BLOCK, (b + 1) * BLOCK)
            dkv[route[s, b], s] = jnp.stack(
                [(dk_acc[s, rows] * SCALE).astype(BF), dv_acc[s, rows].astype(BF)])
        return carry

    for n in range(SHARDS // SPAN):
        lax.fori_loop(n * SPAN, (n + 1) * SPAN, regroup, 0)
        outbound(n).start()
    pltpu.make_async_copy(att, att_hbm, store.at[0]).wait()
    pltpu.make_async_copy(dq, dq_hbm, store.at[1]).wait()
    for n in range(SHARDS // SPAN):
        outbound(n).wait()


def attention(route, docs, q, g, k, v):
    return pl.pallas_call(
        attention_kernel,
        name="attention",
        out_shape=(
            jax.ShapeDtypeStruct((SHARDS, BLOCK, COLS), BF),
            jax.ShapeDtypeStruct((SHARDS, BLOCK, COLS), F32),
            jax.ShapeDtypeStruct((SHARDS, SHARDS, 2, BLOCK, HD), BF),
        ),
        in_specs=[ANY, ANY, ANY, ANY, ANY, ANY],
        out_specs=(ANY, ANY, ANY),
        scratch_shapes=[
            pltpu.VMEM((SHARDS, BLOCK, COLS), BF),
            pltpu.VMEM((SHARDS, BLOCK, COLS), BF),
            pltpu.VMEM((SHARDS, ROWS, HD), BF),
            pltpu.VMEM((SHARDS, ROWS, HD), BF),
            pltpu.VMEM((SHARDS, BLOCK, COLS), BF),
            pltpu.VMEM((SHARDS, BLOCK, COLS), F32),
            pltpu.VMEM((SHARDS, SHARDS, 2, BLOCK, HD), BF),
            pltpu.VMEM((SHARDS, ROWS, LANES), F32),
            pltpu.VMEM((SHARDS, ROWS, LANES), F32),
            pltpu.VMEM((SHARDS, HD, ROWS), BF),
            pltpu.VMEM((SHARDS, HD, ROWS), BF),
            pltpu.VMEM((SHARDS, ROWS, HD), F32),
            pltpu.VMEM((SHARDS, ROWS, HD), F32),
            pltpu.VMEM((HD, LANES), F32),
            pltpu.VMEM((HD, LANES), F32),
            pltpu.SMEM((SHARDS, SHARDS), jnp.int32),
            pltpu.SMEM((DOCS,), jnp.int32),
            pltpu.SMEM((SHARDS,), jnp.int32),
            pltpu.SemaphoreType.DMA((SHARDS // SPAN, 4)),
            pltpu.SemaphoreType.DMA((2,)),
        ],
    )(route, docs, q, g, k, v)


def reduce_kernel(
    part, chip, keep, mine, mate, ready, hold, kept, from_y, from_x,
    s1, r1, sy, ry, sx, rx, s2, r2, local,
):
    c = lax.axis_index("ctx")
    h = lax.axis_index("head")
    x, yl, core = c // 4, lax.rem(c // 2, 2), lax.rem(c, 2)
    other = ctx_of(x, yl, core + 1)
    across = ctx_of(x, yl + 1, core)
    far = (2, 1, 3, 0)
    order = [(dx, dy) for dx in far for dy in (1, 0)]

    def along(dx):
        return ctx_of(x + dx, yl, core)

    def place(dx, dy):
        return lax.rem(x + dx, 4) * 2 + lax.rem(yl + dy, 2)

    loads = []
    for i, (dx, dy) in enumerate(order):
        t = place(dx, dy)
        copy = pltpu.make_async_copy(part.at[t * 2 + core], mine.at[t], local.at[i])
        copy.start()
        loads.append(copy)

    barrier = pltpu.get_barrier_semaphore()
    for peer in (other, across, along(1), along(2), along(3)):
        pl.semaphore_signal(barrier, inc=1, device_id=(peer, h), device_id_type=MESH)
    pl.semaphore_wait(barrier, 5)

    sent = []

    def start(*args):
        copy = remote(*args, h)
        copy.start()
        sent.append(copy)
        return copy

    pairs = []
    for i, (dx, dy) in enumerate(order):
        t = place(dx, dy)
        pairs.append(start(part.at[t * 2 + 1 - core], mate.at[t], s1.at[i], r1.at[i], other))

    for (dx, dy), pair, load in zip(order, pairs, loads):
        t = place(dx, dy)
        load.wait()
        pair.wait_recv()
        sums = [mine[t, :, a].astype(F32) + mate[t, :, a].astype(F32) for a in range(2)]
        if dy == 1:
            ready[t, 0] = sums[0].astype(BF)
            start(ready.at[t, 0], from_y.at[dx], sy.at[dx], ry.at[dx], across)
        else:
            hold[dx] = sums[0]
        if dx == 0:
            kept[1 - dy] = sums[1]
        else:
            ready[t, 1] = sums[1].astype(BF)
            start(ready.at[t, 1], from_x.at[dx - 1, dy], sx.at[dx - 1, dy], rx.at[dx - 1, dy],
                  along(dx))

    for dx in far:
        remote(from_y.at[dx], from_y.at[dx], sy.at[dx], ry.at[dx], across, h).wait_recv()
        hold[dx] += from_y[dx].astype(F32)
        if dx:
            t = place(dx, 0)
            ready[t, 0] = hold[dx].astype(BF)
            start(ready.at[t, 0], chip.at[dx - 1], s2.at[dx], r2.at[dx], along(dx))
    for dy in (1, 0):
        for dx in (1, 3, 2):
            part_in = from_x.at[dx - 1, dy]
            remote(part_in, part_in, sx.at[dx - 1, dy], rx.at[dx - 1, dy], across, h).wait_recv()
            kept[1 - dy] += from_x[dx - 1, dy].astype(F32)
        if dy:
            t = place(0, 1)
            ready[t, 1] = kept[0].astype(BF)
            start(ready.at[t, 1], chip.at[3], s2.at[0], r2.at[0], across)
    outs = [
        pltpu.make_async_copy(hold.at[0], keep.at[0], local.at[0]),
        pltpu.make_async_copy(kept.at[1], keep.at[1], local.at[1]),
    ]
    for out in outs:
        out.start()
    for j in range(4):
        slot = chip.at[(j + 3) % 4]
        remote(slot, slot, s2.at[j], r2.at[j], across, h).wait_recv()
    for copy in sent:
        copy.wait_send()
    for out in outs:
        out.wait()


def reduce(part):
    shape = (SHARDS, BLOCK, HD)
    return pl.pallas_call(
        reduce_kernel,
        name="reduce",
        out_shape=(
            jax.ShapeDtypeStruct((4,) + shape, BF),
            jax.ShapeDtypeStruct((2,) + shape, F32),
        ),
        in_specs=[ANY],
        out_specs=(ANY, ANY),
        scratch_shapes=[
            pltpu.VMEM((8, SHARDS, 2, BLOCK, HD), BF),
            pltpu.VMEM((8, SHARDS, 2, BLOCK, HD), BF),
            pltpu.VMEM((8, 2) + shape, BF),
            pltpu.VMEM((4,) + shape, F32),
            pltpu.VMEM((2,) + shape, F32),
            pltpu.VMEM((4,) + shape, BF),
            pltpu.VMEM((3, 2) + shape, BF),
            pltpu.SemaphoreType.DMA((8,)),
            pltpu.SemaphoreType.DMA((8,)),
            pltpu.SemaphoreType.DMA((4,)),
            pltpu.SemaphoreType.DMA((4,)),
            pltpu.SemaphoreType.DMA((3, 2)),
            pltpu.SemaphoreType.DMA((3, 2)),
            pltpu.SemaphoreType.DMA((4,)),
            pltpu.SemaphoreType.DMA((4,)),
            pltpu.SemaphoreType.DMA((8,)),
        ],
        compiler_params=pltpu.CompilerParams(collective_id=1, has_side_effects=True),
    )(part)


def finish_kernel(chip, keep, dk, dv):
    def add(s, carry):
        dk[s] = keep[0, s] + chip[0, s].astype(F32) + chip[1, s].astype(F32) + chip[2, s].astype(F32)
        dv[s] = keep[1, s] + chip[3, s].astype(F32)
        return carry

    lax.fori_loop(0, SHARDS, add, 0)


def finish(chip, keep):
    out = jax.ShapeDtypeStruct((SHARDS, BLOCK, HD), F32)
    return pl.pallas_call(
        finish_kernel,
        name="finish",
        out_shape=(out, out),
        in_specs=[VMEM, VMEM],
        out_specs=(VMEM, VMEM),
    )(chip, keep)


def on_device(queries, key_rows, value_rows, cotangent, doc_lengths, block_route):
    q, g, k, v = exchange(
        block_route,
        queries.reshape(2, BLOCK, HEADS * COLS),
        key_rows,
        value_rows,
        cotangent.reshape(2, BLOCK, HEADS * COLS),
    )
    att, dq, part = attention(
        block_route, doc_lengths, q, g, k.reshape(SHARDS, ROWS, HD), v.reshape(SHARDS, ROWS, HD))
    dk, dv = finish(*reduce(part))
    return (
        att.reshape(ROWS, COLS),
        dq.reshape(ROWS, COLS),
        dk.reshape(ROWS, HD),
        dv.reshape(ROWS, HD),
    )


def solution(mesh):
    placed = P(("ctx", "head"), None)
    return jax.shard_map(
        on_device,
        mesh=mesh,
        in_specs=(placed, placed, placed, placed, P(), P()),
        out_specs=(P("ctx", "head"),) * 4,
        check_vma=False,
    )
```

```python
import functools
import math

import jax
import jax.numpy as jnp
from jax import lax
from jax.experimental import pallas as pl
from jax.experimental.pallas import tpu as pltpu
from jax.sharding import PartitionSpec as P

HD = 128
GROUP = 8
SHARDS = 16
BLOCK = 16
ROWS = SHARDS * BLOCK
SEQ = SHARDS * ROWS
DOCS = 8
HEADS = 8
COLS = GROUP * HD

SPAN = 4
WIDTH = GROUP * BLOCK
LANES = SPAN * WIDTH
NEGATIVE = -1e30
FLOOR = -0.5e30
SCALE = 1.0 / math.sqrt(HD)
LOG2E = 1.4426950408889634

BF = jnp.bfloat16
F32 = jnp.float32
MESH = pl.DeviceIdType.MESH
ANY = pl.BlockSpec(memory_space=pl.ANY)
VMEM = pl.BlockSpec(memory_space=pltpu.VMEM)
SMEM = pl.BlockSpec(memory_space=pltpu.SMEM)


def ctx_of(x, y, core):
    return (lax.rem(x, 4) * 2 + lax.rem(y, 2)) * 2 + lax.rem(core, 2)


def head_of(z, y):
    return lax.rem(z, 4) * 2 + lax.rem(y, 2)


def remote(src, dst, send, recv, ctx, head):
    return pltpu.make_async_remote_copy(
        src_ref=src,
        dst_ref=dst,
        send_sem=send,
        recv_sem=recv,
        device_id=(ctx, head),
        device_id_type=MESH,
    )


def exchange_kernel(
    route_hbm, q, k, v, g, qo, go, ko, vo, kto, vto,
    xq, xg, sq, sg, own_kv, all_kv, turned, route,
    p1s, p1r, p2s, p2r, rs, rr, cs, cr, local,
):
    c = lax.axis_index("ctx")
    h = lax.axis_index("head")
    z, yh = h // 2, lax.rem(h, 2)
    x, yl, core = c // 4, lax.rem(c // 2, 2), lax.rem(c, 2)
    head_peers = [(jz, jy) for jz in range(4) for jy in range(2) if (jz, jy) != (0, 0)]
    ctx_peers = [
        (jx, jy, jc) for jx in range(4) for jy in range(2) for jc in range(2)
        if (jx, jy, jc) != (0, 0, 0)
    ]

    table = pltpu.make_async_copy(route_hbm, route, local.at[6])
    table.start()
    own_cols = pl.ds(pl.multiple_of(h * HD, HD), HD)
    staged = [
        pltpu.make_async_copy(src.at[:, own_cols], own_kv.at[a], local.at[a])
        for a, src in enumerate((k, v))
    ]
    for copy in staged:
        copy.start()

    barrier = pltpu.get_barrier_semaphore()
    for jz, jy in head_peers:
        pl.semaphore_signal(
            barrier, inc=1, device_id=(c, head_of(z + jz, yh + jy)), device_id_type=MESH
        )
    for jx, jy, jc in ctx_peers:
        pl.semaphore_signal(
            barrier, inc=1, device_id=(ctx_of(x + jx, yl + jy, core + jc), h), device_id_type=MESH
        )
    pl.semaphore_wait(barrier, len(head_peers) + len(ctx_peers))

    sent = []

    def go_remote(copy):
        copy.start()
        sent.append(copy)
        return copy

    kv_rows = pl.ds(c * ROWS + h * 32, 32)
    p1 = [[], [], [], []]
    for jz, jy in head_peers:
        j = jz * 2 + jy
        peer = head_of(z + jz, yh + jy)
        cols = pl.ds(pl.multiple_of(peer * HD, HD), HD)
        for a, (src, dst) in enumerate(((k, ko), (v, vo))):
            p1[a].append(go_remote(remote(
                src.at[:, cols], dst.at[kv_rows], p1s.at[a, j], p1r.at[a, j], c, peer)))
    own = [
        pltpu.make_async_copy(own_kv.at[a], dst.at[kv_rows], local.at[a])
        for a, dst in enumerate((ko, vo))
    ]

    def first(a, src, dst):
        for jz, jy in head_peers:
            j = jz * 2 + jy
            peer = head_of(z + jz, yh + jy)
            cols = pl.ds(pl.multiple_of(peer * COLS, COLS), COLS)
            p1[2 + a].append(go_remote(remote(
                src.at[:, :, cols], dst.at[pl.ds(h * 2, 2)],
                p1s.at[2 + a, j], p1r.at[2 + a, j], c, peer)))
        cols = pl.ds(pl.multiple_of(h * COLS, COLS), COLS)
        own.append(pltpu.make_async_copy(
            src.at[:, :, cols], dst.at[pl.ds(h * 2, 2)], local.at[2 + a]))
        own[-1].start()

    first(0, q, xq)
    for a in range(2):
        staged[a].wait()
        own[a].start()

    kv = (ko, vo)

    def shard(a, dx, dy):
        return kv[a].at[pl.ds(ctx_of(x + dx, yl + dy, core) * ROWS, ROWS)]

    def ring(a, dx, dy, tx, ty):
        slot = ((dx - tx) % 4) * 2 + (dy - ty) % 2
        part = shard(a, dx, dy)
        return remote(part, part, rs.at[a, slot], rr.at[a, slot],
                      ctx_of(x + tx + 4, yl + ty + 2, core), h)

    def partner(a, dx, dy):
        slot = dx * 2 + dy
        part = shard(a, dx, dy)
        return remote(part, part, cs.at[a, slot], cr.at[a, slot], ctx_of(x, yl, core + 1), h)

    def arrived(a, dx, dy):
        slot = dx * 2 + dy
        part = shard(a, dx, dy)
        remote(part, part, rs.at[a, slot], rr.at[a, slot], c, h).wait_recv()

    for a in range(2):
        own[a].wait()
        for copy in p1[a]:
            copy.wait_recv()
    for a in range(2):
        go_remote(ring(a, 0, 0, 0, 1))
        go_remote(ring(a, 0, 0, 1, 0))
        go_remote(ring(a, 0, 0, -1, 0))
    first(1, g, xg)
    for a in range(2):
        go_remote(partner(a, 0, 0))

    table.wait()

    def second(a, stage, send, out):
        own[2 + a].wait()
        for copy in p1[2 + a]:
            copy.wait_recv()

        def pick(d, carry):
            block = jnp.int32(0)
            for b in range(SHARDS):
                block = jnp.where(route[c, b] == d, b, block)
            send[d] = stage[block]
            return carry

        lax.fori_loop(0, SHARDS, pick, 0)
        mine = pltpu.make_async_copy(send.at[c], out.at[c], local.at[4 + a])
        mine.start()
        copies = []
        for jx, jy, jc in ctx_peers:
            j = (jx * 2 + jy) * 2 + jc
            d = ctx_of(x + jx, yl + jy, core + jc)
            copies.append(go_remote(remote(
                send.at[d], out.at[c], p2s.at[a, j], p2r.at[a, j], d, h)))
        return mine, copies

    def sides(dy):
        arrived(0, 3, dy)
        go_remote(ring(0, 3, dy, 1, 0))
        arrived(1, 1, dy)
        go_remote(ring(1, 1, dy, -1, 0))
        arrived(0, 1, dy)
        arrived(1, 3, dy)
        for a in range(2):
            go_remote(partner(a, 3, dy))
            go_remote(partner(a, 1, dy))

    sides(0)
    for a in range(2):
        arrived(a, 0, 1)
        go_remote(ring(a, 0, 1, 1, 0))
        go_remote(ring(a, 0, 1, -1, 0))
        go_remote(partner(a, 0, 1))
    mine_q, p2q = second(0, xq, sq, qo)
    sides(1)
    for a in range(2):
        arrived(a, 2, 0)
        go_remote(partner(a, 2, 0))
    mine_g, p2g = second(1, xg, sg, go)
    for a in range(2):
        arrived(a, 2, 1)
        go_remote(partner(a, 2, 1))
    for a in range(2):
        for dx in range(4):
            for dy in range(2):
                slot = dx * 2 + dy
                part = kv[a].at[pl.ds(ctx_of(x + dx, yl + dy, core + 1) * ROWS, ROWS)]
                remote(part, part, cs.at[a, slot], cr.at[a, slot], c, h).wait_recv()
    fetch = [pltpu.make_async_copy(kv[a], all_kv.at[a], local.at[a]) for a in range(2)]
    for copy in fetch:
        copy.start()
    turns = []
    for a, out in enumerate((kto, vto)):
        fetch[a].wait()

        def turn(i, carry):
            for e in range(4):
                t = i * 4 + e
                turned[a, t] = all_kv[a, pl.ds(pl.multiple_of(t * ROWS, ROWS), ROWS), :].T
            return carry

        lax.fori_loop(0, SHARDS // 4, turn, 0)
        turns.append(pltpu.make_async_copy(turned.at[a], out, local.at[2 + a]))
        turns[-1].start()
    mine_q.wait()
    mine_g.wait()

    def received(a, out):
        for jx, jy, jc in ctx_peers:
            j = (jx * 2 + jy) * 2 + jc
            src = ctx_of(x - jx + 4, yl - jy + 2, core - jc + 2)
            remote(out.at[src], out.at[src], p2s.at[a, j], p2r.at[a, j], c, h).wait_recv()

    received(0, qo)
    for copy in turns:
        copy.wait()
    received(1, go)
    for copy in sent:
        copy.wait_send()


def exchange(route, q, k, v, g):
    return pl.pallas_call(
        exchange_kernel,
        name="exchange",
        out_shape=(
            jax.ShapeDtypeStruct((SHARDS, BLOCK, COLS), BF),
            jax.ShapeDtypeStruct((SHARDS, BLOCK, COLS), BF),
            jax.ShapeDtypeStruct((SEQ, HD), BF),
            jax.ShapeDtypeStruct((SEQ, HD), BF),
            jax.ShapeDtypeStruct((SHARDS, HD, ROWS), BF),
            jax.ShapeDtypeStruct((SHARDS, HD, ROWS), BF),
        ),
        in_specs=[ANY, ANY, ANY, ANY, ANY],
        out_specs=(ANY,) * 6,
        scratch_shapes=[
            pltpu.VMEM((SHARDS, BLOCK, COLS), BF),
            pltpu.VMEM((SHARDS, BLOCK, COLS), BF),
            pltpu.VMEM((SHARDS, BLOCK, COLS), BF),
            pltpu.VMEM((SHARDS, BLOCK, COLS), BF),
            pltpu.VMEM((2, 32, HD), BF),
            pltpu.VMEM((2, SEQ, HD), BF),
            pltpu.VMEM((2, SHARDS, HD, ROWS), BF),
            pltpu.SMEM((SHARDS, SHARDS), jnp.int32),
            pltpu.SemaphoreType.DMA((4, 8)),
            pltpu.SemaphoreType.DMA((4, 8)),
            pltpu.SemaphoreType.DMA((2, 16)),
            pltpu.SemaphoreType.DMA((2, 16)),
            pltpu.SemaphoreType.DMA((2, 24)),
            pltpu.SemaphoreType.DMA((2, 8)),
            pltpu.SemaphoreType.DMA((2, 8)),
            pltpu.SemaphoreType.DMA((2, 8)),
            pltpu.SemaphoreType.DMA((7,)),
        ],
        compiler_params=pltpu.CompilerParams(collective_id=0, has_side_effects=True),
    )(route, q, k, v, g)


def attention_kernel(
    route_hbm, docs_hbm, q_hbm, g_hbm, k_hbm, v_hbm, kt_hbm, vt_hbm, att_hbm, dq_hbm, dkv_hbm,
    q, g, k, v, att, dq, dkv,
    s_buf, dp_buf, kt, vt, dk_acc, dv_acc, ot_acc, dqt_acc, route, docs, starts, load, store,
):
    tables = (
        pltpu.make_async_copy(route_hbm, route, store.at[0]),
        pltpu.make_async_copy(docs_hbm, docs, store.at[1]),
    )
    for copy in tables:
        copy.start()
    pairs = ((k_hbm, k), (q_hbm, q), (v_hbm, v), (g_hbm, g), (vt_hbm, vt), (kt_hbm, kt))

    def incoming(n):
        rows = pl.ds(n * SPAN, SPAN)
        return [
            pltpu.make_async_copy(src.at[rows], dst.at[rows], load.at[n, i])
            for i, (src, dst) in enumerate(pairs)
        ]

    for n in range(SHARDS // SPAN):
        for copy in incoming(n):
            copy.start()
    for copy in tables:
        copy.wait()
    c = lax.axis_index("ctx")
    ends = []
    total = jnp.int32(0)
    for j in range(DOCS):
        total = total + docs[j]
        ends.append(total)

    def find(s, carry):
        block = jnp.int32(0)
        for b in range(SHARDS):
            block = jnp.where(route[s, b] == c, b, block)
        starts[s] = s * ROWS + block * BLOCK
        return carry

    lax.fori_loop(0, SHARDS, find, 0)
    def stack(ref, first):
        parts = []
        for i in range(SPAN):
            rows = ref[first + i]
            parts += [rows[:, n * HD:(n + 1) * HD] for n in range(GROUP)]
        return jnp.concatenate(parts, axis=0)

    def outgoing(n):
        rows = pl.ds(n * SPAN, SPAN)
        return (
            pltpu.make_async_copy(att.at[rows], att_hbm.at[rows], store.at[0]),
            pltpu.make_async_copy(dq.at[rows], dq_hbm.at[rows], store.at[1]),
        )

    within = lax.rem(lax.broadcasted_iota(jnp.int32, (1, WIDTH), 1), BLOCK)
    key = lax.broadcasted_iota(jnp.int32, (ROWS, WIDTH), 0)

    def group(n, carry):
        first = n * SPAN
        for copy in incoming(n):
            copy.wait()
        qg = stack(q, first)
        gg = stack(g, first)
        qt = qg.T
        gt = gg.T
        q_pos = jnp.concatenate([within + starts[first + i] for i in range(SPAN)], axis=1)
        q_doc = jnp.zeros_like(q_pos)
        marks = [starts[first], starts[first + 1], starts[first + 2]]
        lows = [jnp.int32(0)] * 3
        for end in ends:
            q_doc = jnp.where(q_pos >= end, end, q_doc)
            lows = [jnp.where(mark >= end, end, low) for mark, low in zip(marks, lows)]
        t_one, t_two, t_low = [jnp.minimum(low // ROWS, first) for low in lows]
        t_even = t_low + lax.rem(first - t_low, 2)
        twos = (first - t_even) // 2
        reach = (q_pos - q_doc).astype(jnp.uint32)

        def scores(t, lane, stop=LANES):
            s = jnp.dot(k[t], qt[:, lane:stop], preferred_element_type=F32)
            return s * (SCALE * LOG2E)

        def slopes(t, lane, stop=LANES):
            return jnp.dot(v[t], gt[:, lane:stop], preferred_element_type=F32)

        def masked(t, lane, stop=LANES):
            s = scores(t, lane, stop)
            offset = t * ROWS - q_doc[:, lane:stop]
            parts = []
            for i in range(0, stop - lane, WIDTH):
                past = (key + offset[:, i:i + WIDTH]).astype(jnp.uint32)
                seen = past <= reach[:, lane + i:lane + i + WIDTH]
                parts.append(jnp.where(seen, s[:, i:i + WIDTH], NEGATIVE))
            return jnp.concatenate(parts, axis=1)

        ot_acc[...] = jnp.zeros_like(ot_acc)
        dqt_acc[...] = jnp.zeros_like(dqt_acc)

        def forward(base, width, stop):
            def step(n, carried):
                peak, mass = carried
                tiles = [base + n * width + i for i in range(width)]
                new_peak = peak[:, :stop]
                for t in tiles:
                    s = masked(t, 0, stop)
                    s_buf[t, :, :stop] = s
                    if stop < LANES or width == 2:
                        dp_buf[t, :, :stop] = slopes(t, 0, stop)
                    new_peak = jnp.maximum(new_peak, jnp.max(s, axis=0, keepdims=True))
                fade = jnp.exp2(peak[:, :stop] - new_peak)
                new_mass = mass[:, :stop] * fade
                total = ot_acc[:, :stop] * fade
                for t in tiles:
                    p = jnp.exp2(s_buf[t, :, :stop] - new_peak)
                    new_mass = new_mass + jnp.sum(p, axis=0, keepdims=True)
                    total = total + jnp.dot(vt[t], p.astype(BF), preferred_element_type=F32)
                ot_acc[:, :stop] = total
                if stop < LANES:
                    new_peak = jnp.concatenate([new_peak, peak[:, stop:]], axis=1)
                    new_mass = jnp.concatenate([new_mass, mass[:, stop:]], axis=1)
                return new_peak, new_mass

            return step

        state = (jnp.full((1, LANES), FLOOR, F32), jnp.zeros((1, LANES), F32))
        state = lax.fori_loop(0, t_two - t_one, forward(t_one, 1, WIDTH), state)
        state = lax.fori_loop(0, t_low - t_two, forward(t_two, 1, 2 * WIDTH), state)
        state = lax.fori_loop(0, t_even - t_low, forward(t_low, 1, LANES), state)
        peak, mass = lax.fori_loop(0, twos, forward(t_even, 2, LANES), state)

        tops = [[peak[:, i * WIDTH:(i + 1) * WIDTH]] for i in range(SPAN)]
        for e in range(SPAN):
            s = masked(first + e, e * WIDTH)
            s_buf[first + e, :, e * WIDTH:] = s
            dp_buf[first + e, :, e * WIDTH:] = slopes(first + e, e * WIDTH)
            top = jnp.max(s, axis=0, keepdims=True)
            for i in range(e, SPAN):
                tops[i].append(top[:, (i - e) * WIDTH:(i - e + 1) * WIDTH])
        new_peak = jnp.concatenate([functools.reduce(jnp.maximum, t) for t in tops], axis=1)
        fade = jnp.exp2(peak - new_peak)
        mass = mass * fade
        masses = [[mass[:, i * WIDTH:(i + 1) * WIDTH]] for i in range(SPAN)]
        ot_acc[...] = ot_acc[...] * fade
        for e in range(SPAN):
            p = jnp.exp2(s_buf[first + e, :, e * WIDTH:] - new_peak[:, e * WIDTH:])
            add = jnp.sum(p, axis=0, keepdims=True)
            for i in range(e, SPAN):
                masses[i].append(add[:, (i - e) * WIDTH:(i - e + 1) * WIDTH])
            ot_acc[:, e * WIDTH:] += jnp.dot(
                vt[first + e], p.astype(BF), preferred_element_type=F32)
        mass = jnp.concatenate([functools.reduce(jnp.add, t) for t in masses], axis=1)
        lse = new_peak + jnp.log2(mass)
        ot = (ot_acc[...] * (1.0 / mass)).astype(BF)
        delta = jnp.sum(gt.astype(F32) * ot.astype(F32), axis=0, keepdims=True)
        o = ot.T
        for i in range(SPAN):
            for m in range(GROUP):
                r = (i * GROUP + m) * BLOCK
                att[first + i, :, m * HD:(m + 1) * HD] = o[r:r + BLOCK]

        def pull(t, lane, stop=LANES, held=True):
            p = jnp.exp2(s_buf[t, :, lane:stop] - lse[:, lane:stop])
            dp = dp_buf[t, :, lane:stop] if held else slopes(t, lane, stop)
            ds = (p * (dp - delta[:, lane:stop])).astype(BF)
            grad_v = jnp.dot(p.astype(BF), gg[lane:stop], preferred_element_type=F32)
            grad_k = jnp.dot(ds, qg[lane:stop], preferred_element_type=F32)
            dqt_acc[:, lane:stop] += jnp.dot(kt[t], ds, preferred_element_type=F32)
            return grad_v, grad_k

        for e in range(SPAN):
            grad_v, grad_k = pull(first + e, e * WIDTH)
            dv_acc[first + e] = grad_v
            dk_acc[first + e] = grad_k

        def backward(stop, held):
            def step(t, carried):
                grad_v, grad_k = pull(t, 0, stop, held)
                dv_acc[t] += grad_v
                dk_acc[t] += grad_k
                return carried

            return step

        lax.fori_loop(t_one, t_two, backward(WIDTH, True), 0)
        lax.fori_loop(t_two, t_low, backward(2 * WIDTH, True), 0)
        lax.fori_loop(t_low, t_even, backward(LANES, False), 0)

        def backward_two(n, carried):
            for i in range(2):
                backward(LANES, True)(t_even + n * 2 + i, carried)
            return carried

        lax.fori_loop(0, twos, backward_two, 0)
        grad = dqt_acc[...].T * SCALE
        for i in range(SPAN):
            for m in range(GROUP):
                r = (i * GROUP + m) * BLOCK
                dq[first + i, :, m * HD:(m + 1) * HD] = grad[r:r + BLOCK]
        for copy in outgoing(n):
            copy.start()
        return carry

    lax.fori_loop(0, SHARDS // SPAN, group, 0)

    def outbound(n):
        cols = pl.ds(n * SPAN, SPAN)
        return pltpu.make_async_copy(dkv.at[:, cols], dkv_hbm.at[:, cols], load.at[n, 0])

    def regroup(s, carry):
        for b in range(SHARDS):
            rows = slice(b * BLOCK, (b + 1) * BLOCK)
            dkv[route[s, b], s] = jnp.stack(
                [(dk_acc[s, rows] * SCALE).astype(BF), dv_acc[s, rows].astype(BF)])
        return carry

    for n in range(SHARDS // SPAN):
        lax.fori_loop(n * SPAN, (n + 1) * SPAN, regroup, 0)
        outbound(n).start()
    pltpu.make_async_copy(att, att_hbm, store.at[0]).wait()
    pltpu.make_async_copy(dq, dq_hbm, store.at[1]).wait()
    for n in range(SHARDS // SPAN):
        outbound(n).wait()


def attention(route, docs, q, g, k, v, kt, vt):
    return pl.pallas_call(
        attention_kernel,
        name="attention",
        out_shape=(
            jax.ShapeDtypeStruct((SHARDS, BLOCK, COLS), BF),
            jax.ShapeDtypeStruct((SHARDS, BLOCK, COLS), F32),
            jax.ShapeDtypeStruct((SHARDS, SHARDS, 2, BLOCK, HD), BF),
        ),
        in_specs=[ANY] * 8,
        out_specs=(ANY, ANY, ANY),
        scratch_shapes=[
            pltpu.VMEM((SHARDS, BLOCK, COLS), BF),
            pltpu.VMEM((SHARDS, BLOCK, COLS), BF),
            pltpu.VMEM((SHARDS, ROWS, HD), BF),
            pltpu.VMEM((SHARDS, ROWS, HD), BF),
            pltpu.VMEM((SHARDS, BLOCK, COLS), BF),
            pltpu.VMEM((SHARDS, BLOCK, COLS), F32),
            pltpu.VMEM((SHARDS, SHARDS, 2, BLOCK, HD), BF),
            pltpu.VMEM((SHARDS, ROWS, LANES), F32),
            pltpu.VMEM((SHARDS, ROWS, LANES), F32),
            pltpu.VMEM((SHARDS, HD, ROWS), BF),
            pltpu.VMEM((SHARDS, HD, ROWS), BF),
            pltpu.VMEM((SHARDS, ROWS, HD), F32),
            pltpu.VMEM((SHARDS, ROWS, HD), F32),
            pltpu.VMEM((HD, LANES), F32),
            pltpu.VMEM((HD, LANES), F32),
            pltpu.SMEM((SHARDS, SHARDS), jnp.int32),
            pltpu.SMEM((DOCS,), jnp.int32),
            pltpu.SMEM((SHARDS,), jnp.int32),
            pltpu.SemaphoreType.DMA((SHARDS // SPAN, 6)),
            pltpu.SemaphoreType.DMA((2,)),
        ],
    )(route, docs, q, g, k, v, kt, vt)


def reduce_kernel(
    part, chip, keep, mine, mate, ready, hold, kept, from_y, from_x,
    s1, r1, sy, ry, sx, rx, s2, r2, local,
):
    c = lax.axis_index("ctx")
    h = lax.axis_index("head")
    x, yl, core = c // 4, lax.rem(c // 2, 2), lax.rem(c, 2)
    other = ctx_of(x, yl, core + 1)
    across = ctx_of(x, yl + 1, core)
    far = (2, 1, 3, 0)
    order = [(dx, dy) for dx in far for dy in (1, 0)]

    def along(dx):
        return ctx_of(x + dx, yl, core)

    def place(dx, dy):
        return lax.rem(x + dx, 4) * 2 + lax.rem(yl + dy, 2)

    loads = []
    for i, (dx, dy) in enumerate(order):
        t = place(dx, dy)
        copy = pltpu.make_async_copy(part.at[t * 2 + core], mine.at[t], local.at[i])
        copy.start()
        loads.append(copy)

    barrier = pltpu.get_barrier_semaphore()
    for peer in (other, across, along(1), along(2), along(3)):
        pl.semaphore_signal(barrier, inc=1, device_id=(peer, h), device_id_type=MESH)
    pl.semaphore_wait(barrier, 5)

    sent = []

    def start(*args):
        copy = remote(*args, h)
        copy.start()
        sent.append(copy)
        return copy

    pairs = []
    for i, (dx, dy) in enumerate(order):
        t = place(dx, dy)
        pairs.append(start(part.at[t * 2 + 1 - core], mate.at[t], s1.at[i], r1.at[i], other))

    for (dx, dy), pair, load in zip(order, pairs, loads):
        t = place(dx, dy)
        load.wait()
        pair.wait_recv()
        sums = [mine[t, :, a].astype(F32) + mate[t, :, a].astype(F32) for a in range(2)]
        if dy == 1:
            ready[t, 0] = sums[0].astype(BF)
            start(ready.at[t, 0], from_y.at[dx], sy.at[dx], ry.at[dx], across)
        else:
            hold[dx] = sums[0]
        if dx == 0:
            kept[1 - dy] = sums[1]
        else:
            ready[t, 1] = sums[1].astype(BF)
            start(ready.at[t, 1], from_x.at[dx - 1, dy], sx.at[dx - 1, dy], rx.at[dx - 1, dy],
                  along(dx))

    for dx in far:
        remote(from_y.at[dx], from_y.at[dx], sy.at[dx], ry.at[dx], across, h).wait_recv()
        hold[dx] += from_y[dx].astype(F32)
        if dx:
            t = place(dx, 0)
            ready[t, 0] = hold[dx].astype(BF)
            start(ready.at[t, 0], chip.at[dx - 1], s2.at[dx], r2.at[dx], along(dx))
    for dy in (1, 0):
        for dx in (1, 3, 2):
            part_in = from_x.at[dx - 1, dy]
            remote(part_in, part_in, sx.at[dx - 1, dy], rx.at[dx - 1, dy], across, h).wait_recv()
            kept[1 - dy] += from_x[dx - 1, dy].astype(F32)
        if dy:
            t = place(0, 1)
            ready[t, 1] = kept[0].astype(BF)
            start(ready.at[t, 1], chip.at[3], s2.at[0], r2.at[0], across)
    outs = [
        pltpu.make_async_copy(hold.at[0], keep.at[0], local.at[0]),
        pltpu.make_async_copy(kept.at[1], keep.at[1], local.at[1]),
    ]
    for out in outs:
        out.start()
    for j in range(4):
        slot = chip.at[(j + 3) % 4]
        remote(slot, slot, s2.at[j], r2.at[j], across, h).wait_recv()
    for copy in sent:
        copy.wait_send()
    for out in outs:
        out.wait()


def reduce(part):
    shape = (SHARDS, BLOCK, HD)
    return pl.pallas_call(
        reduce_kernel,
        name="reduce",
        out_shape=(
            jax.ShapeDtypeStruct((4,) + shape, BF),
            jax.ShapeDtypeStruct((2,) + shape, F32),
        ),
        in_specs=[ANY],
        out_specs=(ANY, ANY),
        scratch_shapes=[
            pltpu.VMEM((8, SHARDS, 2, BLOCK, HD), BF),
            pltpu.VMEM((8, SHARDS, 2, BLOCK, HD), BF),
            pltpu.VMEM((8, 2) + shape, BF),
            pltpu.VMEM((4,) + shape, F32),
            pltpu.VMEM((2,) + shape, F32),
            pltpu.VMEM((4,) + shape, BF),
            pltpu.VMEM((3, 2) + shape, BF),
            pltpu.SemaphoreType.DMA((8,)),
            pltpu.SemaphoreType.DMA((8,)),
            pltpu.SemaphoreType.DMA((4,)),
            pltpu.SemaphoreType.DMA((4,)),
            pltpu.SemaphoreType.DMA((3, 2)),
            pltpu.SemaphoreType.DMA((3, 2)),
            pltpu.SemaphoreType.DMA((4,)),
            pltpu.SemaphoreType.DMA((4,)),
            pltpu.SemaphoreType.DMA((8,)),
        ],
        compiler_params=pltpu.CompilerParams(collective_id=1, has_side_effects=True),
    )(part)


def finish_kernel(chip_hbm, keep_hbm, dk_hbm, dv_hbm, chip, keep, load, store):
    parts = (pl.ds(0, 3), pl.ds(3, 1))
    loads = []
    for a in range(2):
        loads.append((
            pltpu.make_async_copy(chip_hbm.at[parts[a]], chip.at[parts[a]], load.at[a, 0]),
            pltpu.make_async_copy(keep_hbm.at[a], keep.at[a], load.at[a, 1]),
        ))
        for copy in loads[a]:
            copy.start()
    outs = []
    for a, out in enumerate((dk_hbm, dv_hbm)):
        for copy in loads[a]:
            copy.wait()
        total = keep[a]
        for j in ((0, 1, 2), (3,))[a]:
            total = total + chip[j].astype(F32)
        keep[a] = total
        outs.append(pltpu.make_async_copy(keep.at[a], out, store.at[a]))
        outs[a].start()
    for copy in outs:
        copy.wait()


def finish(chip, keep):
    out = jax.ShapeDtypeStruct((SHARDS, BLOCK, HD), F32)
    return pl.pallas_call(
        finish_kernel,
        name="finish",
        out_shape=(out, out),
        in_specs=[ANY, ANY],
        out_specs=(ANY, ANY),
        scratch_shapes=[
            pltpu.VMEM(chip.shape, BF),
            pltpu.VMEM(keep.shape, F32),
            pltpu.SemaphoreType.DMA((2, 2)),
            pltpu.SemaphoreType.DMA((2,)),
        ],
    )(chip, keep)


def on_device(queries, key_rows, value_rows, cotangent, doc_lengths, block_route):
    q, g, k, v, kt, vt = exchange(
        block_route,
        queries.reshape(2, BLOCK, HEADS * COLS),
        key_rows,
        value_rows,
        cotangent.reshape(2, BLOCK, HEADS * COLS),
    )
    att, dq, part = attention(
        block_route, doc_lengths, q, g, k.reshape(SHARDS, ROWS, HD), v.reshape(SHARDS, ROWS, HD), kt, vt)
    dk, dv = finish(*reduce(part))
    return (
        att.reshape(ROWS, COLS),
        dq.reshape(ROWS, COLS),
        dk.reshape(ROWS, HD),
        dv.reshape(ROWS, HD),
    )


def solution(mesh):
    placed = P(("ctx", "head"), None)
    return jax.shard_map(
        on_device,
        mesh=mesh,
        in_specs=(placed, placed, placed, placed, P(), P()),
        out_specs=(P("ctx", "head"),) * 4,
        check_vma=False,
    )
```

```python
import functools
import math

import jax
import jax.numpy as jnp
from jax import lax
from jax.experimental import pallas as pl
from jax.experimental.pallas import tpu as pltpu
from jax.sharding import PartitionSpec as P

HD = 128
GROUP = 8
SHARDS = 16
BLOCK = 16
ROWS = SHARDS * BLOCK
SEQ = SHARDS * ROWS
DOCS = 8
HEADS = 8
COLS = GROUP * HD

SPAN = 4
WIDTH = GROUP * BLOCK
LANES = SPAN * WIDTH
NEGATIVE = -1e30
FLOOR = -0.5e30
SCALE = 1.0 / math.sqrt(HD)
LOG2E = 1.4426950408889634

BF = jnp.bfloat16
F32 = jnp.float32
MESH = pl.DeviceIdType.MESH
ANY = pl.BlockSpec(memory_space=pl.ANY)
VMEM = pl.BlockSpec(memory_space=pltpu.VMEM)
SMEM = pl.BlockSpec(memory_space=pltpu.SMEM)


def ctx_of(x, y, core):
    return (lax.rem(x, 4) * 2 + lax.rem(y, 2)) * 2 + lax.rem(core, 2)


def head_of(z, y):
    return lax.rem(z, 4) * 2 + lax.rem(y, 2)


def remote(src, dst, send, recv, ctx, head):
    return pltpu.make_async_remote_copy(
        src_ref=src,
        dst_ref=dst,
        send_sem=send,
        recv_sem=recv,
        device_id=(ctx, head),
        device_id_type=MESH,
    )


def exchange_kernel(
    route_hbm, q, k, v, g, qo, go, ko, vo, kto, vto,
    xq, xg, sq, sg, own_kv, all_kv, turned, route,
    p1s, p1r, p2s, p2r, rs, rr, cs, cr, local,
):
    c = lax.axis_index("ctx")
    h = lax.axis_index("head")
    z, yh = h // 2, lax.rem(h, 2)
    x, yl, core = c // 4, lax.rem(c // 2, 2), lax.rem(c, 2)
    head_peers = [(jz, jy) for jz in range(4) for jy in range(2) if (jz, jy) != (0, 0)]
    ctx_peers = [
        (jx, jy, jc) for jx in range(4) for jy in range(2) for jc in range(2)
        if (jx, jy, jc) != (0, 0, 0)
    ]

    table = pltpu.make_async_copy(route_hbm, route, local.at[6])
    table.start()
    own_cols = pl.ds(pl.multiple_of(h * HD, HD), HD)
    staged = [
        pltpu.make_async_copy(src.at[:, own_cols], own_kv.at[a], local.at[a])
        for a, src in enumerate((k, v))
    ]
    for copy in staged:
        copy.start()

    barrier = pltpu.get_barrier_semaphore()
    for jz, jy in head_peers:
        pl.semaphore_signal(
            barrier, inc=1, device_id=(c, head_of(z + jz, yh + jy)), device_id_type=MESH
        )
    for jx, jy, jc in ctx_peers:
        pl.semaphore_signal(
            barrier, inc=1, device_id=(ctx_of(x + jx, yl + jy, core + jc), h), device_id_type=MESH
        )
    pl.semaphore_wait(barrier, len(head_peers) + len(ctx_peers))

    sent = []

    def go_remote(copy):
        copy.start()
        sent.append(copy)
        return copy

    kv_rows = pl.ds(c * ROWS + h * 32, 32)
    p1 = [[], [], [], []]
    for jz, jy in head_peers:
        j = jz * 2 + jy
        peer = head_of(z + jz, yh + jy)
        cols = pl.ds(pl.multiple_of(peer * HD, HD), HD)
        for a, (src, dst) in enumerate(((k, ko), (v, vo))):
            p1[a].append(go_remote(remote(
                src.at[:, cols], dst.at[kv_rows], p1s.at[a, j], p1r.at[a, j], c, peer)))
    own = [
        pltpu.make_async_copy(own_kv.at[a], dst.at[kv_rows], local.at[a])
        for a, dst in enumerate((ko, vo))
    ]

    def first(a, src, dst):
        for jz, jy in head_peers:
            j = jz * 2 + jy
            peer = head_of(z + jz, yh + jy)
            cols = pl.ds(pl.multiple_of(peer * COLS, COLS), COLS)
            p1[2 + a].append(go_remote(remote(
                src.at[:, :, cols], dst.at[pl.ds(h * 2, 2)],
                p1s.at[2 + a, j], p1r.at[2 + a, j], c, peer)))
        cols = pl.ds(pl.multiple_of(h * COLS, COLS), COLS)
        own.append(pltpu.make_async_copy(
            src.at[:, :, cols], dst.at[pl.ds(h * 2, 2)], local.at[2 + a]))
        own[-1].start()

    first(0, q, xq)
    for a in range(2):
        staged[a].wait()
        own[a].start()

    kv = (ko, vo)

    def shard(a, dx, dy):
        return kv[a].at[pl.ds(ctx_of(x + dx, yl + dy, core) * ROWS, ROWS)]

    def ring(a, dx, dy, tx, ty):
        slot = ((dx - tx) % 4) * 2 + (dy - ty) % 2
        part = shard(a, dx, dy)
        return remote(part, part, rs.at[a, slot], rr.at[a, slot],
                      ctx_of(x + tx + 4, yl + ty + 2, core), h)

    def partner(a, dx, dy):
        slot = dx * 2 + dy
        part = shard(a, dx, dy)
        return remote(part, part, cs.at[a, slot], cr.at[a, slot], ctx_of(x, yl, core + 1), h)

    def arrived(a, dx, dy):
        slot = dx * 2 + dy
        part = shard(a, dx, dy)
        remote(part, part, rs.at[a, slot], rr.at[a, slot], c, h).wait_recv()

    for a in range(2):
        own[a].wait()
        for copy in p1[a]:
            copy.wait_recv()
    for a in range(2):
        go_remote(ring(a, 0, 0, 0, 1))
        go_remote(ring(a, 0, 0, 1, 0))
        go_remote(ring(a, 0, 0, -1, 0))
    first(1, g, xg)
    for a in range(2):
        go_remote(partner(a, 0, 0))

    table.wait()

    def second(a, stage, send, out):
        own[2 + a].wait()
        for copy in p1[2 + a]:
            copy.wait_recv()

        def pick(d, carry):
            block = jnp.int32(0)
            for b in range(SHARDS):
                block = jnp.where(route[c, b] == d, b, block)
            send[d] = stage[block]
            return carry

        lax.fori_loop(0, SHARDS, pick, 0)
        mine = pltpu.make_async_copy(send.at[c], out.at[c], local.at[4 + a])
        mine.start()
        copies = []
        for jx, jy, jc in ctx_peers:
            j = (jx * 2 + jy) * 2 + jc
            d = ctx_of(x + jx, yl + jy, core + jc)
            copies.append(go_remote(remote(
                send.at[d], out.at[c], p2s.at[a, j], p2r.at[a, j], d, h)))
        return mine, copies

    def sides(dy):
        arrived(0, 3, dy)
        go_remote(ring(0, 3, dy, 1, 0))
        arrived(1, 1, dy)
        go_remote(ring(1, 1, dy, -1, 0))
        arrived(0, 1, dy)
        arrived(1, 3, dy)
        for a in range(2):
            go_remote(partner(a, 3, dy))
            go_remote(partner(a, 1, dy))

    sides(0)
    for a in range(2):
        arrived(a, 0, 1)
        go_remote(ring(a, 0, 1, 1, 0))
        go_remote(ring(a, 0, 1, -1, 0))
        go_remote(partner(a, 0, 1))
    mine_q, p2q = second(0, xq, sq, qo)
    sides(1)
    for a in range(2):
        arrived(a, 2, 0)
        go_remote(partner(a, 2, 0))
    mine_g, p2g = second(1, xg, sg, go)
    for a in range(2):
        arrived(a, 2, 1)
        go_remote(partner(a, 2, 1))
    for a in range(2):
        for dx in range(4):
            for dy in range(2):
                slot = dx * 2 + dy
                part = kv[a].at[pl.ds(ctx_of(x + dx, yl + dy, core + 1) * ROWS, ROWS)]
                remote(part, part, cs.at[a, slot], cr.at[a, slot], c, h).wait_recv()
    fetch = [pltpu.make_async_copy(kv[a], all_kv.at[a], local.at[a]) for a in range(2)]
    for copy in fetch:
        copy.start()
    turns = []
    for a, out in enumerate((kto, vto)):
        fetch[a].wait()

        def turn(i, carry):
            for e in range(4):
                t = i * 4 + e
                turned[a, t] = all_kv[a, pl.ds(pl.multiple_of(t * ROWS, ROWS), ROWS), :].T
            return carry

        lax.fori_loop(0, SHARDS // 4, turn, 0)
        turns.append(pltpu.make_async_copy(turned.at[a], out, local.at[2 + a]))
        turns[-1].start()
    mine_q.wait()
    mine_g.wait()

    def received(a, out):
        for jx, jy, jc in ctx_peers:
            j = (jx * 2 + jy) * 2 + jc
            src = ctx_of(x - jx + 4, yl - jy + 2, core - jc + 2)
            remote(out.at[src], out.at[src], p2s.at[a, j], p2r.at[a, j], c, h).wait_recv()

    received(0, qo)
    for copy in turns:
        copy.wait()
    received(1, go)
    for copy in sent:
        copy.wait_send()


def exchange(route, q, k, v, g):
    return pl.pallas_call(
        exchange_kernel,
        name="exchange",
        out_shape=(
            jax.ShapeDtypeStruct((SHARDS, BLOCK, COLS), BF),
            jax.ShapeDtypeStruct((SHARDS, BLOCK, COLS), BF),
            jax.ShapeDtypeStruct((SEQ, HD), BF),
            jax.ShapeDtypeStruct((SEQ, HD), BF),
            jax.ShapeDtypeStruct((SHARDS, HD, ROWS), BF),
            jax.ShapeDtypeStruct((SHARDS, HD, ROWS), BF),
        ),
        in_specs=[ANY, ANY, ANY, ANY, ANY],
        out_specs=(ANY,) * 6,
        scratch_shapes=[
            pltpu.VMEM((SHARDS, BLOCK, COLS), BF),
            pltpu.VMEM((SHARDS, BLOCK, COLS), BF),
            pltpu.VMEM((SHARDS, BLOCK, COLS), BF),
            pltpu.VMEM((SHARDS, BLOCK, COLS), BF),
            pltpu.VMEM((2, 32, HD), BF),
            pltpu.VMEM((2, SEQ, HD), BF),
            pltpu.VMEM((2, SHARDS, HD, ROWS), BF),
            pltpu.SMEM((SHARDS, SHARDS), jnp.int32),
            pltpu.SemaphoreType.DMA((4, 8)),
            pltpu.SemaphoreType.DMA((4, 8)),
            pltpu.SemaphoreType.DMA((2, 16)),
            pltpu.SemaphoreType.DMA((2, 16)),
            pltpu.SemaphoreType.DMA((2, 24)),
            pltpu.SemaphoreType.DMA((2, 8)),
            pltpu.SemaphoreType.DMA((2, 8)),
            pltpu.SemaphoreType.DMA((2, 8)),
            pltpu.SemaphoreType.DMA((7,)),
        ],
        compiler_params=pltpu.CompilerParams(collective_id=0, has_side_effects=True),
    )(route, q, k, v, g)


def attention_kernel(
    route_hbm, docs_hbm, q_hbm, g_hbm, k_hbm, v_hbm, kt_hbm, vt_hbm, att_hbm, dq_hbm, dkv_hbm,
    q, g, k, v, att, dq, dkv,
    s_buf, dp_buf, kt, vt, dk_acc, dv_acc, ot_acc, dqt_acc, route, docs, starts, load, store,
):
    tables = (
        pltpu.make_async_copy(route_hbm, route, store.at[0]),
        pltpu.make_async_copy(docs_hbm, docs, store.at[1]),
    )
    for copy in tables:
        copy.start()
    pairs = ((k_hbm, k), (q_hbm, q), (v_hbm, v), (g_hbm, g), (vt_hbm, vt), (kt_hbm, kt))

    def incoming(n):
        rows = pl.ds(n * SPAN, SPAN)
        return [
            pltpu.make_async_copy(src.at[rows], dst.at[rows], load.at[n, i])
            for i, (src, dst) in enumerate(pairs)
        ]

    for n in range(SHARDS // SPAN):
        for copy in incoming(n):
            copy.start()
    for copy in tables:
        copy.wait()
    c = lax.axis_index("ctx")
    ends = []
    total = jnp.int32(0)
    for j in range(DOCS):
        total = total + docs[j]
        ends.append(total)

    def find(s, carry):
        block = jnp.int32(0)
        for b in range(SHARDS):
            block = jnp.where(route[s, b] == c, b, block)
        starts[s] = s * ROWS + block * BLOCK
        return carry

    lax.fori_loop(0, SHARDS, find, 0)
    def stack(ref, first):
        parts = []
        for i in range(SPAN):
            rows = ref[first + i]
            parts += [rows[:, n * HD:(n + 1) * HD] for n in range(GROUP)]
        return jnp.concatenate(parts, axis=0)

    def outgoing(n):
        rows = pl.ds(n * SPAN, SPAN)
        return (
            pltpu.make_async_copy(att.at[rows], att_hbm.at[rows], store.at[0]),
            pltpu.make_async_copy(dq.at[rows], dq_hbm.at[rows], store.at[1]),
        )

    within = lax.rem(lax.broadcasted_iota(jnp.int32, (1, WIDTH), 1), BLOCK)
    key = lax.broadcasted_iota(jnp.int32, (ROWS, WIDTH), 0)

    def group(n, carry):
        first = n * SPAN
        for copy in incoming(n):
            copy.wait()
        qg = stack(q, first)
        gg = stack(g, first)
        qt = qg.T
        gt = gg.T
        q_pos = jnp.concatenate([within + starts[first + i] for i in range(SPAN)], axis=1)
        q_doc = jnp.zeros_like(q_pos)
        marks = [starts[first], starts[first + 1], starts[first + 2]]
        lows = [jnp.int32(0)] * 3
        for end in ends:
            q_doc = jnp.where(q_pos >= end, end, q_doc)
            lows = [jnp.where(mark >= end, end, low) for mark, low in zip(marks, lows)]
        t_one, t_two, t_low = [jnp.minimum(low // ROWS, first) for low in lows]
        spans = ((t_one, t_two, WIDTH), (t_two, t_low, 2 * WIDTH), (t_low, first, LANES))
        reach = (q_pos - q_doc).astype(jnp.uint32)

        def scores(t, lane, stop=LANES):
            s = jnp.dot(k[t], qt[:, lane:stop], preferred_element_type=F32)
            return s * (SCALE * LOG2E)

        def slopes(t, lane, stop=LANES):
            return jnp.dot(v[t], gt[:, lane:stop], preferred_element_type=F32)

        def masked(t, lane, stop=LANES):
            s = scores(t, lane, stop)
            offset = t * ROWS - q_doc[:, lane:stop]
            parts = []
            for i in range(0, stop - lane, WIDTH):
                past = (key + offset[:, i:i + WIDTH]).astype(jnp.uint32)
                seen = past <= reach[:, lane + i:lane + i + WIDTH]
                parts.append(jnp.where(seen, s[:, i:i + WIDTH], NEGATIVE))
            return jnp.concatenate(parts, axis=1)

        ot_acc[...] = jnp.zeros_like(ot_acc)
        dqt_acc[...] = jnp.zeros_like(dqt_acc)

        def forward(base, width, stop):
            def step(n, carried):
                peak, mass = carried
                tiles = [base + n * width + i for i in range(width)]
                new_peak = peak[:, :stop]
                for t in tiles:
                    s = masked(t, 0, stop)
                    s_buf[t, :, :stop] = s
                    if stop < LANES or width == 2:
                        dp_buf[t, :, :stop] = slopes(t, 0, stop)
                    new_peak = jnp.maximum(new_peak, jnp.max(s, axis=0, keepdims=True))
                fade = jnp.exp2(peak[:, :stop] - new_peak)
                new_mass = mass[:, :stop] * fade
                total = ot_acc[:, :stop] * fade
                for t in tiles:
                    p = jnp.exp2(s_buf[t, :, :stop] - new_peak)
                    new_mass = new_mass + jnp.sum(p, axis=0, keepdims=True)
                    total = total + jnp.dot(vt[t], p.astype(BF), preferred_element_type=F32)
                ot_acc[:, :stop] = total
                if stop < LANES:
                    new_peak = jnp.concatenate([new_peak, peak[:, stop:]], axis=1)
                    new_mass = jnp.concatenate([new_mass, mass[:, stop:]], axis=1)
                return new_peak, new_mass

            return step

        state = (jnp.full((1, LANES), FLOOR, F32), jnp.zeros((1, LANES), F32))
        for start, stop, lanes in spans:
            odd = lax.rem(stop - start, 2)
            state = lax.fori_loop(0, odd, forward(start, 1, lanes), state)
            state = lax.fori_loop(0, (stop - start) // 2, forward(start + odd, 2, lanes), state)
        peak, mass = state

        tops = [[peak[:, i * WIDTH:(i + 1) * WIDTH]] for i in range(SPAN)]
        for e in range(SPAN):
            s = masked(first + e, e * WIDTH)
            s_buf[first + e, :, e * WIDTH:] = s
            dp_buf[first + e, :, e * WIDTH:] = slopes(first + e, e * WIDTH)
            top = jnp.max(s, axis=0, keepdims=True)
            for i in range(e, SPAN):
                tops[i].append(top[:, (i - e) * WIDTH:(i - e + 1) * WIDTH])
        new_peak = jnp.concatenate([functools.reduce(jnp.maximum, t) for t in tops], axis=1)
        fade = jnp.exp2(peak - new_peak)
        mass = mass * fade
        masses = [[mass[:, i * WIDTH:(i + 1) * WIDTH]] for i in range(SPAN)]
        ot_acc[...] = ot_acc[...] * fade
        for e in range(SPAN):
            p = jnp.exp2(s_buf[first + e, :, e * WIDTH:] - new_peak[:, e * WIDTH:])
            add = jnp.sum(p, axis=0, keepdims=True)
            for i in range(e, SPAN):
                masses[i].append(add[:, (i - e) * WIDTH:(i - e + 1) * WIDTH])
            ot_acc[:, e * WIDTH:] += jnp.dot(
                vt[first + e], p.astype(BF), preferred_element_type=F32)
        mass = jnp.concatenate([functools.reduce(jnp.add, t) for t in masses], axis=1)
        lse = new_peak + jnp.log2(mass)
        ot = (ot_acc[...] * (1.0 / mass)).astype(BF)
        delta = jnp.sum(gt.astype(F32) * ot.astype(F32), axis=0, keepdims=True)
        o = ot.T
        for i in range(SPAN):
            for m in range(GROUP):
                r = (i * GROUP + m) * BLOCK
                att[first + i, :, m * HD:(m + 1) * HD] = o[r:r + BLOCK]

        def pull(t, lane, stop=LANES, held=True):
            p = jnp.exp2(s_buf[t, :, lane:stop] - lse[:, lane:stop])
            dp = dp_buf[t, :, lane:stop] if held else slopes(t, lane, stop)
            ds = (p * (dp - delta[:, lane:stop])).astype(BF)
            grad_v = jnp.dot(p.astype(BF), gg[lane:stop], preferred_element_type=F32)
            grad_k = jnp.dot(ds, qg[lane:stop], preferred_element_type=F32)
            dqt_acc[:, lane:stop] += jnp.dot(kt[t], ds, preferred_element_type=F32)
            return grad_v, grad_k

        for e in range(SPAN):
            grad_v, grad_k = pull(first + e, e * WIDTH)
            dv_acc[first + e] = grad_v
            dk_acc[first + e] = grad_k

        def backward(base, width, stop):
            def step(n, carried):
                for i in range(width):
                    t = base + n * width + i
                    grad_v, grad_k = pull(t, 0, stop, stop < LANES or width == 2)
                    dv_acc[t] += grad_v
                    dk_acc[t] += grad_k
                return carried

            return step

        for start, stop, lanes in spans:
            odd = lax.rem(stop - start, 2) if lanes == LANES else stop - start
            lax.fori_loop(0, odd, backward(start, 1, lanes), 0)
            if lanes == LANES:
                lax.fori_loop(0, (stop - start) // 2, backward(start + odd, 2, lanes), 0)
        grad = dqt_acc[...].T * SCALE
        for i in range(SPAN):
            for m in range(GROUP):
                r = (i * GROUP + m) * BLOCK
                dq[first + i, :, m * HD:(m + 1) * HD] = grad[r:r + BLOCK]
        for copy in outgoing(n):
            copy.start()
        return carry

    lax.fori_loop(0, SHARDS // SPAN, group, 0)

    def outbound(n):
        cols = pl.ds(n * SPAN, SPAN)
        return pltpu.make_async_copy(dkv.at[:, cols], dkv_hbm.at[:, cols], load.at[n, 0])

    def regroup(s, carry):
        for b in range(SHARDS):
            rows = slice(b * BLOCK, (b + 1) * BLOCK)
            dkv[route[s, b], s] = jnp.stack(
                [(dk_acc[s, rows] * SCALE).astype(BF), dv_acc[s, rows].astype(BF)])
        return carry

    for n in range(SHARDS // SPAN):
        lax.fori_loop(n * SPAN, (n + 1) * SPAN, regroup, 0)
        outbound(n).start()
    pltpu.make_async_copy(att, att_hbm, store.at[0]).wait()
    pltpu.make_async_copy(dq, dq_hbm, store.at[1]).wait()
    for n in range(SHARDS // SPAN):
        outbound(n).wait()


def attention(route, docs, q, g, k, v, kt, vt):
    return pl.pallas_call(
        attention_kernel,
        name="attention",
        out_shape=(
            jax.ShapeDtypeStruct((SHARDS, BLOCK, COLS), BF),
            jax.ShapeDtypeStruct((SHARDS, BLOCK, COLS), F32),
            jax.ShapeDtypeStruct((SHARDS, SHARDS, 2, BLOCK, HD), BF),
        ),
        in_specs=[ANY] * 8,
        out_specs=(ANY, ANY, ANY),
        scratch_shapes=[
            pltpu.VMEM((SHARDS, BLOCK, COLS), BF),
            pltpu.VMEM((SHARDS, BLOCK, COLS), BF),
            pltpu.VMEM((SHARDS, ROWS, HD), BF),
            pltpu.VMEM((SHARDS, ROWS, HD), BF),
            pltpu.VMEM((SHARDS, BLOCK, COLS), BF),
            pltpu.VMEM((SHARDS, BLOCK, COLS), F32),
            pltpu.VMEM((SHARDS, SHARDS, 2, BLOCK, HD), BF),
            pltpu.VMEM((SHARDS, ROWS, LANES), F32),
            pltpu.VMEM((SHARDS, ROWS, LANES), F32),
            pltpu.VMEM((SHARDS, HD, ROWS), BF),
            pltpu.VMEM((SHARDS, HD, ROWS), BF),
            pltpu.VMEM((SHARDS, ROWS, HD), F32),
            pltpu.VMEM((SHARDS, ROWS, HD), F32),
            pltpu.VMEM((HD, LANES), F32),
            pltpu.VMEM((HD, LANES), F32),
            pltpu.SMEM((SHARDS, SHARDS), jnp.int32),
            pltpu.SMEM((DOCS,), jnp.int32),
            pltpu.SMEM((SHARDS,), jnp.int32),
            pltpu.SemaphoreType.DMA((SHARDS // SPAN, 6)),
            pltpu.SemaphoreType.DMA((2,)),
        ],
    )(route, docs, q, g, k, v, kt, vt)


def reduce_kernel(
    part, chip, keep, mine, mate, ready, hold, kept, from_y, from_x,
    s1, r1, sy, ry, sx, rx, s2, r2, local,
):
    c = lax.axis_index("ctx")
    h = lax.axis_index("head")
    x, yl, core = c // 4, lax.rem(c // 2, 2), lax.rem(c, 2)
    other = ctx_of(x, yl, core + 1)
    across = ctx_of(x, yl + 1, core)
    far = (2, 1, 3, 0)
    order = [(dx, dy) for dx in far for dy in (1, 0)]

    def along(dx):
        return ctx_of(x + dx, yl, core)

    def place(dx, dy):
        return lax.rem(x + dx, 4) * 2 + lax.rem(yl + dy, 2)

    loads = []
    for i, (dx, dy) in enumerate(order):
        t = place(dx, dy)
        copy = pltpu.make_async_copy(part.at[t * 2 + core], mine.at[t], local.at[i])
        copy.start()
        loads.append(copy)

    barrier = pltpu.get_barrier_semaphore()
    for peer in (other, across, along(1), along(2), along(3)):
        pl.semaphore_signal(barrier, inc=1, device_id=(peer, h), device_id_type=MESH)
    pl.semaphore_wait(barrier, 5)

    sent = []

    def start(*args):
        copy = remote(*args, h)
        copy.start()
        sent.append(copy)
        return copy

    pairs = []
    for i, (dx, dy) in enumerate(order):
        t = place(dx, dy)
        pairs.append(start(part.at[t * 2 + 1 - core], mate.at[t], s1.at[i], r1.at[i], other))

    for (dx, dy), pair, load in zip(order, pairs, loads):
        t = place(dx, dy)
        load.wait()
        pair.wait_recv()
        sums = [mine[t, :, a].astype(F32) + mate[t, :, a].astype(F32) for a in range(2)]
        if dy == 1:
            ready[t, 0] = sums[0].astype(BF)
            start(ready.at[t, 0], from_y.at[dx], sy.at[dx], ry.at[dx], across)
        else:
            hold[dx] = sums[0]
        if dx == 0:
            kept[1 - dy] = sums[1]
        else:
            ready[t, 1] = sums[1].astype(BF)
            start(ready.at[t, 1], from_x.at[dx - 1, dy], sx.at[dx - 1, dy], rx.at[dx - 1, dy],
                  along(dx))

    for dx in far:
        remote(from_y.at[dx], from_y.at[dx], sy.at[dx], ry.at[dx], across, h).wait_recv()
        hold[dx] += from_y[dx].astype(F32)
        if dx:
            t = place(dx, 0)
            ready[t, 0] = hold[dx].astype(BF)
            start(ready.at[t, 0], chip.at[dx - 1], s2.at[dx], r2.at[dx], along(dx))
    for dy in (1, 0):
        for dx in (1, 3, 2):
            part_in = from_x.at[dx - 1, dy]
            remote(part_in, part_in, sx.at[dx - 1, dy], rx.at[dx - 1, dy], across, h).wait_recv()
            kept[1 - dy] += from_x[dx - 1, dy].astype(F32)
        if dy:
            t = place(0, 1)
            ready[t, 1] = kept[0].astype(BF)
            start(ready.at[t, 1], chip.at[3], s2.at[0], r2.at[0], across)
    outs = [
        pltpu.make_async_copy(hold.at[0], keep.at[0], local.at[0]),
        pltpu.make_async_copy(kept.at[1], keep.at[1], local.at[1]),
    ]
    for out in outs:
        out.start()
    for j in range(4):
        slot = chip.at[(j + 3) % 4]
        remote(slot, slot, s2.at[j], r2.at[j], across, h).wait_recv()
    for copy in sent:
        copy.wait_send()
    for out in outs:
        out.wait()


def reduce(part):
    shape = (SHARDS, BLOCK, HD)
    return pl.pallas_call(
        reduce_kernel,
        name="reduce",
        out_shape=(
            jax.ShapeDtypeStruct((4,) + shape, BF),
            jax.ShapeDtypeStruct((2,) + shape, F32),
        ),
        in_specs=[ANY],
        out_specs=(ANY, ANY),
        scratch_shapes=[
            pltpu.VMEM((8, SHARDS, 2, BLOCK, HD), BF),
            pltpu.VMEM((8, SHARDS, 2, BLOCK, HD), BF),
            pltpu.VMEM((8, 2) + shape, BF),
            pltpu.VMEM((4,) + shape, F32),
            pltpu.VMEM((2,) + shape, F32),
            pltpu.VMEM((4,) + shape, BF),
            pltpu.VMEM((3, 2) + shape, BF),
            pltpu.SemaphoreType.DMA((8,)),
            pltpu.SemaphoreType.DMA((8,)),
            pltpu.SemaphoreType.DMA((4,)),
            pltpu.SemaphoreType.DMA((4,)),
            pltpu.SemaphoreType.DMA((3, 2)),
            pltpu.SemaphoreType.DMA((3, 2)),
            pltpu.SemaphoreType.DMA((4,)),
            pltpu.SemaphoreType.DMA((4,)),
            pltpu.SemaphoreType.DMA((8,)),
        ],
        compiler_params=pltpu.CompilerParams(collective_id=1, has_side_effects=True),
    )(part)


def finish_kernel(chip_hbm, keep_hbm, dk_hbm, dv_hbm, chip, keep, load, store):
    parts = (pl.ds(0, 3), pl.ds(3, 1))
    loads = []
    for a in range(2):
        loads.append((
            pltpu.make_async_copy(chip_hbm.at[parts[a]], chip.at[parts[a]], load.at[a, 0]),
            pltpu.make_async_copy(keep_hbm.at[a], keep.at[a], load.at[a, 1]),
        ))
        for copy in loads[a]:
            copy.start()
    outs = []
    for a, out in enumerate((dk_hbm, dv_hbm)):
        for copy in loads[a]:
            copy.wait()
        total = keep[a]
        for j in ((0, 1, 2), (3,))[a]:
            total = total + chip[j].astype(F32)
        keep[a] = total
        outs.append(pltpu.make_async_copy(keep.at[a], out, store.at[a]))
        outs[a].start()
    for copy in outs:
        copy.wait()


def finish(chip, keep):
    out = jax.ShapeDtypeStruct((SHARDS, BLOCK, HD), F32)
    return pl.pallas_call(
        finish_kernel,
        name="finish",
        out_shape=(out, out),
        in_specs=[ANY, ANY],
        out_specs=(ANY, ANY),
        scratch_shapes=[
            pltpu.VMEM(chip.shape, BF),
            pltpu.VMEM(keep.shape, F32),
            pltpu.SemaphoreType.DMA((2, 2)),
            pltpu.SemaphoreType.DMA((2,)),
        ],
    )(chip, keep)


def on_device(queries, key_rows, value_rows, cotangent, doc_lengths, block_route):
    q, g, k, v, kt, vt = exchange(
        block_route,
        queries.reshape(2, BLOCK, HEADS * COLS),
        key_rows,
        value_rows,
        cotangent.reshape(2, BLOCK, HEADS * COLS),
    )
    att, dq, part = attention(
        block_route, doc_lengths, q, g, k.reshape(SHARDS, ROWS, HD), v.reshape(SHARDS, ROWS, HD), kt, vt)
    dk, dv = finish(*reduce(part))
    return (
        att.reshape(ROWS, COLS),
        dq.reshape(ROWS, COLS),
        dk.reshape(ROWS, HD),
        dv.reshape(ROWS, HD),
    )


def solution(mesh):
    placed = P(("ctx", "head"), None)
    return jax.shard_map(
        on_device,
        mesh=mesh,
        in_specs=(placed, placed, placed, placed, P(), P()),
        out_specs=(P("ctx", "head"),) * 4,
        check_vma=False,
    )
```

```python
import functools
import math

import jax
import jax.numpy as jnp
from jax import lax
from jax.experimental import pallas as pl
from jax.experimental.pallas import tpu as pltpu
from jax.sharding import PartitionSpec as P

HD = 128
GROUP = 8
SHARDS = 16
BLOCK = 16
ROWS = SHARDS * BLOCK
SEQ = SHARDS * ROWS
DOCS = 8
HEADS = 8
COLS = GROUP * HD

SPAN = 4
WIDTH = GROUP * BLOCK
LANES = SPAN * WIDTH
NEGATIVE = -1e30
FLOOR = -0.5e30
SCALE = 1.0 / math.sqrt(HD)
LOG2E = 1.4426950408889634

BF = jnp.bfloat16
F32 = jnp.float32
MESH = pl.DeviceIdType.MESH
ANY = pl.BlockSpec(memory_space=pl.ANY)
VMEM = pl.BlockSpec(memory_space=pltpu.VMEM)
SMEM = pl.BlockSpec(memory_space=pltpu.SMEM)


def ctx_of(x, y, core):
    return (lax.rem(x, 4) * 2 + lax.rem(y, 2)) * 2 + lax.rem(core, 2)


def head_of(z, y):
    return lax.rem(z, 4) * 2 + lax.rem(y, 2)


def remote(src, dst, send, recv, ctx, head):
    return pltpu.make_async_remote_copy(
        src_ref=src,
        dst_ref=dst,
        send_sem=send,
        recv_sem=recv,
        device_id=(ctx, head),
        device_id_type=MESH,
    )


def exchange_kernel(
    route_hbm, q, k, v, g, qo, go, ko, vo, kto, vto,
    xq, xg, sq, sg, own_kv, all_kv, turned, route,
    p1s, p1r, p2s, p2r, rs, rr, cs, cr, local,
):
    c = lax.axis_index("ctx")
    h = lax.axis_index("head")
    z, yh = h // 2, lax.rem(h, 2)
    x, yl, core = c // 4, lax.rem(c // 2, 2), lax.rem(c, 2)
    head_peers = [(jz, jy) for jz in range(4) for jy in range(2) if (jz, jy) != (0, 0)]
    ctx_peers = [
        (jx, jy, jc) for jx in range(4) for jy in range(2) for jc in range(2)
        if (jx, jy, jc) != (0, 0, 0)
    ]

    table = pltpu.make_async_copy(route_hbm, route, local.at[6])
    table.start()
    own_cols = pl.ds(pl.multiple_of(h * HD, HD), HD)
    staged = [
        pltpu.make_async_copy(src.at[:, own_cols], own_kv.at[a], local.at[a])
        for a, src in enumerate((k, v))
    ]
    for copy in staged:
        copy.start()

    barrier = pltpu.get_barrier_semaphore()
    for jz, jy in head_peers:
        pl.semaphore_signal(
            barrier, inc=1, device_id=(c, head_of(z + jz, yh + jy)), device_id_type=MESH
        )
    for jx, jy, jc in ctx_peers:
        pl.semaphore_signal(
            barrier, inc=1, device_id=(ctx_of(x + jx, yl + jy, core + jc), h), device_id_type=MESH
        )
    pl.semaphore_wait(barrier, len(head_peers) + len(ctx_peers))

    sent = []

    def go_remote(copy):
        copy.start()
        sent.append(copy)
        return copy

    kv_rows = pl.ds(c * ROWS + h * 32, 32)
    p1 = [[], [], [], []]
    for jz, jy in head_peers:
        j = jz * 2 + jy
        peer = head_of(z + jz, yh + jy)
        cols = pl.ds(pl.multiple_of(peer * HD, HD), HD)
        for a, (src, dst) in enumerate(((k, ko), (v, vo))):
            p1[a].append(go_remote(remote(
                src.at[:, cols], dst.at[kv_rows], p1s.at[a, j], p1r.at[a, j], c, peer)))
    own = [
        pltpu.make_async_copy(own_kv.at[a], dst.at[kv_rows], local.at[a])
        for a, dst in enumerate((ko, vo))
    ]

    def first(a, src, dst):
        for jz, jy in head_peers:
            j = jz * 2 + jy
            peer = head_of(z + jz, yh + jy)
            cols = pl.ds(pl.multiple_of(peer * COLS, COLS), COLS)
            p1[2 + a].append(go_remote(remote(
                src.at[:, :, cols], dst.at[pl.ds(h * 2, 2)],
                p1s.at[2 + a, j], p1r.at[2 + a, j], c, peer)))
        cols = pl.ds(pl.multiple_of(h * COLS, COLS), COLS)
        own.append(pltpu.make_async_copy(
            src.at[:, :, cols], dst.at[pl.ds(h * 2, 2)], local.at[2 + a]))
        own[-1].start()

    first(0, q, xq)
    for a in range(2):
        staged[a].wait()
        own[a].start()

    kv = (ko, vo)

    def shard(a, dx, dy):
        return kv[a].at[pl.ds(ctx_of(x + dx, yl + dy, core) * ROWS, ROWS)]

    def ring(a, dx, dy, tx, ty):
        slot = ((dx - tx) % 4) * 2 + (dy - ty) % 2
        part = shard(a, dx, dy)
        return remote(part, part, rs.at[a, slot], rr.at[a, slot],
                      ctx_of(x + tx + 4, yl + ty + 2, core), h)

    def partner(a, dx, dy):
        slot = dx * 2 + dy
        part = shard(a, dx, dy)
        return remote(part, part, cs.at[a, slot], cr.at[a, slot], ctx_of(x, yl, core + 1), h)

    def arrived(a, dx, dy):
        slot = dx * 2 + dy
        part = shard(a, dx, dy)
        remote(part, part, rs.at[a, slot], rr.at[a, slot], c, h).wait_recv()

    for a in range(2):
        own[a].wait()
        for copy in p1[a]:
            copy.wait_recv()
    for a in range(2):
        go_remote(ring(a, 0, 0, 0, 1))
        go_remote(ring(a, 0, 0, 1, 0))
        go_remote(ring(a, 0, 0, -1, 0))
    first(1, g, xg)
    for a in range(2):
        go_remote(partner(a, 0, 0))

    table.wait()

    def second(a, stage, send, out):
        own[2 + a].wait()
        for copy in p1[2 + a]:
            copy.wait_recv()

        def pick(d, carry):
            block = jnp.int32(0)
            for b in range(SHARDS):
                block = jnp.where(route[c, b] == d, b, block)
            send[d] = stage[block]
            return carry

        lax.fori_loop(0, SHARDS, pick, 0)
        mine = pltpu.make_async_copy(send.at[c], out.at[c], local.at[4 + a])
        mine.start()
        copies = []
        for jx, jy, jc in ctx_peers:
            j = (jx * 2 + jy) * 2 + jc
            d = ctx_of(x + jx, yl + jy, core + jc)
            copies.append(go_remote(remote(
                send.at[d], out.at[c], p2s.at[a, j], p2r.at[a, j], d, h)))
        return mine, copies

    def sides(dy):
        arrived(0, 3, dy)
        go_remote(ring(0, 3, dy, 1, 0))
        arrived(1, 1, dy)
        go_remote(ring(1, 1, dy, -1, 0))
        arrived(0, 1, dy)
        arrived(1, 3, dy)
        for a in range(2):
            go_remote(partner(a, 3, dy))
            go_remote(partner(a, 1, dy))

    sides(0)
    for a in range(2):
        arrived(a, 0, 1)
        go_remote(ring(a, 0, 1, 1, 0))
        go_remote(ring(a, 0, 1, -1, 0))
        go_remote(partner(a, 0, 1))
    mine_q, p2q = second(0, xq, sq, qo)
    sides(1)
    for a in range(2):
        arrived(a, 2, 0)
        go_remote(partner(a, 2, 0))
    mine_g, p2g = second(1, xg, sg, go)
    for a in range(2):
        arrived(a, 2, 1)
        go_remote(partner(a, 2, 1))
    for a in range(2):
        for dx in range(4):
            for dy in range(2):
                slot = dx * 2 + dy
                part = kv[a].at[pl.ds(ctx_of(x + dx, yl + dy, core + 1) * ROWS, ROWS)]
                remote(part, part, cs.at[a, slot], cr.at[a, slot], c, h).wait_recv()
    fetch = [pltpu.make_async_copy(kv[a], all_kv.at[a], local.at[a]) for a in range(2)]
    for copy in fetch:
        copy.start()
    turns = []
    for a, out in enumerate((kto, vto)):
        fetch[a].wait()

        def turn(i, carry):
            for e in range(4):
                t = i * 4 + e
                turned[a, t] = all_kv[a, pl.ds(pl.multiple_of(t * ROWS, ROWS), ROWS), :].T
            return carry

        lax.fori_loop(0, SHARDS // 4, turn, 0)
        turns.append(pltpu.make_async_copy(turned.at[a], out, local.at[2 + a]))
        turns[-1].start()
    mine_q.wait()
    mine_g.wait()

    def received(a, out):
        for jx, jy, jc in ctx_peers:
            j = (jx * 2 + jy) * 2 + jc
            src = ctx_of(x - jx + 4, yl - jy + 2, core - jc + 2)
            remote(out.at[src], out.at[src], p2s.at[a, j], p2r.at[a, j], c, h).wait_recv()

    received(0, qo)
    for copy in turns:
        copy.wait()
    received(1, go)
    for copy in sent:
        copy.wait_send()


def exchange(route, q, k, v, g):
    return pl.pallas_call(
        exchange_kernel,
        name="exchange",
        out_shape=(
            jax.ShapeDtypeStruct((SHARDS, BLOCK, COLS), BF),
            jax.ShapeDtypeStruct((SHARDS, BLOCK, COLS), BF),
            jax.ShapeDtypeStruct((SEQ, HD), BF),
            jax.ShapeDtypeStruct((SEQ, HD), BF),
            jax.ShapeDtypeStruct((SHARDS, HD, ROWS), BF),
            jax.ShapeDtypeStruct((SHARDS, HD, ROWS), BF),
        ),
        in_specs=[ANY, ANY, ANY, ANY, ANY],
        out_specs=(ANY,) * 6,
        scratch_shapes=[
            pltpu.VMEM((SHARDS, BLOCK, COLS), BF),
            pltpu.VMEM((SHARDS, BLOCK, COLS), BF),
            pltpu.VMEM((SHARDS, BLOCK, COLS), BF),
            pltpu.VMEM((SHARDS, BLOCK, COLS), BF),
            pltpu.VMEM((2, 32, HD), BF),
            pltpu.VMEM((2, SEQ, HD), BF),
            pltpu.VMEM((2, SHARDS, HD, ROWS), BF),
            pltpu.SMEM((SHARDS, SHARDS), jnp.int32),
            pltpu.SemaphoreType.DMA((4, 8)),
            pltpu.SemaphoreType.DMA((4, 8)),
            pltpu.SemaphoreType.DMA((2, 16)),
            pltpu.SemaphoreType.DMA((2, 16)),
            pltpu.SemaphoreType.DMA((2, 24)),
            pltpu.SemaphoreType.DMA((2, 8)),
            pltpu.SemaphoreType.DMA((2, 8)),
            pltpu.SemaphoreType.DMA((2, 8)),
            pltpu.SemaphoreType.DMA((7,)),
        ],
        compiler_params=pltpu.CompilerParams(collective_id=0, has_side_effects=True),
    )(route, q, k, v, g)


def attention_kernel(
    route_hbm, docs_hbm, q_hbm, g_hbm, k_hbm, v_hbm, kt_hbm, vt_hbm, att_hbm, dq_hbm, dkv_hbm,
    q, g, k, v, att, dq, dkv,
    s_buf, dp_buf, kt, vt, dk_acc, dv_acc, ot_acc, dqt_acc, route, docs, starts, load, store,
):
    tables = (
        pltpu.make_async_copy(route_hbm, route, store.at[0]),
        pltpu.make_async_copy(docs_hbm, docs, store.at[1]),
    )
    for copy in tables:
        copy.start()
    pairs = ((k_hbm, k), (q_hbm, q), (v_hbm, v), (g_hbm, g), (vt_hbm, vt), (kt_hbm, kt))

    def incoming(n):
        rows = pl.ds(n * SPAN, SPAN)
        return [
            pltpu.make_async_copy(src.at[rows], dst.at[rows], load.at[n, i])
            for i, (src, dst) in enumerate(pairs)
        ]

    for n in range(SHARDS // SPAN):
        for copy in incoming(n):
            copy.start()
    for copy in tables:
        copy.wait()
    c = lax.axis_index("ctx")
    ends = []
    total = jnp.int32(0)
    for j in range(DOCS):
        total = total + docs[j]
        ends.append(total)

    def find(s, carry):
        block = jnp.int32(0)
        for b in range(SHARDS):
            block = jnp.where(route[s, b] == c, b, block)
        starts[s] = s * ROWS + block * BLOCK
        return carry

    lax.fori_loop(0, SHARDS, find, 0)
    def stack(ref, first):
        parts = []
        for i in range(SPAN):
            rows = ref[first + i]
            parts += [rows[:, n * HD:(n + 1) * HD] for n in range(GROUP)]
        return jnp.concatenate(parts, axis=0)

    def outgoing(n):
        rows = pl.ds(n * SPAN, SPAN)
        return (
            pltpu.make_async_copy(att.at[rows], att_hbm.at[rows], store.at[0]),
            pltpu.make_async_copy(dq.at[rows], dq_hbm.at[rows], store.at[1]),
        )

    within = lax.rem(lax.broadcasted_iota(jnp.int32, (1, WIDTH), 1), BLOCK)
    key = lax.broadcasted_iota(jnp.int32, (ROWS, WIDTH), 0)

    def group(n, carry):
        first = n * SPAN
        for copy in incoming(n):
            copy.wait()
        qg = stack(q, first)
        gg = stack(g, first)
        qt = qg.T
        gt = gg.T
        q_pos = jnp.concatenate([within + starts[first + i] for i in range(SPAN)], axis=1)
        q_doc = jnp.zeros_like(q_pos)
        marks = [starts[first], starts[first + 1], starts[first + 2]]
        lows = [jnp.int32(0)] * 3
        for end in ends:
            q_doc = jnp.where(q_pos >= end, end, q_doc)
            lows = [jnp.where(mark >= end, end, low) for mark, low in zip(marks, lows)]
        t_one, t_two, t_low = [jnp.minimum(low // ROWS, first) for low in lows]
        spans = ((t_one, t_two, WIDTH), (t_two, t_low, 2 * WIDTH), (t_low, first, LANES))
        reach = (q_pos - q_doc).astype(jnp.uint32)

        def scores(t, lane, stop=LANES):
            s = jnp.dot(k[t], qt[:, lane:stop], preferred_element_type=F32)
            return s * (SCALE * LOG2E)

        def slopes(t, lane, stop=LANES):
            return jnp.dot(v[t], gt[:, lane:stop], preferred_element_type=F32)

        def masked(t, lane, stop=LANES):
            s = scores(t, lane, stop)
            offset = t * ROWS - q_doc[:, lane:stop]
            parts = []
            for i in range(0, stop - lane, WIDTH):
                past = (key + offset[:, i:i + WIDTH]).astype(jnp.uint32)
                seen = past <= reach[:, lane + i:lane + i + WIDTH]
                parts.append(jnp.where(seen, s[:, i:i + WIDTH], NEGATIVE))
            return jnp.concatenate(parts, axis=1)

        ot_acc[...] = jnp.zeros_like(ot_acc)
        dqt_acc[...] = jnp.zeros_like(dqt_acc)

        def forward(base, width, stop):
            def step(n, carried):
                peak, mass = carried
                tiles = [base + n * width + i for i in range(width)]
                new_peak = peak[:, :stop]
                for t in tiles:
                    s = masked(t, 0, stop)
                    s_buf[t, :, :stop] = s
                    if stop < LANES or width == 2:
                        dp_buf[t, :, :stop] = slopes(t, 0, stop)
                    new_peak = jnp.maximum(new_peak, jnp.max(s, axis=0, keepdims=True))
                fade = jnp.exp2(peak[:, :stop] - new_peak)
                new_mass = mass[:, :stop] * fade
                total = ot_acc[:, :stop] * fade
                for t in tiles:
                    p = jnp.exp2(s_buf[t, :, :stop] - new_peak)
                    new_mass = new_mass + jnp.sum(p, axis=0, keepdims=True)
                    total = total + jnp.dot(vt[t], p.astype(BF), preferred_element_type=F32)
                ot_acc[:, :stop] = total
                if stop < LANES:
                    new_peak = jnp.concatenate([new_peak, peak[:, stop:]], axis=1)
                    new_mass = jnp.concatenate([new_mass, mass[:, stop:]], axis=1)
                return new_peak, new_mass

            return step

        state = (jnp.full((1, LANES), FLOOR, F32), jnp.zeros((1, LANES), F32))
        for start, stop, lanes in spans:
            odd = lax.rem(stop - start, 2)
            state = lax.fori_loop(0, odd, forward(start, 1, lanes), state)
            state = lax.fori_loop(0, (stop - start) // 2, forward(start + odd, 2, lanes), state)
        peak, mass = state

        tops = [[peak[:, i * WIDTH:(i + 1) * WIDTH]] for i in range(SPAN)]
        for e in range(SPAN):
            s = masked(first + e, e * WIDTH)
            s_buf[first + e, :, e * WIDTH:] = s
            dp_buf[first + e, :, e * WIDTH:] = slopes(first + e, e * WIDTH)
            top = jnp.max(s, axis=0, keepdims=True)
            for i in range(e, SPAN):
                tops[i].append(top[:, (i - e) * WIDTH:(i - e + 1) * WIDTH])
        new_peak = jnp.concatenate([functools.reduce(jnp.maximum, t) for t in tops], axis=1)
        fade = jnp.exp2(peak - new_peak)
        mass = mass * fade
        masses = [[mass[:, i * WIDTH:(i + 1) * WIDTH]] for i in range(SPAN)]
        ot_acc[...] = ot_acc[...] * fade
        for e in range(SPAN):
            p = jnp.exp2(s_buf[first + e, :, e * WIDTH:] - new_peak[:, e * WIDTH:])
            add = jnp.sum(p, axis=0, keepdims=True)
            for i in range(e, SPAN):
                masses[i].append(add[:, (i - e) * WIDTH:(i - e + 1) * WIDTH])
            ot_acc[:, e * WIDTH:] += jnp.dot(
                vt[first + e], p.astype(BF), preferred_element_type=F32)
        mass = jnp.concatenate([functools.reduce(jnp.add, t) for t in masses], axis=1)
        lse = new_peak + jnp.log2(mass)
        ot = (ot_acc[...] * (1.0 / mass)).astype(BF)
        delta = jnp.sum(gt.astype(F32) * ot.astype(F32), axis=0, keepdims=True)
        o = ot.T
        for i in range(SPAN):
            for m in range(GROUP):
                r = (i * GROUP + m) * BLOCK
                att[first + i, :, m * HD:(m + 1) * HD] = o[r:r + BLOCK]

        def pull(t, lane, stop=LANES, held=True):
            p = jnp.exp2(s_buf[t, :, lane:stop] - lse[:, lane:stop])
            dp = dp_buf[t, :, lane:stop] if held else slopes(t, lane, stop)
            ds = (p * (dp - delta[:, lane:stop])).astype(BF)
            grad_v = jnp.dot(p.astype(BF), gg[lane:stop], preferred_element_type=F32)
            grad_k = jnp.dot(ds, qg[lane:stop], preferred_element_type=F32)
            dqt_acc[:, lane:stop] += jnp.dot(kt[t], ds, preferred_element_type=F32)
            return grad_v, grad_k

        for e in range(SPAN):
            grad_v, grad_k = pull(first + e, e * WIDTH)
            dv_acc[first + e] = grad_v
            dk_acc[first + e] = grad_k

        def backward(base, width, stop):
            def step(n, carried):
                for i in range(width):
                    t = base + n * width + i
                    grad_v, grad_k = pull(t, 0, stop, stop < LANES or width == 2)
                    dv_acc[t] += grad_v
                    dk_acc[t] += grad_k
                return carried

            return step

        for start, stop, lanes in spans:
            odd = lax.rem(stop - start, 2) if lanes == LANES else stop - start
            lax.fori_loop(0, odd, backward(start, 1, lanes), 0)
            if lanes == LANES:
                lax.fori_loop(0, (stop - start) // 2, backward(start + odd, 2, lanes), 0)
        grad = dqt_acc[...].T * SCALE
        for i in range(SPAN):
            for m in range(GROUP):
                r = (i * GROUP + m) * BLOCK
                dq[first + i, :, m * HD:(m + 1) * HD] = grad[r:r + BLOCK]
        for copy in outgoing(n):
            copy.start()
        return carry

    lax.fori_loop(0, SHARDS // SPAN, group, 0)

    def outbound(n):
        cols = pl.ds(n * SPAN, SPAN)
        return pltpu.make_async_copy(dkv.at[:, cols], dkv_hbm.at[:, cols], load.at[n, 0])

    def regroup(s, carry):
        for b in range(SHARDS):
            rows = slice(b * BLOCK, (b + 1) * BLOCK)
            dkv[route[s, b], s] = jnp.stack(
                [(dk_acc[s, rows] * SCALE).astype(BF), dv_acc[s, rows].astype(BF)])
        return carry

    for n in range(SHARDS // SPAN):
        lax.fori_loop(n * SPAN, (n + 1) * SPAN, regroup, 0)
        outbound(n).start()
    pltpu.make_async_copy(att, att_hbm, store.at[0]).wait()
    pltpu.make_async_copy(dq, dq_hbm, store.at[1]).wait()
    for n in range(SHARDS // SPAN):
        outbound(n).wait()


def attention(route, docs, q, g, k, v, kt, vt):
    return pl.pallas_call(
        attention_kernel,
        name="attention",
        out_shape=(
            jax.ShapeDtypeStruct((SHARDS, BLOCK, COLS), BF),
            jax.ShapeDtypeStruct((SHARDS, BLOCK, COLS), F32),
            jax.ShapeDtypeStruct((SHARDS, SHARDS, 2, BLOCK, HD), BF),
        ),
        in_specs=[ANY] * 8,
        out_specs=(ANY, ANY, ANY),
        scratch_shapes=[
            pltpu.VMEM((SHARDS, BLOCK, COLS), BF),
            pltpu.VMEM((SHARDS, BLOCK, COLS), BF),
            pltpu.VMEM((SHARDS, ROWS, HD), BF),
            pltpu.VMEM((SHARDS, ROWS, HD), BF),
            pltpu.VMEM((SHARDS, BLOCK, COLS), BF),
            pltpu.VMEM((SHARDS, BLOCK, COLS), F32),
            pltpu.VMEM((SHARDS, SHARDS, 2, BLOCK, HD), BF),
            pltpu.VMEM((SHARDS, ROWS, LANES), F32),
            pltpu.VMEM((SHARDS, ROWS, LANES), F32),
            pltpu.VMEM((SHARDS, HD, ROWS), BF),
            pltpu.VMEM((SHARDS, HD, ROWS), BF),
            pltpu.VMEM((SHARDS, ROWS, HD), F32),
            pltpu.VMEM((SHARDS, ROWS, HD), F32),
            pltpu.VMEM((HD, LANES), F32),
            pltpu.VMEM((HD, LANES), F32),
            pltpu.SMEM((SHARDS, SHARDS), jnp.int32),
            pltpu.SMEM((DOCS,), jnp.int32),
            pltpu.SMEM((SHARDS,), jnp.int32),
            pltpu.SemaphoreType.DMA((SHARDS // SPAN, 6)),
            pltpu.SemaphoreType.DMA((2,)),
        ],
    )(route, docs, q, g, k, v, kt, vt)


def reduce_kernel(
    part, chip, keep, mine, mate, ready, hold, kept, from_y, from_x,
    s1, r1, sy, ry, sx, rx, s2, r2, local,
):
    c = lax.axis_index("ctx")
    h = lax.axis_index("head")
    x, yl, core = c // 4, lax.rem(c // 2, 2), lax.rem(c, 2)
    other = ctx_of(x, yl, core + 1)
    across = ctx_of(x, yl + 1, core)
    far = (2, 1, 3, 0)
    order = [(dx, dy) for dy in (1, 0) for dx in far]

    def along(dx):
        return ctx_of(x + dx, yl, core)

    def place(dx, dy):
        return lax.rem(x + dx, 4) * 2 + lax.rem(yl + dy, 2)

    loads = []
    for i, (dx, dy) in enumerate(order):
        t = place(dx, dy)
        copy = pltpu.make_async_copy(part.at[t * 2 + core], mine.at[t], local.at[i])
        copy.start()
        loads.append(copy)

    barrier = pltpu.get_barrier_semaphore()
    for peer in (other, across, along(1), along(2), along(3)):
        pl.semaphore_signal(barrier, inc=1, device_id=(peer, h), device_id_type=MESH)
    pl.semaphore_wait(barrier, 5)

    sent = []

    def start(*args):
        copy = remote(*args, h)
        copy.start()
        sent.append(copy)
        return copy

    pairs = []
    for i, (dx, dy) in enumerate(order):
        t = place(dx, dy)
        pairs.append(start(part.at[t * 2 + 1 - core], mate.at[t], s1.at[i], r1.at[i], other))

    for (dx, dy), pair, load in zip(order, pairs, loads):
        t = place(dx, dy)
        load.wait()
        pair.wait_recv()
        sums = [mine[t, :, a].astype(F32) + mate[t, :, a].astype(F32) for a in range(2)]
        if dy == 1:
            ready[t, 0] = sums[0].astype(BF)
            start(ready.at[t, 0], from_y.at[dx], sy.at[dx], ry.at[dx], across)
        else:
            hold[dx] = sums[0]
        if dx == 0:
            kept[1 - dy] = sums[1]
        else:
            ready[t, 1] = sums[1].astype(BF)
            start(ready.at[t, 1], from_x.at[dx - 1, dy], sx.at[dx - 1, dy], rx.at[dx - 1, dy],
                  along(dx))

    for dx in far:
        remote(from_y.at[dx], from_y.at[dx], sy.at[dx], ry.at[dx], across, h).wait_recv()
        hold[dx] += from_y[dx].astype(F32)
        if dx:
            t = place(dx, 0)
            ready[t, 0] = hold[dx].astype(BF)
            start(ready.at[t, 0], chip.at[dx - 1], s2.at[dx], r2.at[dx], along(dx))
    for dy in (1, 0):
        for dx in (1, 3, 2):
            part_in = from_x.at[dx - 1, dy]
            remote(part_in, part_in, sx.at[dx - 1, dy], rx.at[dx - 1, dy], across, h).wait_recv()
            kept[1 - dy] += from_x[dx - 1, dy].astype(F32)
        if dy:
            t = place(0, 1)
            ready[t, 1] = kept[0].astype(BF)
            start(ready.at[t, 1], chip.at[3], s2.at[0], r2.at[0], across)
    outs = [
        pltpu.make_async_copy(hold.at[0], keep.at[0], local.at[0]),
        pltpu.make_async_copy(kept.at[1], keep.at[1], local.at[1]),
    ]
    for out in outs:
        out.start()
    for j in range(4):
        slot = chip.at[(j + 3) % 4]
        remote(slot, slot, s2.at[j], r2.at[j], across, h).wait_recv()
    for copy in sent:
        copy.wait_send()
    for out in outs:
        out.wait()


def reduce(part):
    shape = (SHARDS, BLOCK, HD)
    return pl.pallas_call(
        reduce_kernel,
        name="reduce",
        out_shape=(
            jax.ShapeDtypeStruct((4,) + shape, BF),
            jax.ShapeDtypeStruct((2,) + shape, F32),
        ),
        in_specs=[ANY],
        out_specs=(ANY, ANY),
        scratch_shapes=[
            pltpu.VMEM((8, SHARDS, 2, BLOCK, HD), BF),
            pltpu.VMEM((8, SHARDS, 2, BLOCK, HD), BF),
            pltpu.VMEM((8, 2) + shape, BF),
            pltpu.VMEM((4,) + shape, F32),
            pltpu.VMEM((2,) + shape, F32),
            pltpu.VMEM((4,) + shape, BF),
            pltpu.VMEM((3, 2) + shape, BF),
            pltpu.SemaphoreType.DMA((8,)),
            pltpu.SemaphoreType.DMA((8,)),
            pltpu.SemaphoreType.DMA((4,)),
            pltpu.SemaphoreType.DMA((4,)),
            pltpu.SemaphoreType.DMA((3, 2)),
            pltpu.SemaphoreType.DMA((3, 2)),
            pltpu.SemaphoreType.DMA((4,)),
            pltpu.SemaphoreType.DMA((4,)),
            pltpu.SemaphoreType.DMA((8,)),
        ],
        compiler_params=pltpu.CompilerParams(collective_id=1, has_side_effects=True),
    )(part)


def finish_kernel(chip_hbm, keep_hbm, dk_hbm, dv_hbm, chip, keep, load, store):
    parts = (pl.ds(0, 3), pl.ds(3, 1))
    loads = []
    for a in range(2):
        loads.append((
            pltpu.make_async_copy(chip_hbm.at[parts[a]], chip.at[parts[a]], load.at[a, 0]),
            pltpu.make_async_copy(keep_hbm.at[a], keep.at[a], load.at[a, 1]),
        ))
        for copy in loads[a]:
            copy.start()
    outs = []
    for a, out in enumerate((dk_hbm, dv_hbm)):
        for copy in loads[a]:
            copy.wait()
        total = keep[a]
        for j in ((0, 1, 2), (3,))[a]:
            total = total + chip[j].astype(F32)
        keep[a] = total
        outs.append(pltpu.make_async_copy(keep.at[a], out, store.at[a]))
        outs[a].start()
    for copy in outs:
        copy.wait()


def finish(chip, keep):
    out = jax.ShapeDtypeStruct((SHARDS, BLOCK, HD), F32)
    return pl.pallas_call(
        finish_kernel,
        name="finish",
        out_shape=(out, out),
        in_specs=[ANY, ANY],
        out_specs=(ANY, ANY),
        scratch_shapes=[
            pltpu.VMEM(chip.shape, BF),
            pltpu.VMEM(keep.shape, F32),
            pltpu.SemaphoreType.DMA((2, 2)),
            pltpu.SemaphoreType.DMA((2,)),
        ],
    )(chip, keep)


def on_device(queries, key_rows, value_rows, cotangent, doc_lengths, block_route):
    q, g, k, v, kt, vt = exchange(
        block_route,
        queries.reshape(2, BLOCK, HEADS * COLS),
        key_rows,
        value_rows,
        cotangent.reshape(2, BLOCK, HEADS * COLS),
    )
    att, dq, part = attention(
        block_route, doc_lengths, q, g, k.reshape(SHARDS, ROWS, HD), v.reshape(SHARDS, ROWS, HD), kt, vt)
    dk, dv = finish(*reduce(part))
    return (
        att.reshape(ROWS, COLS),
        dq.reshape(ROWS, COLS),
        dk.reshape(ROWS, HD),
        dv.reshape(ROWS, HD),
    )


def solution(mesh):
    placed = P(("ctx", "head"), None)
    return jax.shard_map(
        on_device,
        mesh=mesh,
        in_specs=(placed, placed, placed, placed, P(), P()),
        out_specs=(P("ctx", "head"),) * 4,
        check_vma=False,
    )
```

```python
import functools
import math

import jax
import jax.numpy as jnp
from jax import lax
from jax.experimental import pallas as pl
from jax.experimental.pallas import tpu as pltpu
from jax.sharding import PartitionSpec as P

HD = 128
GROUP = 8
SHARDS = 16
BLOCK = 16
ROWS = SHARDS * BLOCK
SEQ = SHARDS * ROWS
DOCS = 8
HEADS = 8
COLS = GROUP * HD

SPAN = 4
WIDTH = GROUP * BLOCK
LANES = SPAN * WIDTH
NEGATIVE = -1e30
FLOOR = -0.5e30
SCALE = 1.0 / math.sqrt(HD)
LOG2E = 1.4426950408889634

BF = jnp.bfloat16
F32 = jnp.float32
MESH = pl.DeviceIdType.MESH
ANY = pl.BlockSpec(memory_space=pl.ANY)
VMEM = pl.BlockSpec(memory_space=pltpu.VMEM)
SMEM = pl.BlockSpec(memory_space=pltpu.SMEM)


def ctx_of(x, y, core):
    return (lax.rem(x, 4) * 2 + lax.rem(y, 2)) * 2 + lax.rem(core, 2)


def head_of(z, y):
    return lax.rem(z, 4) * 2 + lax.rem(y, 2)


def remote(src, dst, send, recv, ctx, head):
    return pltpu.make_async_remote_copy(
        src_ref=src,
        dst_ref=dst,
        send_sem=send,
        recv_sem=recv,
        device_id=(ctx, head),
        device_id_type=MESH,
    )


def exchange_kernel(
    route_hbm, q, k, v, g, qo, go, ko, vo, kto, vto,
    xq, xg, sq, sg, own_kv, all_kv, turned, route,
    p1s, p1r, p2s, p2r, rs, rr, cs, cr, local,
):
    c = lax.axis_index("ctx")
    h = lax.axis_index("head")
    z, yh = h // 2, lax.rem(h, 2)
    x, yl, core = c // 4, lax.rem(c // 2, 2), lax.rem(c, 2)
    head_peers = [(jz, jy) for jz in range(4) for jy in range(2) if (jz, jy) != (0, 0)]
    ctx_peers = [
        (jx, jy, jc) for jx in range(4) for jy in range(2) for jc in range(2)
        if (jx, jy, jc) != (0, 0, 0)
    ]

    table = pltpu.make_async_copy(route_hbm, route, local.at[6])
    table.start()
    own_cols = pl.ds(pl.multiple_of(h * HD, HD), HD)
    staged = [
        pltpu.make_async_copy(src.at[:, own_cols], own_kv.at[a], local.at[a])
        for a, src in enumerate((k, v))
    ]
    for copy in staged:
        copy.start()

    barrier = pltpu.get_barrier_semaphore()
    for jz, jy in head_peers:
        pl.semaphore_signal(
            barrier, inc=1, device_id=(c, head_of(z + jz, yh + jy)), device_id_type=MESH
        )
    for jx, jy, jc in ctx_peers:
        pl.semaphore_signal(
            barrier, inc=1, device_id=(ctx_of(x + jx, yl + jy, core + jc), h), device_id_type=MESH
        )
    pl.semaphore_wait(barrier, len(head_peers) + len(ctx_peers))

    sent = []

    def go_remote(copy):
        copy.start()
        sent.append(copy)
        return copy

    kv_rows = pl.ds(c * ROWS + h * 32, 32)
    p1 = [[], [], [], []]
    for jz, jy in head_peers:
        j = jz * 2 + jy
        peer = head_of(z + jz, yh + jy)
        cols = pl.ds(pl.multiple_of(peer * HD, HD), HD)
        for a, (src, dst) in enumerate(((k, ko), (v, vo))):
            p1[a].append(go_remote(remote(
                src.at[:, cols], dst.at[kv_rows], p1s.at[a, j], p1r.at[a, j], c, peer)))
    own = [
        pltpu.make_async_copy(own_kv.at[a], dst.at[kv_rows], local.at[a])
        for a, dst in enumerate((ko, vo))
    ]

    def first(a, src, dst):
        for jz, jy in head_peers:
            j = jz * 2 + jy
            peer = head_of(z + jz, yh + jy)
            cols = pl.ds(pl.multiple_of(peer * COLS, COLS), COLS)
            p1[2 + a].append(go_remote(remote(
                src.at[:, :, cols], dst.at[pl.ds(h * 2, 2)],
                p1s.at[2 + a, j], p1r.at[2 + a, j], c, peer)))
        cols = pl.ds(pl.multiple_of(h * COLS, COLS), COLS)
        own.append(pltpu.make_async_copy(
            src.at[:, :, cols], dst.at[pl.ds(h * 2, 2)], local.at[2 + a]))
        own[-1].start()

    first(0, q, xq)
    for a in range(2):
        staged[a].wait()
        own[a].start()

    kv = (ko, vo)

    def shard(a, dx, dy):
        return kv[a].at[pl.ds(ctx_of(x + dx, yl + dy, core) * ROWS, ROWS)]

    def ring(a, dx, dy, tx, ty):
        slot = ((dx - tx) % 4) * 2 + (dy - ty) % 2
        part = shard(a, dx, dy)
        return remote(part, part, rs.at[a, slot], rr.at[a, slot],
                      ctx_of(x + tx + 4, yl + ty + 2, core), h)

    def partner(a, dx, dy):
        slot = dx * 2 + dy
        part = shard(a, dx, dy)
        return remote(part, part, cs.at[a, slot], cr.at[a, slot], ctx_of(x, yl, core + 1), h)

    def arrived(a, dx, dy):
        slot = dx * 2 + dy
        part = shard(a, dx, dy)
        remote(part, part, rs.at[a, slot], rr.at[a, slot], c, h).wait_recv()

    for a in range(2):
        own[a].wait()
        for copy in p1[a]:
            copy.wait_recv()
    for a in range(2):
        go_remote(ring(a, 0, 0, 0, 1))
        go_remote(ring(a, 0, 0, 1, 0))
        go_remote(ring(a, 0, 0, -1, 0))
    first(1, g, xg)
    for a in range(2):
        go_remote(partner(a, 0, 0))

    table.wait()

    def second(a, stage, send, out):
        own[2 + a].wait()
        for copy in p1[2 + a]:
            copy.wait_recv()

        def pick(d, carry):
            block = jnp.int32(0)
            for b in range(SHARDS):
                block = jnp.where(route[c, b] == d, b, block)
            send[d] = stage[block]
            return carry

        lax.fori_loop(0, SHARDS, pick, 0)
        mine = pltpu.make_async_copy(send.at[c], out.at[c], local.at[4 + a])
        mine.start()
        copies = []
        for jx, jy, jc in ctx_peers:
            j = (jx * 2 + jy) * 2 + jc
            d = ctx_of(x + jx, yl + jy, core + jc)
            copies.append(go_remote(remote(
                send.at[d], out.at[c], p2s.at[a, j], p2r.at[a, j], d, h)))
        return mine, copies

    def sides(dy):
        arrived(0, 3, dy)
        go_remote(ring(0, 3, dy, 1, 0))
        arrived(1, 1, dy)
        go_remote(ring(1, 1, dy, -1, 0))
        arrived(0, 1, dy)
        arrived(1, 3, dy)
        for a in range(2):
            go_remote(partner(a, 3, dy))
            go_remote(partner(a, 1, dy))

    sides(0)
    for a in range(2):
        arrived(a, 0, 1)
        go_remote(ring(a, 0, 1, 1, 0))
        go_remote(ring(a, 0, 1, -1, 0))
        go_remote(partner(a, 0, 1))
    mine_q, p2q = second(0, xq, sq, qo)
    sides(1)
    for a in range(2):
        arrived(a, 2, 0)
        go_remote(partner(a, 2, 0))
    mine_g, p2g = second(1, xg, sg, go)
    for a in range(2):
        arrived(a, 2, 1)
        go_remote(partner(a, 2, 1))
    for a in range(2):
        for dx in range(4):
            for dy in range(2):
                slot = dx * 2 + dy
                part = kv[a].at[pl.ds(ctx_of(x + dx, yl + dy, core + 1) * ROWS, ROWS)]
                remote(part, part, cs.at[a, slot], cr.at[a, slot], c, h).wait_recv()
    fetch = [pltpu.make_async_copy(kv[a], all_kv.at[a], local.at[a]) for a in range(2)]
    for copy in fetch:
        copy.start()
    turns = []
    for a, out in enumerate((kto, vto)):
        fetch[a].wait()

        def turn(i, carry):
            for e in range(4):
                t = i * 4 + e
                turned[a, t] = all_kv[a, pl.ds(pl.multiple_of(t * ROWS, ROWS), ROWS), :].T
            return carry

        lax.fori_loop(0, SHARDS // 4, turn, 0)
        turns.append(pltpu.make_async_copy(turned.at[a], out, local.at[2 + a]))
        turns[-1].start()
    mine_q.wait()
    mine_g.wait()

    def received(a, out):
        for jx, jy, jc in ctx_peers:
            j = (jx * 2 + jy) * 2 + jc
            src = ctx_of(x - jx + 4, yl - jy + 2, core - jc + 2)
            remote(out.at[src], out.at[src], p2s.at[a, j], p2r.at[a, j], c, h).wait_recv()

    received(0, qo)
    for copy in turns:
        copy.wait()
    received(1, go)
    for copy in sent:
        copy.wait_send()


def exchange(route, q, k, v, g):
    return pl.pallas_call(
        exchange_kernel,
        name="exchange",
        out_shape=(
            jax.ShapeDtypeStruct((SHARDS, BLOCK, COLS), BF),
            jax.ShapeDtypeStruct((SHARDS, BLOCK, COLS), BF),
            jax.ShapeDtypeStruct((SEQ, HD), BF),
            jax.ShapeDtypeStruct((SEQ, HD), BF),
            jax.ShapeDtypeStruct((SHARDS, HD, ROWS), BF),
            jax.ShapeDtypeStruct((SHARDS, HD, ROWS), BF),
        ),
        in_specs=[ANY, ANY, ANY, ANY, ANY],
        out_specs=(ANY,) * 6,
        scratch_shapes=[
            pltpu.VMEM((SHARDS, BLOCK, COLS), BF),
            pltpu.VMEM((SHARDS, BLOCK, COLS), BF),
            pltpu.VMEM((SHARDS, BLOCK, COLS), BF),
            pltpu.VMEM((SHARDS, BLOCK, COLS), BF),
            pltpu.VMEM((2, 32, HD), BF),
            pltpu.VMEM((2, SEQ, HD), BF),
            pltpu.VMEM((2, SHARDS, HD, ROWS), BF),
            pltpu.SMEM((SHARDS, SHARDS), jnp.int32),
            pltpu.SemaphoreType.DMA((4, 8)),
            pltpu.SemaphoreType.DMA((4, 8)),
            pltpu.SemaphoreType.DMA((2, 16)),
            pltpu.SemaphoreType.DMA((2, 16)),
            pltpu.SemaphoreType.DMA((2, 24)),
            pltpu.SemaphoreType.DMA((2, 8)),
            pltpu.SemaphoreType.DMA((2, 8)),
            pltpu.SemaphoreType.DMA((2, 8)),
            pltpu.SemaphoreType.DMA((7,)),
        ],
        compiler_params=pltpu.CompilerParams(collective_id=0, has_side_effects=True),
    )(route, q, k, v, g)


def attention_kernel(
    route_hbm, docs_hbm, q_hbm, g_hbm, k_hbm, v_hbm, kt_hbm, vt_hbm, att_hbm, dq_hbm, dkv_hbm,
    q, g, k, v, att, dq, dkv,
    s_buf, dp_buf, kt, vt, dk_acc, dv_acc, ot_acc, dqt_acc, route, docs, starts, load, store,
):
    tables = (
        pltpu.make_async_copy(route_hbm, route, store.at[0]),
        pltpu.make_async_copy(docs_hbm, docs, store.at[1]),
    )
    for copy in tables:
        copy.start()
    pairs = ((k_hbm, k), (q_hbm, q), (v_hbm, v), (g_hbm, g), (vt_hbm, vt), (kt_hbm, kt))

    def incoming(n):
        rows = pl.ds(n * SPAN, SPAN)
        return [
            pltpu.make_async_copy(src.at[rows], dst.at[rows], load.at[n, i])
            for i, (src, dst) in enumerate(pairs)
        ]

    for n in range(SHARDS // SPAN):
        for copy in incoming(n):
            copy.start()
    for copy in tables:
        copy.wait()
    c = lax.axis_index("ctx")
    ends = []
    total = jnp.int32(0)
    for j in range(DOCS):
        total = total + docs[j]
        ends.append(total)

    def find(s, carry):
        block = jnp.int32(0)
        for b in range(SHARDS):
            block = jnp.where(route[s, b] == c, b, block)
        starts[s] = s * ROWS + block * BLOCK
        return carry

    lax.fori_loop(0, SHARDS, find, 0)
    def stack(ref, first):
        parts = []
        for i in range(SPAN):
            rows = ref[first + i]
            parts += [rows[:, n * HD:(n + 1) * HD] for n in range(GROUP)]
        return jnp.concatenate(parts, axis=0)

    def outgoing(n):
        rows = pl.ds(n * SPAN, SPAN)
        return (
            pltpu.make_async_copy(att.at[rows], att_hbm.at[rows], store.at[0]),
            pltpu.make_async_copy(dq.at[rows], dq_hbm.at[rows], store.at[1]),
        )

    within = lax.rem(lax.broadcasted_iota(jnp.int32, (1, WIDTH), 1), BLOCK)
    key = lax.broadcasted_iota(jnp.int32, (ROWS, WIDTH), 0)

    def group(n, carry):
        first = n * SPAN
        for copy in incoming(n)[:4]:
            copy.wait()
        qg = stack(q, first)
        gg = stack(g, first)
        qt = qg.T
        gt = gg.T
        q_pos = jnp.concatenate([within + starts[first + i] for i in range(SPAN)], axis=1)
        q_doc = jnp.zeros_like(q_pos)
        marks = [starts[first], starts[first + 1], starts[first + 2]]
        lows = [jnp.int32(0)] * 3
        for end in ends:
            q_doc = jnp.where(q_pos >= end, end, q_doc)
            lows = [jnp.where(mark >= end, end, low) for mark, low in zip(marks, lows)]
        t_one, t_two, t_low = [jnp.minimum(low // ROWS, first) for low in lows]
        spans = ((t_one, t_two, WIDTH), (t_two, t_low, 2 * WIDTH), (t_low, first, LANES))
        reach = (q_pos - q_doc).astype(jnp.uint32)

        def scores(t, lane, stop=LANES):
            s = jnp.dot(k[t], qt[:, lane:stop], preferred_element_type=F32)
            return s * (SCALE * LOG2E)

        def slopes(t, lane, stop=LANES):
            return jnp.dot(v[t], gt[:, lane:stop], preferred_element_type=F32)

        def masked(t, lane, stop=LANES):
            s = scores(t, lane, stop)
            offset = t * ROWS - q_doc[:, lane:stop]
            parts = []
            for i in range(0, stop - lane, WIDTH):
                past = (key + offset[:, i:i + WIDTH]).astype(jnp.uint32)
                seen = past <= reach[:, lane + i:lane + i + WIDTH]
                parts.append(jnp.where(seen, s[:, i:i + WIDTH], NEGATIVE))
            return jnp.concatenate(parts, axis=1)

        ot_acc[...] = jnp.zeros_like(ot_acc)
        dqt_acc[...] = jnp.zeros_like(dqt_acc)

        def forward(base, width, stop):
            def step(n, carried):
                peak, mass = carried
                tiles = [base + n * width + i for i in range(width)]
                new_peak = peak[:, :stop]
                for t in tiles:
                    s = masked(t, 0, stop)
                    s_buf[t, :, :stop] = s
                    if stop < LANES or width == 2:
                        dp_buf[t, :, :stop] = slopes(t, 0, stop)
                    new_peak = jnp.maximum(new_peak, jnp.max(s, axis=0, keepdims=True))
                fade = jnp.exp2(peak[:, :stop] - new_peak)
                new_mass = mass[:, :stop] * fade
                total = ot_acc[:, :stop] * fade
                for t in tiles:
                    p = jnp.exp2(s_buf[t, :, :stop] - new_peak)
                    new_mass = new_mass + jnp.sum(p, axis=0, keepdims=True)
                    total = total + jnp.dot(vt[t], p.astype(BF), preferred_element_type=F32)
                ot_acc[:, :stop] = total
                if stop < LANES:
                    new_peak = jnp.concatenate([new_peak, peak[:, stop:]], axis=1)
                    new_mass = jnp.concatenate([new_mass, mass[:, stop:]], axis=1)
                return new_peak, new_mass

            return step

        state = (jnp.full((1, LANES), FLOOR, F32), jnp.zeros((1, LANES), F32))
        for start, stop, lanes in spans:
            odd = lax.rem(stop - start, 2)
            state = lax.fori_loop(0, odd, forward(start, 1, lanes), state)
            state = lax.fori_loop(0, (stop - start) // 2, forward(start + odd, 2, lanes), state)
        peak, mass = state

        for copy in incoming(n)[4:]:
            copy.wait()
        tops = [[peak[:, i * WIDTH:(i + 1) * WIDTH]] for i in range(SPAN)]
        for e in range(SPAN):
            s = masked(first + e, e * WIDTH)
            s_buf[first + e, :, e * WIDTH:] = s
            dp_buf[first + e, :, e * WIDTH:] = slopes(first + e, e * WIDTH)
            top = jnp.max(s, axis=0, keepdims=True)
            for i in range(e, SPAN):
                tops[i].append(top[:, (i - e) * WIDTH:(i - e + 1) * WIDTH])
        new_peak = jnp.concatenate([functools.reduce(jnp.maximum, t) for t in tops], axis=1)
        fade = jnp.exp2(peak - new_peak)
        mass = mass * fade
        masses = [[mass[:, i * WIDTH:(i + 1) * WIDTH]] for i in range(SPAN)]
        ot_acc[...] = ot_acc[...] * fade
        for e in range(SPAN):
            p = jnp.exp2(s_buf[first + e, :, e * WIDTH:] - new_peak[:, e * WIDTH:])
            add = jnp.sum(p, axis=0, keepdims=True)
            for i in range(e, SPAN):
                masses[i].append(add[:, (i - e) * WIDTH:(i - e + 1) * WIDTH])
            ot_acc[:, e * WIDTH:] += jnp.dot(
                vt[first + e], p.astype(BF), preferred_element_type=F32)
        mass = jnp.concatenate([functools.reduce(jnp.add, t) for t in masses], axis=1)
        lse = new_peak + jnp.log2(mass)
        ot = (ot_acc[...] * (1.0 / mass)).astype(BF)
        delta = jnp.sum(gt.astype(F32) * ot.astype(F32), axis=0, keepdims=True)
        o = ot.T
        for i in range(SPAN):
            for m in range(GROUP):
                r = (i * GROUP + m) * BLOCK
                att[first + i, :, m * HD:(m + 1) * HD] = o[r:r + BLOCK]

        def pull(t, lane, stop=LANES, held=True):
            p = jnp.exp2(s_buf[t, :, lane:stop] - lse[:, lane:stop])
            dp = dp_buf[t, :, lane:stop] if held else slopes(t, lane, stop)
            ds = (p * (dp - delta[:, lane:stop])).astype(BF)
            grad_v = jnp.dot(p.astype(BF), gg[lane:stop], preferred_element_type=F32)
            grad_k = jnp.dot(ds, qg[lane:stop], preferred_element_type=F32)
            dqt_acc[:, lane:stop] += jnp.dot(kt[t], ds, preferred_element_type=F32)
            return grad_v, grad_k

        for e in range(SPAN):
            grad_v, grad_k = pull(first + e, e * WIDTH)
            dv_acc[first + e] = grad_v
            dk_acc[first + e] = grad_k

        def backward(base, width, stop):
            def step(n, carried):
                for i in range(width):
                    t = base + n * width + i
                    grad_v, grad_k = pull(t, 0, stop, stop < LANES or width == 2)
                    dv_acc[t] += grad_v
                    dk_acc[t] += grad_k
                return carried

            return step

        for start, stop, lanes in spans:
            odd = lax.rem(stop - start, 2) if lanes == LANES else stop - start
            lax.fori_loop(0, odd, backward(start, 1, lanes), 0)
            if lanes == LANES:
                lax.fori_loop(0, (stop - start) // 2, backward(start + odd, 2, lanes), 0)
        grad = dqt_acc[...].T * SCALE
        for i in range(SPAN):
            for m in range(GROUP):
                r = (i * GROUP + m) * BLOCK
                dq[first + i, :, m * HD:(m + 1) * HD] = grad[r:r + BLOCK]
        for copy in outgoing(n):
            copy.start()
        return carry

    lax.fori_loop(0, SHARDS // SPAN, group, 0)

    def outbound(n):
        cols = pl.ds(n * SPAN, SPAN)
        return pltpu.make_async_copy(dkv.at[:, cols], dkv_hbm.at[:, cols], load.at[n, 0])

    def regroup(s, carry):
        for b in range(SHARDS):
            rows = slice(b * BLOCK, (b + 1) * BLOCK)
            dkv[route[s, b], s] = jnp.stack(
                [(dk_acc[s, rows] * SCALE).astype(BF), dv_acc[s, rows].astype(BF)])
        return carry

    for n in range(SHARDS // SPAN):
        lax.fori_loop(n * SPAN, (n + 1) * SPAN, regroup, 0)
        outbound(n).start()
    pltpu.make_async_copy(att, att_hbm, store.at[0]).wait()
    pltpu.make_async_copy(dq, dq_hbm, store.at[1]).wait()
    for n in range(SHARDS // SPAN):
        outbound(n).wait()


def attention(route, docs, q, g, k, v, kt, vt):
    return pl.pallas_call(
        attention_kernel,
        name="attention",
        out_shape=(
            jax.ShapeDtypeStruct((SHARDS, BLOCK, COLS), BF),
            jax.ShapeDtypeStruct((SHARDS, BLOCK, COLS), F32),
            jax.ShapeDtypeStruct((SHARDS, SHARDS, 2, BLOCK, HD), BF),
        ),
        in_specs=[ANY] * 8,
        out_specs=(ANY, ANY, ANY),
        scratch_shapes=[
            pltpu.VMEM((SHARDS, BLOCK, COLS), BF),
            pltpu.VMEM((SHARDS, BLOCK, COLS), BF),
            pltpu.VMEM((SHARDS, ROWS, HD), BF),
            pltpu.VMEM((SHARDS, ROWS, HD), BF),
            pltpu.VMEM((SHARDS, BLOCK, COLS), BF),
            pltpu.VMEM((SHARDS, BLOCK, COLS), F32),
            pltpu.VMEM((SHARDS, SHARDS, 2, BLOCK, HD), BF),
            pltpu.VMEM((SHARDS, ROWS, LANES), F32),
            pltpu.VMEM((SHARDS, ROWS, LANES), F32),
            pltpu.VMEM((SHARDS, HD, ROWS), BF),
            pltpu.VMEM((SHARDS, HD, ROWS), BF),
            pltpu.VMEM((SHARDS, ROWS, HD), F32),
            pltpu.VMEM((SHARDS, ROWS, HD), F32),
            pltpu.VMEM((HD, LANES), F32),
            pltpu.VMEM((HD, LANES), F32),
            pltpu.SMEM((SHARDS, SHARDS), jnp.int32),
            pltpu.SMEM((DOCS,), jnp.int32),
            pltpu.SMEM((SHARDS,), jnp.int32),
            pltpu.SemaphoreType.DMA((SHARDS // SPAN, 6)),
            pltpu.SemaphoreType.DMA((2,)),
        ],
    )(route, docs, q, g, k, v, kt, vt)


def reduce_kernel(
    part, chip, keep, mine, mate, ready, hold, kept, from_y, from_x,
    s1, r1, sy, ry, sx, rx, s2, r2, local,
):
    c = lax.axis_index("ctx")
    h = lax.axis_index("head")
    x, yl, core = c // 4, lax.rem(c // 2, 2), lax.rem(c, 2)
    other = ctx_of(x, yl, core + 1)
    across = ctx_of(x, yl + 1, core)
    far = (2, 1, 3, 0)
    order = [(dx, dy) for dy in (1, 0) for dx in far]

    def along(dx):
        return ctx_of(x + dx, yl, core)

    def place(dx, dy):
        return lax.rem(x + dx, 4) * 2 + lax.rem(yl + dy, 2)

    loads = []
    for i, (dx, dy) in enumerate(order):
        t = place(dx, dy)
        copy = pltpu.make_async_copy(part.at[t * 2 + core], mine.at[t], local.at[i])
        copy.start()
        loads.append(copy)

    barrier = pltpu.get_barrier_semaphore()
    for peer in (other, across, along(1), along(2), along(3)):
        pl.semaphore_signal(barrier, inc=1, device_id=(peer, h), device_id_type=MESH)
    pl.semaphore_wait(barrier, 5)

    sent = []

    def start(*args):
        copy = remote(*args, h)
        copy.start()
        sent.append(copy)
        return copy

    pairs = []
    for i, (dx, dy) in enumerate(order):
        t = place(dx, dy)
        pairs.append(start(part.at[t * 2 + 1 - core], mate.at[t], s1.at[i], r1.at[i], other))

    for (dx, dy), pair, load in zip(order, pairs, loads):
        t = place(dx, dy)
        load.wait()
        pair.wait_recv()
        sums = [mine[t, :, a].astype(F32) + mate[t, :, a].astype(F32) for a in range(2)]
        if dy == 1:
            ready[t, 0] = sums[0].astype(BF)
            start(ready.at[t, 0], from_y.at[dx], sy.at[dx], ry.at[dx], across)
        else:
            hold[dx] = sums[0]
        if dx == 0:
            kept[1 - dy] = sums[1]
        else:
            ready[t, 1] = sums[1].astype(BF)
            start(ready.at[t, 1], from_x.at[dx - 1, dy], sx.at[dx - 1, dy], rx.at[dx - 1, dy],
                  along(dx))

    for dx in far:
        remote(from_y.at[dx], from_y.at[dx], sy.at[dx], ry.at[dx], across, h).wait_recv()
        hold[dx] += from_y[dx].astype(F32)
        if dx:
            t = place(dx, 0)
            ready[t, 0] = hold[dx].astype(BF)
            start(ready.at[t, 0], chip.at[dx - 1], s2.at[dx], r2.at[dx], along(dx))
    for dy in (1, 0):
        for dx in (1, 3, 2):
            part_in = from_x.at[dx - 1, dy]
            remote(part_in, part_in, sx.at[dx - 1, dy], rx.at[dx - 1, dy], across, h).wait_recv()
            kept[1 - dy] += from_x[dx - 1, dy].astype(F32)
        if dy:
            t = place(0, 1)
            ready[t, 1] = kept[0].astype(BF)
            start(ready.at[t, 1], chip.at[3], s2.at[0], r2.at[0], across)
    outs = [
        pltpu.make_async_copy(hold.at[0], keep.at[0], local.at[0]),
        pltpu.make_async_copy(kept.at[1], keep.at[1], local.at[1]),
    ]
    for out in outs:
        out.start()
    for j in range(4):
        slot = chip.at[(j + 3) % 4]
        remote(slot, slot, s2.at[j], r2.at[j], across, h).wait_recv()
    for copy in sent:
        copy.wait_send()
    for out in outs:
        out.wait()


def reduce(part):
    shape = (SHARDS, BLOCK, HD)
    return pl.pallas_call(
        reduce_kernel,
        name="reduce",
        out_shape=(
            jax.ShapeDtypeStruct((4,) + shape, BF),
            jax.ShapeDtypeStruct((2,) + shape, F32),
        ),
        in_specs=[ANY],
        out_specs=(ANY, ANY),
        scratch_shapes=[
            pltpu.VMEM((8, SHARDS, 2, BLOCK, HD), BF),
            pltpu.VMEM((8, SHARDS, 2, BLOCK, HD), BF),
            pltpu.VMEM((8, 2) + shape, BF),
            pltpu.VMEM((4,) + shape, F32),
            pltpu.VMEM((2,) + shape, F32),
            pltpu.VMEM((4,) + shape, BF),
            pltpu.VMEM((3, 2) + shape, BF),
            pltpu.SemaphoreType.DMA((8,)),
            pltpu.SemaphoreType.DMA((8,)),
            pltpu.SemaphoreType.DMA((4,)),
            pltpu.SemaphoreType.DMA((4,)),
            pltpu.SemaphoreType.DMA((3, 2)),
            pltpu.SemaphoreType.DMA((3, 2)),
            pltpu.SemaphoreType.DMA((4,)),
            pltpu.SemaphoreType.DMA((4,)),
            pltpu.SemaphoreType.DMA((8,)),
        ],
        compiler_params=pltpu.CompilerParams(collective_id=1, has_side_effects=True),
    )(part)


def finish_kernel(chip_hbm, keep_hbm, dk_hbm, dv_hbm, chip, keep, load, store):
    parts = (pl.ds(0, 3), pl.ds(3, 1))
    loads = []
    for a in range(2):
        loads.append((
            pltpu.make_async_copy(chip_hbm.at[parts[a]], chip.at[parts[a]], load.at[a, 0]),
            pltpu.make_async_copy(keep_hbm.at[a], keep.at[a], load.at[a, 1]),
        ))
        for copy in loads[a]:
            copy.start()
    outs = []
    for a, out in enumerate((dk_hbm, dv_hbm)):
        for copy in loads[a]:
            copy.wait()
        total = keep[a]
        for j in ((0, 1, 2), (3,))[a]:
            total = total + chip[j].astype(F32)
        keep[a] = total
        outs.append(pltpu.make_async_copy(keep.at[a], out, store.at[a]))
        outs[a].start()
    for copy in outs:
        copy.wait()


def finish(chip, keep):
    out = jax.ShapeDtypeStruct((SHARDS, BLOCK, HD), F32)
    return pl.pallas_call(
        finish_kernel,
        name="finish",
        out_shape=(out, out),
        in_specs=[ANY, ANY],
        out_specs=(ANY, ANY),
        scratch_shapes=[
            pltpu.VMEM(chip.shape, BF),
            pltpu.VMEM(keep.shape, F32),
            pltpu.SemaphoreType.DMA((2, 2)),
            pltpu.SemaphoreType.DMA((2,)),
        ],
    )(chip, keep)


def on_device(queries, key_rows, value_rows, cotangent, doc_lengths, block_route):
    q, g, k, v, kt, vt = exchange(
        block_route,
        queries.reshape(2, BLOCK, HEADS * COLS),
        key_rows,
        value_rows,
        cotangent.reshape(2, BLOCK, HEADS * COLS),
    )
    att, dq, part = attention(
        block_route, doc_lengths, q, g, k.reshape(SHARDS, ROWS, HD), v.reshape(SHARDS, ROWS, HD), kt, vt)
    dk, dv = finish(*reduce(part))
    return (
        att.reshape(ROWS, COLS),
        dq.reshape(ROWS, COLS),
        dk.reshape(ROWS, HD),
        dv.reshape(ROWS, HD),
    )


def solution(mesh):
    placed = P(("ctx", "head"), None)
    return jax.shard_map(
        on_device,
        mesh=mesh,
        in_specs=(placed, placed, placed, placed, P(), P()),
        out_specs=(P("ctx", "head"),) * 4,
        check_vma=False,
    )
```
